32 devices in a mesh: rows: 16 (over z, x, core), tm: 2 (over y).
Axes of the slice: x: 2, y: 2, z: 4, core: 2. Of those that a mesh axis runs over, the one named last changes fastest.
Arguments:
- patches: bfloat16 [16, 1024, 768], P('rows', 'tm'), may hold values from -6 to 6
- segment_ids: int32 [16, 1024], P('rows', 'tm'), may hold values from 0 to 5, never falling along the last dimension, each value on 1 to 512 neighbouring positions
- mask_positions: int32 [16, 409], P('rows'), may hold values from 0 to 1023, as said below
- mask_embed: bfloat16 [768], replicated, may hold values from -6 to 6
- norm1_gain: bfloat16 [768], replicated, may hold values from 0.5 to 1.5
- norm1_bias: bfloat16 [768], replicated, may hold values from -3 to 3
- w_qkv: bfloat16 [768, 2304], replicated, may hold values from -0.21875 to 0.21875
- query_bias: bfloat16 [768], replicated, may hold values from -3 to 3
- value_bias: bfloat16 [768], replicated, may hold values from -3 to 3
- w_out: bfloat16 [768, 768], replicated, may hold values from -1.75 to 1.75
- out_bias: bfloat16 [768], replicated, may hold values from -3 to 3
- norm2_gain: bfloat16 [768], replicated, may hold values from 0.5 to 1.5
- norm2_bias: bfloat16 [768], replicated, may hold values from -3 to 3
- w_up: bfloat16 [768, 3072], replicated, may hold values from -0.21875 to 0.21875
- up_bias: bfloat16 [3072], replicated, may hold values from -3 to 3
- w_down: bfloat16 [3072, 768], replicated, may hold values from -0.109375 to 0.109375
- down_bias: bfloat16 [768], replicated, may hold values from -3 to 3
- cotangent: bfloat16 [16, 1024, 768], P('rows', 'tm'), may hold values from -6 to 6
Outputs:
- output: bfloat16 [16, 1024, 768], P('rows', 'tm')
- grad_patches: bfloat16 [16, 1024, 768], P('rows', 'tm')
- grad_mask_embed: float32 [768], P('tm')
- grad_norm1_gain: float32 [768], P('tm')
- grad_norm1_bias: float32 [768], P('tm')
- grad_w_qkv: float32 [768, 2304], P('tm')
- grad_query_bias: float32 [768], P('tm')
- grad_value_bias: float32 [768], P('tm')
- grad_w_out: float32 [768, 768], P('tm')
- grad_out_bias: float32 [768], P('tm')
- grad_norm2_gain: float32 [768], P('tm')
- grad_norm2_bias: float32 [768], P('tm')
- grad_w_up: float32 [768, 3072], P('tm')
- grad_up_bias: float32 [3072], P('tm')
- grad_w_down: float32 [3072, 768], P('tm')
- grad_down_bias: float32 [768], P('tm')
The draws below stay inside these ranges and needn't reach their ends.
Inputs may be any that keep to these rules, and one draw needn't show every extreme that they name: `mask_positions`: the 409 positions of a row are distinct. `segment_ids`: ids never fall along a row; every row has 6 segments.
All inputs are finite; a program needn't handle non-finite values.
Results may differ from the reference program's by a relative error of at most 0.019.
Values may be sent and summed in bfloat16 or wider, within the bound.
A program may use at most 128 MiB of HBM per device.

```python
import math
import jax
import jax.numpy as jnp
import numpy as np
from jax import lax

D = 768
HEADS = 12
HEAD = 64
FF = 3072
SEGS = 6
L = 1024
ROWS = 16
MASKS = 409


def draw_mask_positions(key, part):
    row_keys = jax.random.split(key, ROWS)

    def one_row(row_key):
        return jax.random.permutation(row_key, L)[:MASKS].astype(jnp.int32)
    return jax.vmap(one_row)(row_keys)


def steps_of(key, extent, cuts, low, high):
    level = 1.0
    for position, shards_of in cuts:
        draws = jax.random.uniform(jax.random.fold_in(jax.random.fold_in(key, 6), position), (shards_of,), jnp.float32, low / len(cuts), high / len(cuts))
        level = level * jnp.repeat(jnp.exp(draws), extent[position] // shards_of).reshape((-1,) + (1,) * (len(extent) - 1 - position))
    return level


def split_up(number_of, total, reach, lean):
    portions = [(1 << 20) // math.isqrt(rank ** lean) + 1 for rank in range(2, number_of + 1)]
    surplus, counts = total - reach - (number_of - 1), [1] * (number_of - 1)
    while surplus > 0:
        movable = [i for i in range(number_of - 1) if counts[i] < reach]
        mass, remaining = sum([portions[i] for i in movable]), surplus
        for i in movable:
            addition = min(reach - counts[i], max(1, remaining * portions[i] // mass), surplus)
            counts[i] = counts[i] + addition
            surplus = surplus - addition
    return np.array([reach] + counts)


def uneven_parts(rng, number_of, total, limit, skew):
    if number_of == 2:
        one = jax.random.randint(rng, (), max(1, total - limit), min(limit, total - 1) + 1)
        return jnp.stack([one, total - one])
    lengths = jnp.asarray(split_up(number_of, total, limit, skew), jnp.int32)
    couples = (number_of - 1) // 2
    source_of, receiver = lengths[1:1 + 2 * couples:2], lengths[2:2 + 2 * couples:2]
    slack = jnp.minimum(source_of - 1, limit - receiver)
    passed = jax.random.randint(jax.random.fold_in(rng, 1), (couples,), 0, 1 << 20) % (slack + 1)
    lengths = lengths.at[1:1 + 2 * couples:2].set(source_of - passed).at[2:2 + 2 * couples:2].set(receiver + passed)
    return lengths[jax.random.permutation(jax.random.fold_in(rng, 2), number_of)]


def normal_values(rng, extent, spread, most, shards=(), kind=jnp.bfloat16):
    factor_of = steps_of(rng, extent, shards, -0.22, 0.18) if shards else 1.0
    array = jax.random.normal(rng, extent, jnp.float32) * spread * factor_of
    return jnp.minimum(jnp.maximum(array, -most), most).astype(kind)


def setup_inputs(seed: int = 0) -> dict:
    streams_of = jax.random.split(jax.random.key(seed), 19)
    patches = normal_values(streams_of[0], (ROWS, L, D), 1.0, 6.0, ((0, 16), (1, 2)))
    segment_ids = jax.vmap(lambda own: jnp.searchsorted(jnp.cumsum(uneven_parts(own, SEGS, L, L // 2, 0)), jnp.arange(L), side="right"))(jax.random.split(streams_of[1], ROWS)).reshape((ROWS, L)).astype(jnp.int32)
    mask_positions = draw_mask_positions(jax.random.fold_in(streams_of[18], 71), 0)
    mask_embed = normal_values(streams_of[3], (D,), 1.0, 6.0)
    norm1_gain = jnp.clip(1.0 + 0.1 * jax.random.normal(streams_of[4], (D,), jnp.float32), 0.5, 1.5).astype(jnp.bfloat16)
    norm1_bias = normal_values(streams_of[5], (D,), 0.5, 3.0)
    w_qkv = normal_values(streams_of[6], (D, 3 * D), D ** -0.5, 0.21875)
    query_bias = normal_values(streams_of[7], (D,), 0.5, 3.0)
    value_bias = normal_values(streams_of[8], (D,), 0.5, 3.0)
    w_out = normal_values(streams_of[9], (D, D), (max(D // 64, 1)) ** -0.5, 1.75)
    out_bias = normal_values(streams_of[10], (D,), 0.5, 3.0)
    norm2_gain = jnp.clip(1.0 + 0.1 * jax.random.normal(streams_of[11], (D,), jnp.float32), 0.5, 1.5).astype(jnp.bfloat16)
    norm2_bias = normal_values(streams_of[12], (D,), 0.5, 3.0)
    w_up = normal_values(streams_of[13], (D, FF), D ** -0.5, 0.21875)
    up_bias = normal_values(streams_of[14], (FF,), 0.5, 3.0)
    w_down = normal_values(streams_of[15], (FF, D), FF ** -0.5, 0.109375)
    down_bias = normal_values(streams_of[16], (D,), 0.5, 3.0)
    cotangent = normal_values(streams_of[17], (ROWS, L, D), 1.0, 6.0, ((0, 16), (1, 2)))
    return dict(patches=patches, segment_ids=segment_ids, mask_positions=mask_positions, mask_embed=mask_embed, norm1_gain=norm1_gain, norm1_bias=norm1_bias, w_qkv=w_qkv, query_bias=query_bias, value_bias=value_bias, w_out=w_out, out_bias=out_bias, norm2_gain=norm2_gain, norm2_bias=norm2_bias, w_up=w_up, up_bias=up_bias, w_down=w_down, down_bias=down_bias, cotangent=cotangent)


norm_eps = 1e-06
neg_large = -1e+30

@jax.custom_vjp
def low(v):
    return lax.optimization_barrier(v.astype(jnp.bfloat16)).astype(jnp.float32)

@jax.custom_vjp
def low_back(v):
    return v

def low_keep(v):
    return (low(v), None)

def low_pass(kept, grad):
    return (grad,)

def back_keep(v):
    return (v, None)

def back_low(kept, grad):
    return (low(grad),)
low.defvjp(low_keep, low_pass)
low_back.defvjp(back_keep, back_low)

def matmul(left, right):
    return jnp.dot(left, right, precision=lax.Precision.HIGHEST)

def layer_norm(values, norm_gain, norm_shift):
    center = values - lax.optimization_barrier(jnp.mean(values, axis=-1, keepdims=True))
    variance = lax.optimization_barrier(jnp.mean(center * center, axis=-1, keepdims=True))
    return center * lax.rsqrt(variance + norm_eps) * norm_gain + norm_shift

def split_heads(tensor):
    length = tensor.shape[0]
    return tensor.reshape(length, HEADS, HEAD).transpose(1, 0, 2)

def row_forward(params, patches_row, flagged, same):
    mask_embed, norm1_gain, norm1_bias, w_qkv, query_bias, value_bias, w_out, out_bias, norm2_gain, norm2_bias, w_up, up_bias, w_down, down_bias = params
    width = patches_row.shape[1]
    query_scale = 1.0 / math.sqrt(HEAD)
    inputs = jnp.where(flagged[:, None], mask_embed[None, :], patches_row)
    hidden1 = low(layer_norm(inputs, norm1_gain, norm1_bias))
    project = matmul(hidden1, w_qkv)
    queries = low(low_back((project[:, :width] + query_bias) * query_scale))
    keys_all = low(low_back(project[:, width:2 * width]))
    values_all = low(low_back(project[:, 2 * width:] + value_bias))

    def one_head(operands):
        query_h, keys_h, values_h = operands
        scores = low_back(jnp.where(same, matmul(query_h, keys_h.T), neg_large))
        weights = low(jax.nn.softmax(scores, axis=-1))
        return matmul(weights, values_h)
    attended = lax.map(jax.checkpoint(one_head), (split_heads(queries), split_heads(keys_all), split_heads(values_all)))
    attended = attended.transpose(1, 0, 2).reshape(-1, width)
    attended = low(low_back(attended))
    middle = inputs + low_back(matmul(attended, w_out) + out_bias)
    hidden2 = low(layer_norm(middle, norm2_gain, norm2_bias))
    upper = low_back(matmul(hidden2, w_up) + up_bias)
    activated = low(jax.nn.gelu(upper, approximate=False))
    return middle + low_back(matmul(activated, w_down) + down_bias)

def reference(patches, segment_ids, mask_positions, mask_embed, norm1_gain, norm1_bias, w_qkv, query_bias, value_bias, w_out, out_bias, norm2_gain, norm2_bias, w_up, up_bias, w_down, down_bias, cotangent):
    params = (mask_embed.astype(jnp.float32), norm1_gain.astype(jnp.float32), norm1_bias.astype(jnp.float32), w_qkv.astype(jnp.float32), query_bias.astype(jnp.float32), value_bias.astype(jnp.float32), w_out.astype(jnp.float32), out_bias.astype(jnp.float32), norm2_gain.astype(jnp.float32), norm2_bias.astype(jnp.float32), w_up.astype(jnp.float32), up_bias.astype(jnp.float32), w_down.astype(jnp.float32), down_bias.astype(jnp.float32))

    def per_row(totals, items):
        row_patch, row_segment, row_places, row_cot = items
        places = jnp.arange(row_segment.shape[0], dtype=jnp.int32)
        flagged = jnp.any(places[:, None] == row_places[None, :], axis=1)
        same = row_segment[:, None] == row_segment[None, :]

        def forward_fn(param_set, row_inputs):
            return row_forward(param_set, row_inputs, flagged, same)
        result, pull = jax.vjp(forward_fn, params, row_patch.astype(jnp.float32))
        grad_params, grad_input = pull(row_cot.astype(jnp.float32))
        totals = jax.tree.map(jnp.add, totals, grad_params)
        return (totals, (result.astype(jnp.bfloat16), grad_input.astype(jnp.bfloat16)))
    zeros = jax.tree.map(jnp.zeros_like, params)
    totals, outs_pair = lax.scan(per_row, zeros, (patches, segment_ids, mask_positions, cotangent))
    return (outs_pair[0], outs_pair[1], totals[0], totals[1], totals[2], totals[3], totals[4], totals[5], totals[6], totals[7], totals[8], totals[9], totals[10], totals[11], totals[12], totals[13])
```

```python
from functools import partial
import math

import jax
import jax.numpy as jnp
from jax import lax
from jax.experimental import pallas as pl
from jax.experimental.pallas import tpu as pltpu
from jax.sharding import PartitionSpec as P

HEADS = 12
HEAD = 64


norm_eps = 1e-06
neg_large = -1e30


def normalize(values):
    center = values - jnp.mean(values, axis=-1, keepdims=True)
    scale_inv = lax.rsqrt(jnp.mean(center * center, axis=-1, keepdims=True) + norm_eps)
    return (center * scale_inv, scale_inv)


def norm_back(grad_out, normed, scale_inv, norm_gain):
    grad_normed = grad_out * norm_gain
    mean_one = jnp.mean(grad_normed, axis=-1, keepdims=True)
    mean_two = jnp.mean(grad_normed * normed, axis=-1, keepdims=True)
    return scale_inv * (grad_normed - mean_one - normed * mean_two)


def split_heads(tensor):
    rows_n, length, width = tensor.shape
    return tensor.reshape(rows_n, length, HEADS, width // HEADS).transpose(2, 0, 1, 3)


def join_heads(tensor):
    heads_n, rows_n, length, size = tensor.shape
    return tensor.transpose(1, 2, 0, 3).reshape(rows_n, length, heads_n * size)


def head_scores(query, keys_h, same):
    scores = jnp.einsum("rqd,rkd->rqk", query, keys_h, preferred_element_type=jnp.float32)
    return jnp.where(same, scores, neg_large)


def attend_forward(query_heads, key_heads, value_heads, same):

    def one_head(operands):
        query, keys_h, values_h = operands
        scores = head_scores(query, keys_h, same)
        peak = jnp.max(scores, axis=-1, keepdims=True)
        total = jnp.sum(jnp.exp(scores - peak), axis=-1, keepdims=True)
        log_total = peak + jnp.log(total)
        weights = jnp.exp(scores - log_total).astype(jnp.bfloat16)
        result = jnp.einsum("rqk,rkd->rqd", weights, values_h, preferred_element_type=jnp.float32)
        return (result, log_total[..., 0])

    return lax.map(one_head, (query_heads, key_heads, value_heads))


def attend_backward(query_heads, key_heads, value_heads, grad_heads, log_totals, same):

    def one_head(operands):
        query, keys_h, values_h, grad_out, log_total = operands
        scores = head_scores(query, keys_h, same)
        probs_full = jnp.exp(scores - log_total[..., None])
        probs_low = probs_full.astype(jnp.bfloat16)
        grad_values = jnp.einsum(
            "rqk,rqd->rkd", probs_low, grad_out, preferred_element_type=jnp.float32
        )
        grad_probs = jnp.einsum(
            "rqd,rkd->rqk", grad_out, values_h, preferred_element_type=jnp.float32
        )
        delta = jnp.sum(grad_probs * probs_full, axis=-1, keepdims=True)
        grad_scores = (probs_full * (grad_probs - delta)).astype(jnp.bfloat16)
        grad_query = jnp.einsum(
            "rqk,rkd->rqd", grad_scores, keys_h, preferred_element_type=jnp.float32
        )
        grad_keys = jnp.einsum(
            "rqk,rqd->rkd", grad_scores, query, preferred_element_type=jnp.float32
        )
        return (grad_query, grad_keys, grad_values)

    return lax.map(one_head, (query_heads, key_heads, value_heads, grad_heads, log_totals))


MESH = pl.DeviceIdType.MESH
SUB = 96
COLS = 384
LAGS = (0, 1, 3, 4, 5, 7, 8, 9)


def places():
    row = lax.axis_index("rows")
    y = lax.axis_index("tm")
    core = row % 2
    x = (row // 2) % 2
    z_low = (row // 4) % 2
    z_high = row // 8
    peers = (
        (row + 1 - 2 * core, y),
        (row, 1 - y),
        (row + 2 - 4 * x, y),
        (row + 4 - 8 * z_low, y),
        (row + 8 - 16 * z_high, y),
    )
    return core, x, y, peers


def greet(peers):
    barrier = pltpu.get_barrier_semaphore()
    for peer in peers:
        pl.semaphore_signal(barrier, inc=1, device_id=peer, device_id_type=MESH)
    pl.semaphore_wait(barrier, len(peers))


def reduce_kernel(
    count, g_ref, vec_ref, out_ref, vec_out, r1, r2, r3, r4, r5, done, v1, v2, ssem, rsem, vs, vr
):
    core, x, y, peers = places()
    pair, yp, xp, zp1, zp2 = peers
    greet(peers)

    def copy(s, c):
        src, dst, dev = (
            lambda: (g_ref.at[c, 1 - core], r1.at[c], pair),
            lambda: (r1.at[c, 1 - y], r2.at[c], yp),
            lambda: (r2.at[c, 1 - x], r3.at[c], xp),
            lambda: (r3.at[c], r4.at[c], zp1),
            lambda: (r4.at[c], r5.at[c], zp2),
            lambda: (done.at[c, core, x], done.at[c, core, x], xp),
            lambda: (done.at[c, core], done.at[c, core], pair),
        )[s]()
        return pltpu.make_async_remote_copy(
            src_ref=src,
            dst_ref=dst,
            send_sem=ssem.at[s, c],
            recv_sem=rsem.at[s, c],
            device_id=dev,
            device_id_type=MESH,
        )

    def stage(s, c):
        if s > 0:
            copy(s - 1, c).wait_recv()
        if s == 1:
            r1[c] = r1[c] + g_ref[c, core]
        elif s == 2:
            r2[c] = r2[c] + r1[c, y]
        elif s == 3:
            r3[c] = r3[c] + r2[c, x]
        elif s == 4:
            r4[c] = r4[c] + r3[c]
        elif s == 5:
            done[c, core, x] = r5[c] + r4[c]
        elif s == 7:
            out_ref[c] = done[c]
        if s < 7:
            copy(s, c).start()

    def vec_copy(s):
        src, dst, dev = (
            lambda: (vec_ref, v1, pair),
            lambda: (v1.at[1 - y], v2.at[0], yp),
            lambda: (v2.at[0], v2.at[1], xp),
            lambda: (v2.at[1], v2.at[2], zp1),
            lambda: (v2.at[2], v2.at[3], zp2),
        )[s]()
        return pltpu.make_async_remote_copy(
            src_ref=src,
            dst_ref=dst,
            send_sem=vs.at[s],
            recv_sem=vr.at[s],
            device_id=dev,
            device_id_type=MESH,
        )

    def vec_stage(s):
        if s > 0:
            vec_copy(s - 1).wait_recv()
        if s == 1:
            v1[...] = v1[...] + vec_ref[...]
        elif s == 2:
            v2[0] = v2[0] + v1[y]
        elif s == 5:
            vec_out[...] = v2[3] + v2[2]
        elif s > 2:
            v2[s - 2] = v2[s - 2] + v2[s - 3]
        if s < 5:
            vec_copy(s).start()

    def step(t, carry):
        for s in range(8):
            c = t - LAGS[s]

            @pl.when((c >= 0) & (c < count))
            def _():
                stage(s, c)

        for s in range(6):

            @pl.when(t == 2 * s)
            def _():
                vec_stage(s)

        return carry

    lax.fori_loop(0, count + LAGS[7], step, 0)

    def drain(c, carry):
        for s in range(7):
            copy(s, c).wait_send()
        return carry

    lax.fori_loop(0, count, drain, 0)
    for s in range(5):
        vec_copy(s).wait_send()


def reduce_gradients(chunks, vectors):
    count = chunks.shape[0]
    rows_v = vectors.shape[1]

    def low(*shape):
        return pltpu.VMEM(shape, jnp.bfloat16)

    return pl.pallas_call(
        partial(reduce_kernel, count),
        out_shape=(
            jax.ShapeDtypeStruct((count, 2, 2, SUB, COLS), jnp.bfloat16),
            jax.ShapeDtypeStruct((rows_v, COLS), jnp.float32),
        ),
        in_specs=[pl.BlockSpec(memory_space=pltpu.VMEM)] * 2,
        out_specs=(pl.BlockSpec(memory_space=pltpu.VMEM),) * 2,
        scratch_shapes=[
            low(count, 2, 2, SUB, COLS),
            low(count, 2, SUB, COLS),
            low(count, SUB, COLS),
            low(count, SUB, COLS),
            low(count, SUB, COLS),
            low(count, 2, 2, SUB, COLS),
            pltpu.VMEM((2, rows_v, COLS), jnp.float32),
            pltpu.VMEM((4, rows_v, COLS), jnp.float32),
            pltpu.SemaphoreType.DMA((7, count)),
            pltpu.SemaphoreType.DMA((7, count)),
            pltpu.SemaphoreType.DMA((5,)),
            pltpu.SemaphoreType.DMA((5,)),
        ],
        compiler_params=pltpu.CompilerParams(
            collective_id=0, has_side_effects=True, vmem_limit_bytes=62 << 20
        ),
    )(chunks, vectors)


def wide_chunks(grad):
    n = grad.shape[1] // COLS
    return grad.reshape(2, 2, 2, SUB, n, COLS).transpose(4, 1, 0, 2, 3, 5)


def tall_chunks(grad):
    n = grad.shape[0] // 768
    blocks = grad.reshape(2, n, 2, 2, SUB, 2, COLS).transpose(1, 5, 2, 0, 3, 4, 6)
    return blocks.reshape(2 * n, 2, 2, 2, SUB, COLS)


def wide_whole(part):
    n = part.shape[0]
    return part.reshape(n, 384, COLS).transpose(1, 0, 2).reshape(384, n * COLS).astype(jnp.float32)


def tall_whole(part):
    n = part.shape[0] // 2
    blocks = part.reshape(n, 2, 384, COLS).transpose(0, 2, 1, 3)
    return blocks.reshape(n * 384, 768).astype(jnp.float32)


def total_rows(tensor):
    return jnp.sum(tensor.astype(jnp.float32), axis=(0, 1))


def shards(
    block,
    patches,
    segment_ids,
    mask_positions,
    mask_embed,
    norm1_gain,
    norm1_bias,
    w_qkv,
    query_bias,
    value_bias,
    w_out,
    out_bias,
    norm2_gain,
    norm2_bias,
    w_up,
    up_bias,
    w_down,
    down_bias,
    cotangent,
):
    rows_n, time_n, width = patches.shape
    query_scale = 1.0 / math.sqrt(HEAD)
    gain_one = norm1_gain.astype(jnp.float32)
    gain_two = norm2_gain.astype(jnp.float32)
    offset = lax.axis_index("tm") * time_n
    places = offset + lax.broadcasted_iota(jnp.int32, (rows_n, time_n, 1), 1)
    masked = jnp.any(places == mask_positions[:, None, :], axis=-1)[..., None]
    inputs = jnp.where(
        masked, mask_embed.astype(jnp.float32)[None, None, :], patches.astype(jnp.float32)
    )
    normed1, inverse1 = normalize(inputs)
    hidden1 = (normed1 * gain_one + norm1_bias.astype(jnp.float32)).astype(jnp.bfloat16)
    project = jnp.einsum("rtd,de->rte", hidden1, w_qkv, preferred_element_type=jnp.float32)
    queries = ((project[..., :width] + query_bias.astype(jnp.float32)) * query_scale).astype(
        jnp.bfloat16
    )
    keys_own = project[..., width : 2 * width].astype(jnp.bfloat16)
    values_own = (project[..., 2 * width :] + value_bias.astype(jnp.float32)).astype(jnp.bfloat16)
    keys_all, values_all, segments_all = (
        lax.all_gather(keys_own, "tm", axis=1, tiled=True),
        lax.all_gather(values_own, "tm", axis=1, tiled=True),
        lax.all_gather(segment_ids, "tm", axis=1, tiled=True),
    )
    same = segment_ids[:, :, None] == segments_all[:, None, :]
    query_heads = split_heads(queries)
    head_outputs, log_totals = attend_forward(
        query_heads, split_heads(keys_all), split_heads(values_all), same
    )
    attended = join_heads(head_outputs).astype(jnp.bfloat16)
    middle = (
        inputs
        + jnp.einsum("rtd,de->rte", attended, w_out, preferred_element_type=jnp.float32)
        + out_bias.astype(jnp.float32)
    )
    normed2, inverse2 = normalize(middle)
    hidden2 = (normed2 * gain_two + norm2_bias.astype(jnp.float32)).astype(jnp.bfloat16)
    upper = jnp.einsum(
        "rtd,df->rtf", hidden2, w_up, preferred_element_type=jnp.float32
    ) + up_bias.astype(jnp.float32)
    activated = jax.nn.gelu(upper, approximate=False).astype(jnp.bfloat16)
    result = (
        middle
        + jnp.einsum("rtf,fd->rtd", activated, w_down, preferred_element_type=jnp.float32)
        + down_bias.astype(jnp.float32)
    )
    output = result.astype(jnp.bfloat16)
    grad_result = cotangent.astype(jnp.float32)
    grad_w_down = jnp.einsum(
        "rtf,rtd->fd", activated, cotangent, preferred_element_type=jnp.float32
    )
    grad_down_bias = total_rows(grad_result)
    grad_activated = jnp.einsum(
        "rtd,fd->rtf", cotangent, w_down, preferred_element_type=jnp.float32
    )
    unused, gelu_pull = jax.vjp(partial(jax.nn.gelu, approximate=False), upper)
    grad_upper = gelu_pull(grad_activated)[0].astype(jnp.bfloat16)
    grad_w_up = jnp.einsum("rtd,rtf->df", hidden2, grad_upper, preferred_element_type=jnp.float32)
    grad_up_bias = total_rows(grad_upper)
    grad_hidden2 = jnp.einsum("rtf,df->rtd", grad_upper, w_up, preferred_element_type=jnp.float32)
    grad_gain_two = total_rows(grad_hidden2 * normed2)
    grad_bias_two = total_rows(grad_hidden2)
    grad_middle = grad_result + norm_back(grad_hidden2, normed2, inverse2, gain_two)
    mlp_vectors = jnp.stack([grad_gain_two, grad_bias_two, grad_down_bias], axis=1)
    grad_branch = grad_middle.astype(jnp.bfloat16)
    grad_w_out = jnp.einsum(
        "rtd,rte->de", attended, grad_branch, preferred_element_type=jnp.float32
    )
    grad_out_bias = total_rows(grad_branch)
    grad_attended = jnp.einsum(
        "rte,de->rtd", grad_branch, w_out, preferred_element_type=jnp.float32
    ).astype(jnp.bfloat16)
    keys_back, values_back, segments_back = (
        lax.all_gather(keys_own, "tm", axis=1, tiled=True),
        lax.all_gather(values_own, "tm", axis=1, tiled=True),
        lax.all_gather(segment_ids, "tm", axis=1, tiled=True),
    )
    same_back = segment_ids[:, :, None] == segments_back[:, None, :]
    grad_query_h, grad_keys_h, grad_values_h = attend_backward(
        query_heads,
        split_heads(keys_back),
        split_heads(values_back),
        split_heads(grad_attended),
        log_totals,
        same_back,
    )
    grad_keys, grad_values = (
        lax.psum_scatter(
            join_heads(grad_keys_h).astype(jnp.bfloat16), "tm", scatter_dimension=1, tiled=True
        ).astype(jnp.float32),
        lax.psum_scatter(
            join_heads(grad_values_h).astype(jnp.bfloat16), "tm", scatter_dimension=1, tiled=True
        ).astype(jnp.float32),
    )
    grad_queries = join_heads(grad_query_h).astype(jnp.bfloat16)
    grad_project = jnp.concatenate(
        [
            (grad_queries.astype(jnp.float32) * query_scale).astype(jnp.bfloat16),
            grad_keys.astype(jnp.bfloat16),
            grad_values.astype(jnp.bfloat16),
        ],
        axis=-1,
    )
    grad_w_qkv = jnp.einsum(
        "rtd,rte->de", hidden1, grad_project, preferred_element_type=jnp.float32
    )
    grad_query_bias = total_rows(grad_project[..., :width])
    grad_value_bias = total_rows(grad_project[..., 2 * width :])
    grad_hidden1 = jnp.einsum(
        "rte,de->rtd", grad_project, w_qkv, preferred_element_type=jnp.float32
    )
    grad_gain_one = total_rows(grad_hidden1 * normed1)
    grad_bias_one = total_rows(grad_hidden1)
    grad_inputs = grad_middle + norm_back(grad_hidden1, normed1, inverse1, gain_one)
    grad_mask = total_rows(jnp.where(masked, grad_inputs, 0.0))
    grad_patches = jnp.where(masked, 0.0, grad_inputs).astype(jnp.bfloat16)
    attn_vectors = jnp.stack(
        [grad_mask, grad_gain_one, grad_bias_one, grad_query_bias, grad_value_bias, grad_out_bias],
        axis=1,
    )
    if block:
        chunks = jnp.concatenate(
            [
                wide_chunks(grad_w_up.astype(jnp.bfloat16)),
                tall_chunks(grad_w_down.astype(jnp.bfloat16)),
                wide_chunks(grad_w_out.astype(jnp.bfloat16)),
                wide_chunks(grad_w_qkv.astype(jnp.bfloat16)),
            ]
        )
        vectors = jnp.concatenate(
            [attn_vectors.T, mlp_vectors.T, jnp.zeros((3, width), jnp.float32)]
        ).reshape(12, 2, 384)
        vectors = jnp.concatenate([vectors[:9].transpose(1, 0, 2), grad_up_bias.reshape(2, 4, 384), vectors[9:].transpose(1, 0, 2)], axis=1)
        parts, v = reduce_gradients(chunks, vectors)
        return (
            output,
            grad_patches,
            v[0],
            v[1],
            v[2],
            wide_whole(parts[18:]),
            v[3],
            v[4],
            wide_whole(parts[16:18]),
            v[5],
            v[6],
            v[7],
            wide_whole(parts[:8]),
            v[9:13].reshape(-1),
            tall_whole(parts[8:16]),
            v[8],
        )
    every_part = (
        lax.psum_scatter(
            grad_w_qkv.astype(jnp.bfloat16), "tm", scatter_dimension=0, tiled=True
        ).astype(jnp.float32),
        lax.psum_scatter(
            grad_w_out.astype(jnp.bfloat16), "tm", scatter_dimension=0, tiled=True
        ).astype(jnp.float32),
        lax.psum_scatter(
            attn_vectors.astype(jnp.bfloat16), "tm", scatter_dimension=0, tiled=True
        ).astype(jnp.float32),
        lax.psum_scatter(
            grad_w_up.astype(jnp.bfloat16), "tm", scatter_dimension=0, tiled=True
        ).astype(jnp.float32),
        lax.psum_scatter(
            grad_w_down.astype(jnp.bfloat16), "tm", scatter_dimension=0, tiled=True
        ).astype(jnp.float32),
        lax.psum_scatter(
            mlp_vectors.astype(jnp.bfloat16), "tm", scatter_dimension=0, tiled=True
        ).astype(jnp.float32),
        lax.psum_scatter(
            grad_up_bias.astype(jnp.bfloat16), "tm", scatter_dimension=0, tiled=True
        ).astype(jnp.float32),
    )
    every_part = (
        lax.psum(every_part[0].astype(jnp.bfloat16), "rows").astype(jnp.float32),
        lax.psum(every_part[1].astype(jnp.bfloat16), "rows").astype(jnp.float32),
        lax.psum(every_part[2].astype(jnp.bfloat16), "rows").astype(jnp.float32),
        lax.psum(every_part[3].astype(jnp.bfloat16), "rows").astype(jnp.float32),
        lax.psum(every_part[4].astype(jnp.bfloat16), "rows").astype(jnp.float32),
        lax.psum(every_part[5].astype(jnp.bfloat16), "rows").astype(jnp.float32),
        lax.psum(every_part[6].astype(jnp.bfloat16), "rows").astype(jnp.float32),
    )
    summed_qkv, summed_out, summed_attn, summed_up, summed_down, summed_mlp, summed_up_bias = (
        every_part
    )
    return (
        output,
        grad_patches,
        summed_attn[:, 0],
        summed_attn[:, 1],
        summed_attn[:, 2],
        summed_qkv,
        summed_attn[:, 3],
        summed_attn[:, 4],
        summed_out,
        summed_attn[:, 5],
        summed_mlp[:, 0],
        summed_mlp[:, 1],
        summed_up,
        summed_up_bias,
        summed_down,
        summed_mlp[:, 2],
    )


def solution(mesh):
    placed = (
        P("rows", "tm", None),
        P("rows", "tm"),
        P("rows", None),
        P(),
        P(),
        P(),
        P(),
        P(),
        P(),
        P(),
        P(),
        P(),
        P(),
        P(),
        P(),
        P(),
        P(),
        P("rows", "tm", None),
    )
    return jax.shard_map(
        partial(shards, dict(mesh.shape) == {"rows": 16, "tm": 2}),
        mesh=mesh,
        in_specs=placed,
        out_specs=(
            P("rows", "tm", None),
            P("rows", "tm", None),
            P("tm"),
            P("tm"),
            P("tm"),
            P("tm", None),
            P("tm"),
            P("tm"),
            P("tm", None),
            P("tm"),
            P("tm"),
            P("tm"),
            P("tm", None),
            P("tm"),
            P("tm", None),
            P("tm"),
        ),
        check_vma=False,
    )
```

```python
from functools import partial
import math

import jax
import jax.numpy as jnp
from jax import lax
from jax.experimental import pallas as pl
from jax.experimental.pallas import tpu as pltpu
from jax.sharding import PartitionSpec as P

HEADS = 12
HEAD = 64


norm_eps = 1e-06
neg_large = -1e30


def normalize(values):
    center = values - jnp.mean(values, axis=-1, keepdims=True)
    scale_inv = lax.rsqrt(jnp.mean(center * center, axis=-1, keepdims=True) + norm_eps)
    return (center * scale_inv, scale_inv)


def norm_back(grad_out, normed, scale_inv, norm_gain):
    grad_normed = grad_out * norm_gain
    mean_one = jnp.mean(grad_normed, axis=-1, keepdims=True)
    mean_two = jnp.mean(grad_normed * normed, axis=-1, keepdims=True)
    return scale_inv * (grad_normed - mean_one - normed * mean_two)


def split_heads(tensor):
    rows_n, length, width = tensor.shape
    return tensor.reshape(rows_n, length, HEADS, width // HEADS).transpose(2, 0, 1, 3)


def join_heads(tensor):
    heads_n, rows_n, length, size = tensor.shape
    return tensor.transpose(1, 2, 0, 3).reshape(rows_n, length, heads_n * size)


def head_scores(query, keys_h, same):
    scores = jnp.einsum("rqd,rkd->rqk", query, keys_h, preferred_element_type=jnp.float32)
    return jnp.where(same, scores, neg_large)


def attend_forward(query_heads, key_heads, value_heads, same):

    def one_head(operands):
        query, keys_h, values_h = operands
        scores = head_scores(query, keys_h, same)
        peak = jnp.max(scores, axis=-1, keepdims=True)
        total = jnp.sum(jnp.exp(scores - peak), axis=-1, keepdims=True)
        log_total = peak + jnp.log(total)
        weights = jnp.exp(scores - log_total).astype(jnp.bfloat16)
        result = jnp.einsum("rqk,rkd->rqd", weights, values_h, preferred_element_type=jnp.float32)
        return (result, log_total[..., 0])

    return lax.map(one_head, (query_heads, key_heads, value_heads))


def attend_backward(query_heads, key_heads, value_heads, grad_heads, log_totals, same):

    def one_head(operands):
        query, keys_h, values_h, grad_out, log_total = operands
        scores = head_scores(query, keys_h, same)
        probs_full = jnp.exp(scores - log_total[..., None])
        probs_low = probs_full.astype(jnp.bfloat16)
        grad_values = jnp.einsum(
            "rqk,rqd->rkd", probs_low, grad_out, preferred_element_type=jnp.float32
        )
        grad_probs = jnp.einsum(
            "rqd,rkd->rqk", grad_out, values_h, preferred_element_type=jnp.float32
        )
        delta = jnp.sum(grad_probs * probs_full, axis=-1, keepdims=True)
        grad_scores = (probs_full * (grad_probs - delta)).astype(jnp.bfloat16)
        grad_query = jnp.einsum(
            "rqk,rkd->rqd", grad_scores, keys_h, preferred_element_type=jnp.float32
        )
        grad_keys = jnp.einsum(
            "rqk,rqd->rkd", grad_scores, query, preferred_element_type=jnp.float32
        )
        return (grad_query, grad_keys, grad_values)

    return lax.map(one_head, (query_heads, key_heads, value_heads, grad_heads, log_totals))


MESH = pl.DeviceIdType.MESH
SUB = 96
COLS = 384
LAGS = (0, 1, 3, 4, 5, 7, 8, 9)


def places():
    row = lax.axis_index("rows")
    y = lax.axis_index("tm")
    core = row % 2
    x = (row // 2) % 2
    z_low = (row // 4) % 2
    z_high = row // 8
    peers = (
        (row + 1 - 2 * core, y),
        (row, 1 - y),
        (row + 2 - 4 * x, y),
        (row + 4 - 8 * z_low, y),
        (row + 8 - 16 * z_high, y),
    )
    return core, x, y, peers


def greet(peers):
    barrier = pltpu.get_barrier_semaphore()
    for peer in peers:
        pl.semaphore_signal(barrier, inc=1, device_id=peer, device_id_type=MESH)
    pl.semaphore_wait(barrier, len(peers))


def reduce_kernel(
    count, g_ref, vec_ref, out_ref, vec_out, r1, r2, r3, r4, r5, done, v1, v2, ssem, rsem, vs, vr
):
    core, x, y, peers = places()
    pair, yp, xp, zp1, zp2 = peers
    greet(peers)

    def copy(s, c):
        src, dst, dev = (
            lambda: (g_ref.at[c, 1 - core], r1.at[c], pair),
            lambda: (r1.at[c, 1 - y], r2.at[c], yp),
            lambda: (r2.at[c, 1 - x], r3.at[c], xp),
            lambda: (r3.at[c], r4.at[c], zp1),
            lambda: (r4.at[c], r5.at[c], zp2),
            lambda: (done.at[c, core, x], done.at[c, core, x], xp),
            lambda: (done.at[c, core], done.at[c, core], pair),
        )[s]()
        return pltpu.make_async_remote_copy(
            src_ref=src,
            dst_ref=dst,
            send_sem=ssem.at[s, c],
            recv_sem=rsem.at[s, c],
            device_id=dev,
            device_id_type=MESH,
        )

    def stage(s, c):
        if s > 0:
            copy(s - 1, c).wait_recv()
        if s == 1:
            r1[c] = r1[c] + g_ref[c, core]
        elif s == 2:
            r2[c] = r2[c] + r1[c, y]
        elif s == 3:
            r3[c] = r3[c] + r2[c, x]
        elif s == 4:
            r4[c] = r4[c] + r3[c]
        elif s == 5:
            done[c, core, x] = r5[c] + r4[c]
        elif s == 7:
            out_ref[c] = done[c]
        if s < 7:
            copy(s, c).start()

    def vec_copy(s):
        src, dst, dev = (
            lambda: (vec_ref, v1, pair),
            lambda: (v1.at[1 - y], v2.at[0], yp),
            lambda: (v2.at[0], v2.at[1], xp),
            lambda: (v2.at[1], v2.at[2], zp1),
            lambda: (v2.at[2], v2.at[3], zp2),
        )[s]()
        return pltpu.make_async_remote_copy(
            src_ref=src,
            dst_ref=dst,
            send_sem=vs.at[s],
            recv_sem=vr.at[s],
            device_id=dev,
            device_id_type=MESH,
        )

    def vec_stage(s):
        if s > 0:
            vec_copy(s - 1).wait_recv()
        if s == 1:
            v1[...] = v1[...] + vec_ref[...]
        elif s == 2:
            v2[0] = v2[0] + v1[y]
        elif s == 5:
            vec_out[...] = v2[3] + v2[2]
        elif s > 2:
            v2[s - 2] = v2[s - 2] + v2[s - 3]
        if s < 5:
            vec_copy(s).start()

    def step(t, carry):
        for s in range(8):
            c = t - LAGS[s]

            @pl.when((c >= 0) & (c < count))
            def _():
                stage(s, c)

        for s in range(6):

            @pl.when(t == 2 * s)
            def _():
                vec_stage(s)

        return carry

    lax.fori_loop(0, count + LAGS[7], step, 0)

    def drain(c, carry):
        for s in range(7):
            copy(s, c).wait_send()
        return carry

    lax.fori_loop(0, count, drain, 0)
    for s in range(5):
        vec_copy(s).wait_send()


def reduce_gradients(chunks, vectors):
    count = chunks.shape[0]
    rows_v = vectors.shape[1]

    def low(*shape):
        return pltpu.VMEM(shape, jnp.bfloat16)

    return pl.pallas_call(
        partial(reduce_kernel, count),
        out_shape=(
            jax.ShapeDtypeStruct((count, 2, 2, SUB, COLS), jnp.bfloat16),
            jax.ShapeDtypeStruct((rows_v, COLS), jnp.float32),
        ),
        in_specs=[pl.BlockSpec(memory_space=pltpu.VMEM)] * 2,
        out_specs=(pl.BlockSpec(memory_space=pltpu.VMEM),) * 2,
        scratch_shapes=[
            low(count, 2, 2, SUB, COLS),
            low(count, 2, SUB, COLS),
            low(count, SUB, COLS),
            low(count, SUB, COLS),
            low(count, SUB, COLS),
            low(count, 2, 2, SUB, COLS),
            pltpu.VMEM((2, rows_v, COLS), jnp.float32),
            pltpu.VMEM((4, rows_v, COLS), jnp.float32),
            pltpu.SemaphoreType.DMA((7, count)),
            pltpu.SemaphoreType.DMA((7, count)),
            pltpu.SemaphoreType.DMA((5,)),
            pltpu.SemaphoreType.DMA((5,)),
        ],
        compiler_params=pltpu.CompilerParams(
            collective_id=0, has_side_effects=True, vmem_limit_bytes=62 << 20
        ),
    )(chunks, vectors)


def wide_chunks(grad):
    n = grad.shape[1] // COLS
    return grad.reshape(2, 2, 2, SUB, n, COLS).transpose(4, 1, 0, 2, 3, 5)


def tall_chunks(grad):
    n = grad.shape[0] // 768
    blocks = grad.reshape(2, n, 2, 2, SUB, 2, COLS).transpose(1, 5, 2, 0, 3, 4, 6)
    return blocks.reshape(2 * n, 2, 2, 2, SUB, COLS)


def wide_whole(part):
    n = part.shape[0]
    return part.reshape(n, 384, COLS).transpose(1, 0, 2).reshape(384, n * COLS).astype(jnp.float32)


def tall_whole(part):
    n = part.shape[0] // 2
    blocks = part.reshape(n, 2, 384, COLS).transpose(0, 2, 1, 3)
    return blocks.reshape(n * 384, 768).astype(jnp.float32)


def total_rows(tensor):
    return jnp.sum(tensor.astype(jnp.float32), axis=(0, 1))


VMEM = pltpu.VMEM
F32 = jnp.float32
BF16 = jnp.bfloat16
HALF = 512
TILE = 256
R_EMBED, R_G1, R_B1, R_QB, R_VB, R_OB, R_G2, R_B2, R_DB, R_UB = 0, 1, 2, 3, 4, 5, 6, 7, 8, 9
QUERY_SCALE = 1.0 / math.sqrt(HEAD)


def dot(a, b):
    return lax.dot_general(a, b, (((1,), (0,)), ((), ())), preferred_element_type=F32)


def dot_t(a, b):
    return lax.dot_general(a, b, (((1,), (1,)), ((), ())), preferred_element_type=F32)


def t_dot(a, b):
    return lax.dot_general(a, b, (((0,), (0,)), ((), ())), preferred_element_type=F32)


def standard(values):
    center = values - jnp.mean(values, axis=-1, keepdims=True)
    scale_inv = lax.rsqrt(jnp.mean(center * center, axis=-1, keepdims=True) + norm_eps)
    return center * scale_inv, scale_inv


def masked_inputs(patch, first, marks, embed):
    at = first + lax.broadcasted_iota(jnp.int32, (patch.shape[0], 1), 0)
    flagged = jnp.max(jnp.where(at == marks, 1.0, 0.0), axis=-1, keepdims=True) > 0.5
    return flagged, jnp.where(flagged, embed, patch.astype(F32))


def front_kernel(other, p_ref, marks_ref, table_ref, w_ref, h1_ref, qkv_ref):
    y = lax.axis_index("tm")
    first = (1 - y if other else y) * HALF + pl.program_id(0) * TILE
    unused, inputs = masked_inputs(p_ref[...], first, marks_ref[...], table_ref[R_EMBED : R_EMBED + 1, :])
    normed, unused = standard(inputs)
    hidden = (normed * table_ref[R_G1 : R_G1 + 1, :] + table_ref[R_B1 : R_B1 + 1, :]).astype(BF16)
    h1_ref[...] = hidden
    for part in range(6):
        cols = slice(part * 384, part * 384 + 384)
        project = dot(hidden, w_ref[:, cols])
        bias = slice((part % 2) * 384, (part % 2) * 384 + 384)
        if part < 2:
            project = (project + table_ref[R_QB : R_QB + 1, bias]) * QUERY_SCALE
        elif part >= 4:
            project = project + table_ref[R_VB : R_VB + 1, bias]
        qkv_ref[:, cols] = project.astype(BF16)


def front(other, patch, marks, table, w_qkv):
    return pl.pallas_call(
        partial(front_kernel, other),
        grid=(HALF // TILE,),
        out_shape=(
            jax.ShapeDtypeStruct((HALF, 768), BF16),
            jax.ShapeDtypeStruct((HALF, 2304), BF16),
        ),
        in_specs=[
            pl.BlockSpec((TILE, 768), lambda i: (i, 0)),
            pl.BlockSpec(marks.shape, lambda i: (0, 0)),
            pl.BlockSpec(table.shape, lambda i: (0, 0)),
            pl.BlockSpec((768, 2304), lambda i: (0, 0), pipeline_mode=pl.Buffered(1)),
        ],
        out_specs=(
            pl.BlockSpec((TILE, 768), lambda i: (i, 0)),
            pl.BlockSpec((TILE, 2304), lambda i: (i, 0)),
        ),
        cost_estimate=pl.CostEstimate(flops=2 * HALF * 768 * 2304, bytes_accessed=8 << 20, transcendentals=0),
    )(patch, marks, table, w_qkv)


def attend_kernel(q_ref, k_ref, v_ref, kx_ref, vx_ref, qa_ref, ka_ref, kxa_ref, o_ref, lse_ref):
    y = lax.axis_index("tm")
    pair = pl.program_id(0)
    lane = lax.broadcasted_iota(jnp.int32, (1, 128), 1)
    keys = jnp.concatenate([k_ref[...], ka_ref[...]], axis=1)
    far_keys = jnp.concatenate([kx_ref[...], kxa_ref[...]], axis=1)
    near_x = pl.multiple_of(y * TILE, TILE)
    near_keys = jnp.concatenate([kx_ref[pl.ds(near_x, TILE), :], kxa_ref[pl.ds(near_x, TILE), :]], axis=1)
    for far in range(2):
        rows = pl.ds(pl.multiple_of((y if far else 1 - y) * TILE, TILE), TILE)
        q = q_ref[rows, :]
        qa = qa_ref[rows, :]
        kept = None
        marks = jnp.where(pair == 0, 0.0, lse_ref[rows, :])
        for h in range(2):
            mine = (lane // 64) == h
            query = jnp.concatenate([jnp.where(mine, q, 0), qa], axis=1)
            own = dot_t(query, keys)
            cross = dot_t(query, near_keys if far else far_keys)
            peak = jnp.maximum(jnp.max(own, axis=-1, keepdims=True), jnp.max(cross, axis=-1, keepdims=True))
            own = jnp.exp(own - peak)
            cross = jnp.exp(cross - peak)
            total = jnp.sum(own, axis=-1, keepdims=True) + jnp.sum(cross, axis=-1, keepdims=True)
            values = vx_ref[pl.ds(near_x, TILE), :] if far else vx_ref[...]
            out = dot(own.astype(BF16), v_ref[...]) + dot(cross.astype(BF16), values)
            out = out / total
            kept = out if h == 0 else jnp.where(mine, out, kept)
            marks = jnp.where(lane == 2 * pair + h, peak + jnp.log(total), marks)
        o_ref[rows, :] = kept.astype(BF16)
        lse_ref[rows, :] = marks


def attend(qkv, qkv_other, qa, ka, kxa):
    def block(first):
        return pl.BlockSpec((HALF, 128), lambda i: (0, first + i))

    whole = pl.BlockSpec((HALF, 128), lambda i: (0, 0))
    return pl.pallas_call(
        attend_kernel,
        grid=(6,),
        out_shape=(jax.ShapeDtypeStruct((HALF, 768), BF16), jax.ShapeDtypeStruct((HALF, 128), F32)),
        in_specs=[block(0), block(6), block(12), block(6), block(12), whole, whole, whole],
        out_specs=(pl.BlockSpec((HALF, 128), lambda i: (0, i)), whole),
        cost_estimate=pl.CostEstimate(
            flops=4 * 12 * HALF * 1024 * 64, bytes_accessed=8 << 20, transcendentals=12 * HALF * 1024
        ),
    )(qkv, qkv, qkv, qkv_other, qkv_other, qa, ka, kxa)


ERFC_P = 0.3275911
ERFC_C = (
    0.1851102167482524,
    0.17993860771517878,
    0.21041948320823337,
    0.011498087426314028,
    0.47813345988158296,
    -0.4317659362057169,
    0.5111742647535956,
    -0.14450823957827402,
)


def gelu_and_slope(u):
    t = 1.0 / (1.0 + (ERFC_P * math.sqrt(0.5)) * jnp.abs(u))
    bell = jnp.exp(-0.5 * (u * u))
    series = ERFC_C[7]
    for c in ERFC_C[6::-1]:
        series = series * t + c
    tail = (0.5 * t) * series * bell
    phi = jnp.where(u < 0, tail, 1.0 - tail)
    return u * phi, phi + u * (bell * (1.0 / math.sqrt(2.0 * math.pi)))


FF_TILE = 384


def middle_kernel(
    p_ref, marks_ref, table_ref, a_ref, wo_ref, cot_ref, wu_ref, wd_ref, ub_ref, mid_ref, h2_ref, act_ref, gu_ref
):
    y = lax.axis_index("tm")

    @pl.when(pl.program_id(0) == 0)
    def _():
        for tile in range(HALF // TILE):
            rows = slice(tile * TILE, tile * TILE + TILE)
            unused, inputs = masked_inputs(
                p_ref[rows, :], y * HALF + tile * TILE, marks_ref[...], table_ref[R_EMBED : R_EMBED + 1, :]
            )
            mid = inputs + dot(a_ref[rows, :], wo_ref[...]) + table_ref[R_OB : R_OB + 1, :]
            normed, unused = standard(mid)
            mid_ref[rows, :] = mid
            h2_ref[rows, :] = (normed * table_ref[R_G2 : R_G2 + 1, :] + table_ref[R_B2 : R_B2 + 1, :]).astype(BF16)

    for tile in range(HALF // TILE):
        rows = slice(tile * TILE, tile * TILE + TILE)
        upper = dot(h2_ref[rows, :], wu_ref[...]) + ub_ref[...]
        value, slope = gelu_and_slope(upper)
        act_ref[rows, :] = value.astype(BF16)
        grad = dot_t(cot_ref[rows, :], wd_ref[...])
        gu_ref[rows, :] = (grad * slope).astype(BF16)


def middle_part(patch, marks, table, attended, w_out, cot, w_up, w_down, up_bias):
    def full(shape):
        return pl.BlockSpec(shape, lambda i: (0, 0))

    return pl.pallas_call(
        middle_kernel,
        grid=(3072 // FF_TILE,),
        out_shape=(
            jax.ShapeDtypeStruct((HALF, 768), F32),
            jax.ShapeDtypeStruct((HALF, 768), BF16),
            jax.ShapeDtypeStruct((HALF, 3072), BF16),
            jax.ShapeDtypeStruct((HALF, 3072), BF16),
        ),
        in_specs=[
            full((HALF, 768)),
            full(marks.shape),
            full(table.shape),
            full((HALF, 768)),
            full((768, 768)),
            full((HALF, 768)),
            pl.BlockSpec((768, FF_TILE), lambda i: (0, i)),
            pl.BlockSpec((FF_TILE, 768), lambda i: (i, 0)),
            pl.BlockSpec((1, FF_TILE), lambda i: (0, i)),
        ],
        out_specs=(
            full((HALF, 768)),
            full((HALF, 768)),
            pl.BlockSpec((HALF, FF_TILE), lambda i: (0, i)),
            pl.BlockSpec((HALF, FF_TILE), lambda i: (0, i)),
        ),
        cost_estimate=pl.CostEstimate(
            flops=2 * HALF * 768 * (768 + 6144), bytes_accessed=24 << 20, transcendentals=HALF * 3072
        ),
    )(patch, marks, table, attended, w_out, cot, w_up, w_down, up_bias)


def block_shards(
    patches,
    segment_ids,
    mask_positions,
    mask_embed,
    norm1_gain,
    norm1_bias,
    w_qkv,
    query_bias,
    value_bias,
    w_out,
    out_bias,
    norm2_gain,
    norm2_bias,
    w_up,
    up_bias,
    w_down,
    down_bias,
    cotangent,
):
    swap = [(0, 1), (1, 0)]
    width = 768
    patch = patches[0]
    cot = cotangent[0]
    patch_x = lax.ppermute(patch, "tm", swap)
    ids = segment_ids[0]
    ids_x = lax.ppermute(ids, "tm", swap)
    table = jnp.concatenate(
        [
            jnp.stack(
                [
                    mask_embed,
                    norm1_gain,
                    norm1_bias,
                    query_bias,
                    value_bias,
                    out_bias,
                    norm2_gain,
                    norm2_bias,
                    down_bias,
                ]
            ),
            up_bias.reshape(4, 768),
            jnp.zeros((3, 768), BF16),
        ]
    ).astype(F32)
    lane = jnp.arange(128)[None, :]
    qa = jnp.where(ids[:, None] == lane, 1.0, 0.0).astype(BF16)
    ka = jnp.where((lane >= 6) | (ids[:, None] == lane), 0.0, neg_large).astype(BF16)
    kxa = jnp.where((lane >= 6) | (ids_x[:, None] == lane), 0.0, neg_large).astype(BF16)
    hidden1, qkv = front(False, patch, mask_positions, table, w_qkv)
    unused, qkv_x = front(True, patch_x, mask_positions, table, w_qkv)
    attended, lse = attend(qkv, qkv_x, qa, ka, kxa)
    middle, hidden2, activated, grad_upper = middle_part(
        patch, mask_positions, table, attended, w_out, cot, w_up, w_down, up_bias.astype(F32)[None]
    )
    rows_n, time_n = 1, HALF
    gain_one = table[R_G1]
    gain_two = table[R_G2]
    places_own = lax.axis_index("tm") * time_n + jnp.arange(time_n)[:, None]
    masked = jnp.any(places_own == mask_positions, axis=-1)[:, None]
    inputs = jnp.where(masked, table[R_EMBED][None], patch.astype(F32))
    normed1, inverse1 = normalize(inputs)
    normed2, inverse2 = normalize(middle)
    output = (middle + jnp.dot(activated, w_down, preferred_element_type=F32) + table[R_DB]).astype(BF16)
    grad_w_down = t_dot(activated, cot)
    grad_w_up = t_dot(hidden2, grad_upper)
    grad_up_bias = jnp.sum(grad_upper.astype(F32), axis=0)
    grad_hidden2 = dot_t(grad_upper, w_up)
    grad_middle = cot.astype(F32) + norm_back(grad_hidden2, normed2, inverse2, gain_two)
    grad_branch = grad_middle.astype(BF16)
    grad_w_out = t_dot(attended, grad_branch)
    grad_attended = dot_t(grad_branch, w_out).astype(BF16)
    same = ids[None, :, None] == jnp.concatenate([ids, ids_x])[None, None, :]
    both = jnp.concatenate([qkv[:, 768:], qkv_x[:, 768:]])
    gq, gk, gv = attend_backward(
        split_heads(qkv[None, :, :768]),
        split_heads(both[None, :, :768]),
        split_heads(both[None, :, 768:]),
        split_heads(grad_attended[None]),
        lse[:, :12].T[:, None, :],
        same,
    )
    gk, gv = join_heads(gk)[0], join_heads(gv)[0]
    gkv = jnp.concatenate([gk, gv], axis=1).astype(BF16)
    gkv = gkv[:HALF].astype(F32) + lax.ppermute(gkv[HALF:], "tm", swap).astype(F32)
    gq = (join_heads(gq)[0].astype(BF16).astype(F32) * QUERY_SCALE).astype(BF16)
    grad_project = jnp.concatenate([gq, gkv.astype(BF16)], axis=1)
    grad_w_qkv = t_dot(hidden1, grad_project)
    sums = jnp.sum(grad_project.astype(F32), axis=0)
    grad_hidden1 = dot_t(grad_project, w_qkv)
    grad_inputs = grad_middle + norm_back(grad_hidden1, normed1, inverse1, gain_one)
    grad_patches = jnp.where(masked, 0.0, grad_inputs).astype(BF16)
    vectors = jnp.stack(
        [
            jnp.sum(jnp.where(masked, grad_inputs, 0.0), axis=0),
            jnp.sum(grad_hidden1 * normed1, axis=0),
            jnp.sum(grad_hidden1, axis=0),
            sums[:768],
            sums[1536:],
            jnp.sum(grad_branch.astype(F32), axis=0),
            jnp.sum(grad_hidden2 * normed2, axis=0),
            jnp.sum(grad_hidden2, axis=0),
            jnp.sum(cot.astype(F32), axis=0),
        ]
    )
    vectors = vectors.reshape(9, 2, 384).transpose(1, 0, 2)
    vectors = jnp.concatenate([vectors, grad_up_bias.reshape(2, 4, 384), jnp.zeros((2, 3, 384), F32)], axis=1)
    chunks = jnp.concatenate(
        [
            wide_chunks(grad_w_up.astype(BF16)),
            tall_chunks(grad_w_down.astype(BF16)),
            wide_chunks(grad_w_out.astype(BF16)),
            wide_chunks(grad_w_qkv.astype(BF16)),
        ]
    )
    parts, v = reduce_gradients(chunks, vectors)
    return (
        output[None],
        grad_patches[None],
        v[0],
        v[1],
        v[2],
        wide_whole(parts[18:]),
        v[3],
        v[4],
        wide_whole(parts[16:18]),
        v[5],
        v[6],
        v[7],
        wide_whole(parts[:8]),
        v[9:13].reshape(-1),
        tall_whole(parts[8:16]),
        v[8],
    )


def shards(
    patches,
    segment_ids,
    mask_positions,
    mask_embed,
    norm1_gain,
    norm1_bias,
    w_qkv,
    query_bias,
    value_bias,
    w_out,
    out_bias,
    norm2_gain,
    norm2_bias,
    w_up,
    up_bias,
    w_down,
    down_bias,
    cotangent,
):
    rows_n, time_n, width = patches.shape
    query_scale = 1.0 / math.sqrt(HEAD)
    gain_one = norm1_gain.astype(jnp.float32)
    gain_two = norm2_gain.astype(jnp.float32)
    offset = lax.axis_index("tm") * time_n
    places = offset + lax.broadcasted_iota(jnp.int32, (rows_n, time_n, 1), 1)
    masked = jnp.any(places == mask_positions[:, None, :], axis=-1)[..., None]
    inputs = jnp.where(
        masked, mask_embed.astype(jnp.float32)[None, None, :], patches.astype(jnp.float32)
    )
    normed1, inverse1 = normalize(inputs)
    hidden1 = (normed1 * gain_one + norm1_bias.astype(jnp.float32)).astype(jnp.bfloat16)
    project = jnp.einsum("rtd,de->rte", hidden1, w_qkv, preferred_element_type=jnp.float32)
    queries = ((project[..., :width] + query_bias.astype(jnp.float32)) * query_scale).astype(
        jnp.bfloat16
    )
    keys_own = project[..., width : 2 * width].astype(jnp.bfloat16)
    values_own = (project[..., 2 * width :] + value_bias.astype(jnp.float32)).astype(jnp.bfloat16)
    keys_all, values_all, segments_all = (
        lax.all_gather(keys_own, "tm", axis=1, tiled=True),
        lax.all_gather(values_own, "tm", axis=1, tiled=True),
        lax.all_gather(segment_ids, "tm", axis=1, tiled=True),
    )
    same = segment_ids[:, :, None] == segments_all[:, None, :]
    query_heads = split_heads(queries)
    head_outputs, log_totals = attend_forward(
        query_heads, split_heads(keys_all), split_heads(values_all), same
    )
    attended = join_heads(head_outputs).astype(jnp.bfloat16)
    middle = (
        inputs
        + jnp.einsum("rtd,de->rte", attended, w_out, preferred_element_type=jnp.float32)
        + out_bias.astype(jnp.float32)
    )
    normed2, inverse2 = normalize(middle)
    hidden2 = (normed2 * gain_two + norm2_bias.astype(jnp.float32)).astype(jnp.bfloat16)
    upper = jnp.einsum(
        "rtd,df->rtf", hidden2, w_up, preferred_element_type=jnp.float32
    ) + up_bias.astype(jnp.float32)
    activated = jax.nn.gelu(upper, approximate=False).astype(jnp.bfloat16)
    result = (
        middle
        + jnp.einsum("rtf,fd->rtd", activated, w_down, preferred_element_type=jnp.float32)
        + down_bias.astype(jnp.float32)
    )
    output = result.astype(jnp.bfloat16)
    grad_result = cotangent.astype(jnp.float32)
    grad_w_down = jnp.einsum(
        "rtf,rtd->fd", activated, cotangent, preferred_element_type=jnp.float32
    )
    grad_down_bias = total_rows(grad_result)
    grad_activated = jnp.einsum(
        "rtd,fd->rtf", cotangent, w_down, preferred_element_type=jnp.float32
    )
    unused, gelu_pull = jax.vjp(partial(jax.nn.gelu, approximate=False), upper)
    grad_upper = gelu_pull(grad_activated)[0].astype(jnp.bfloat16)
    grad_w_up = jnp.einsum("rtd,rtf->df", hidden2, grad_upper, preferred_element_type=jnp.float32)
    grad_up_bias = total_rows(grad_upper)
    grad_hidden2 = jnp.einsum("rtf,df->rtd", grad_upper, w_up, preferred_element_type=jnp.float32)
    grad_gain_two = total_rows(grad_hidden2 * normed2)
    grad_bias_two = total_rows(grad_hidden2)
    grad_middle = grad_result + norm_back(grad_hidden2, normed2, inverse2, gain_two)
    mlp_vectors = jnp.stack([grad_gain_two, grad_bias_two, grad_down_bias], axis=1)
    grad_branch = grad_middle.astype(jnp.bfloat16)
    grad_w_out = jnp.einsum(
        "rtd,rte->de", attended, grad_branch, preferred_element_type=jnp.float32
    )
    grad_out_bias = total_rows(grad_branch)
    grad_attended = jnp.einsum(
        "rte,de->rtd", grad_branch, w_out, preferred_element_type=jnp.float32
    ).astype(jnp.bfloat16)
    keys_back, values_back, segments_back = (
        lax.all_gather(keys_own, "tm", axis=1, tiled=True),
        lax.all_gather(values_own, "tm", axis=1, tiled=True),
        lax.all_gather(segment_ids, "tm", axis=1, tiled=True),
    )
    same_back = segment_ids[:, :, None] == segments_back[:, None, :]
    grad_query_h, grad_keys_h, grad_values_h = attend_backward(
        query_heads,
        split_heads(keys_back),
        split_heads(values_back),
        split_heads(grad_attended),
        log_totals,
        same_back,
    )
    grad_keys, grad_values = (
        lax.psum_scatter(
            join_heads(grad_keys_h).astype(jnp.bfloat16), "tm", scatter_dimension=1, tiled=True
        ).astype(jnp.float32),
        lax.psum_scatter(
            join_heads(grad_values_h).astype(jnp.bfloat16), "tm", scatter_dimension=1, tiled=True
        ).astype(jnp.float32),
    )
    grad_queries = join_heads(grad_query_h).astype(jnp.bfloat16)
    grad_project = jnp.concatenate(
        [
            (grad_queries.astype(jnp.float32) * query_scale).astype(jnp.bfloat16),
            grad_keys.astype(jnp.bfloat16),
            grad_values.astype(jnp.bfloat16),
        ],
        axis=-1,
    )
    grad_w_qkv = jnp.einsum(
        "rtd,rte->de", hidden1, grad_project, preferred_element_type=jnp.float32
    )
    grad_query_bias = total_rows(grad_project[..., :width])
    grad_value_bias = total_rows(grad_project[..., 2 * width :])
    grad_hidden1 = jnp.einsum(
        "rte,de->rtd", grad_project, w_qkv, preferred_element_type=jnp.float32
    )
    grad_gain_one = total_rows(grad_hidden1 * normed1)
    grad_bias_one = total_rows(grad_hidden1)
    grad_inputs = grad_middle + norm_back(grad_hidden1, normed1, inverse1, gain_one)
    grad_mask = total_rows(jnp.where(masked, grad_inputs, 0.0))
    grad_patches = jnp.where(masked, 0.0, grad_inputs).astype(jnp.bfloat16)
    attn_vectors = jnp.stack(
        [grad_mask, grad_gain_one, grad_bias_one, grad_query_bias, grad_value_bias, grad_out_bias],
        axis=1,
    )
    every_part = (
        lax.psum_scatter(
            grad_w_qkv.astype(jnp.bfloat16), "tm", scatter_dimension=0, tiled=True
        ).astype(jnp.float32),
        lax.psum_scatter(
            grad_w_out.astype(jnp.bfloat16), "tm", scatter_dimension=0, tiled=True
        ).astype(jnp.float32),
        lax.psum_scatter(
            attn_vectors.astype(jnp.bfloat16), "tm", scatter_dimension=0, tiled=True
        ).astype(jnp.float32),
        lax.psum_scatter(
            grad_w_up.astype(jnp.bfloat16), "tm", scatter_dimension=0, tiled=True
        ).astype(jnp.float32),
        lax.psum_scatter(
            grad_w_down.astype(jnp.bfloat16), "tm", scatter_dimension=0, tiled=True
        ).astype(jnp.float32),
        lax.psum_scatter(
            mlp_vectors.astype(jnp.bfloat16), "tm", scatter_dimension=0, tiled=True
        ).astype(jnp.float32),
        lax.psum_scatter(
            grad_up_bias.astype(jnp.bfloat16), "tm", scatter_dimension=0, tiled=True
        ).astype(jnp.float32),
    )
    every_part = (
        lax.psum(every_part[0].astype(jnp.bfloat16), "rows").astype(jnp.float32),
        lax.psum(every_part[1].astype(jnp.bfloat16), "rows").astype(jnp.float32),
        lax.psum(every_part[2].astype(jnp.bfloat16), "rows").astype(jnp.float32),
        lax.psum(every_part[3].astype(jnp.bfloat16), "rows").astype(jnp.float32),
        lax.psum(every_part[4].astype(jnp.bfloat16), "rows").astype(jnp.float32),
        lax.psum(every_part[5].astype(jnp.bfloat16), "rows").astype(jnp.float32),
        lax.psum(every_part[6].astype(jnp.bfloat16), "rows").astype(jnp.float32),
    )
    summed_qkv, summed_out, summed_attn, summed_up, summed_down, summed_mlp, summed_up_bias = (
        every_part
    )
    return (
        output,
        grad_patches,
        summed_attn[:, 0],
        summed_attn[:, 1],
        summed_attn[:, 2],
        summed_qkv,
        summed_attn[:, 3],
        summed_attn[:, 4],
        summed_out,
        summed_attn[:, 5],
        summed_mlp[:, 0],
        summed_mlp[:, 1],
        summed_up,
        summed_up_bias,
        summed_down,
        summed_mlp[:, 2],
    )


def solution(mesh):
    placed = (
        P("rows", "tm", None),
        P("rows", "tm"),
        P("rows", None),
        P(),
        P(),
        P(),
        P(),
        P(),
        P(),
        P(),
        P(),
        P(),
        P(),
        P(),
        P(),
        P(),
        P(),
        P("rows", "tm", None),
    )
    return jax.shard_map(
        block_shards if dict(mesh.shape) == {"rows": 16, "tm": 2} else shards,
        mesh=mesh,
        in_specs=placed,
        out_specs=(
            P("rows", "tm", None),
            P("rows", "tm", None),
            P("tm"),
            P("tm"),
            P("tm"),
            P("tm", None),
            P("tm"),
            P("tm"),
            P("tm", None),
            P("tm"),
            P("tm"),
            P("tm"),
            P("tm", None),
            P("tm"),
            P("tm", None),
            P("tm"),
        ),
        check_vma=False,
    )
```

```python
from functools import partial
import math

import jax
import jax.numpy as jnp
from jax import lax
from jax.experimental import pallas as pl
from jax.experimental.pallas import tpu as pltpu
from jax.sharding import PartitionSpec as P

HEADS = 12
HEAD = 64


norm_eps = 1e-06
neg_large = -1e30


def normalize(values):
    center = values - jnp.mean(values, axis=-1, keepdims=True)
    scale_inv = lax.rsqrt(jnp.mean(center * center, axis=-1, keepdims=True) + norm_eps)
    return (center * scale_inv, scale_inv)


def norm_back(grad_out, normed, scale_inv, norm_gain):
    grad_normed = grad_out * norm_gain
    mean_one = jnp.mean(grad_normed, axis=-1, keepdims=True)
    mean_two = jnp.mean(grad_normed * normed, axis=-1, keepdims=True)
    return scale_inv * (grad_normed - mean_one - normed * mean_two)


def split_heads(tensor):
    rows_n, length, width = tensor.shape
    return tensor.reshape(rows_n, length, HEADS, width // HEADS).transpose(2, 0, 1, 3)


def join_heads(tensor):
    heads_n, rows_n, length, size = tensor.shape
    return tensor.transpose(1, 2, 0, 3).reshape(rows_n, length, heads_n * size)


def head_scores(query, keys_h, same):
    scores = jnp.einsum("rqd,rkd->rqk", query, keys_h, preferred_element_type=jnp.float32)
    return jnp.where(same, scores, neg_large)


def attend_forward(query_heads, key_heads, value_heads, same):

    def one_head(operands):
        query, keys_h, values_h = operands
        scores = head_scores(query, keys_h, same)
        peak = jnp.max(scores, axis=-1, keepdims=True)
        total = jnp.sum(jnp.exp(scores - peak), axis=-1, keepdims=True)
        log_total = peak + jnp.log(total)
        weights = jnp.exp(scores - log_total).astype(jnp.bfloat16)
        result = jnp.einsum("rqk,rkd->rqd", weights, values_h, preferred_element_type=jnp.float32)
        return (result, log_total[..., 0])

    return lax.map(one_head, (query_heads, key_heads, value_heads))


def attend_backward(query_heads, key_heads, value_heads, grad_heads, log_totals, same):

    def one_head(operands):
        query, keys_h, values_h, grad_out, log_total = operands
        scores = head_scores(query, keys_h, same)
        probs_full = jnp.exp(scores - log_total[..., None])
        probs_low = probs_full.astype(jnp.bfloat16)
        grad_values = jnp.einsum(
            "rqk,rqd->rkd", probs_low, grad_out, preferred_element_type=jnp.float32
        )
        grad_probs = jnp.einsum(
            "rqd,rkd->rqk", grad_out, values_h, preferred_element_type=jnp.float32
        )
        delta = jnp.sum(grad_probs * probs_full, axis=-1, keepdims=True)
        grad_scores = (probs_full * (grad_probs - delta)).astype(jnp.bfloat16)
        grad_query = jnp.einsum(
            "rqk,rkd->rqd", grad_scores, keys_h, preferred_element_type=jnp.float32
        )
        grad_keys = jnp.einsum(
            "rqk,rqd->rkd", grad_scores, query, preferred_element_type=jnp.float32
        )
        return (grad_query, grad_keys, grad_values)

    return lax.map(one_head, (query_heads, key_heads, value_heads, grad_heads, log_totals))


MESH = pl.DeviceIdType.MESH
SUB = 96
COLS = 384
LAGS = (0, 1, 3, 4, 5, 7, 8, 9)


def places():
    row = lax.axis_index("rows")
    y = lax.axis_index("tm")
    core = row % 2
    x = (row // 2) % 2
    z_low = (row // 4) % 2
    z_high = row // 8
    peers = (
        (row + 1 - 2 * core, y),
        (row, 1 - y),
        (row + 2 - 4 * x, y),
        (row + 4 - 8 * z_low, y),
        (row + 8 - 16 * z_high, y),
    )
    return core, x, y, peers


def greet(peers):
    barrier = pltpu.get_barrier_semaphore()
    for peer in peers:
        pl.semaphore_signal(barrier, inc=1, device_id=peer, device_id_type=MESH)
    pl.semaphore_wait(barrier, len(peers))


def total_rows(tensor):
    return jnp.sum(tensor.astype(jnp.float32), axis=(0, 1))


VMEM = pltpu.VMEM
F32 = jnp.float32
BF16 = jnp.bfloat16
HALF = 512
TILE = 256
R_EMBED, R_G1, R_B1, R_QB, R_VB, R_OB, R_G2, R_B2, R_DB, R_UB = 0, 1, 2, 3, 4, 5, 6, 7, 8, 9
QUERY_SCALE = 1.0 / math.sqrt(HEAD)


def dot(a, b):
    return lax.dot_general(a, b, (((1,), (0,)), ((), ())), preferred_element_type=F32)


def dot_t(a, b):
    return lax.dot_general(a, b, (((1,), (1,)), ((), ())), preferred_element_type=F32)


def t_dot(a, b):
    return lax.dot_general(a, b, (((0,), (0,)), ((), ())), preferred_element_type=F32)


def standard(values):
    center = values - jnp.mean(values, axis=-1, keepdims=True)
    scale_inv = lax.rsqrt(jnp.mean(center * center, axis=-1, keepdims=True) + norm_eps)
    return center * scale_inv, scale_inv


def masked_inputs(patch, first, marks, embed):
    at = first + lax.broadcasted_iota(jnp.int32, (patch.shape[0], 1), 0)
    flagged = jnp.max(jnp.where(at == marks, 1.0, 0.0), axis=-1, keepdims=True) > 0.5
    return flagged, jnp.where(flagged, embed, patch.astype(F32))


def front_kernel(other, p_ref, marks_ref, table_ref, w_ref, h1_ref, qkv_ref):
    y = lax.axis_index("tm")
    first = (1 - y if other else y) * HALF + pl.program_id(0) * TILE
    unused, inputs = masked_inputs(p_ref[...], first, marks_ref[...], table_ref[R_EMBED : R_EMBED + 1, :])
    normed, unused = standard(inputs)
    hidden = (normed * table_ref[R_G1 : R_G1 + 1, :] + table_ref[R_B1 : R_B1 + 1, :]).astype(BF16)
    h1_ref[...] = hidden
    for part in range(6):
        cols = slice(part * 384, part * 384 + 384)
        project = dot(hidden, w_ref[:, cols])
        bias = slice((part % 2) * 384, (part % 2) * 384 + 384)
        if part < 2:
            project = (project + table_ref[R_QB : R_QB + 1, bias]) * QUERY_SCALE
        elif part >= 4:
            project = project + table_ref[R_VB : R_VB + 1, bias]
        qkv_ref[:, cols] = project.astype(BF16)


def front(other, patch, marks, table, w_qkv):
    return pl.pallas_call(
        partial(front_kernel, other),
        grid=(HALF // TILE,),
        out_shape=(
            jax.ShapeDtypeStruct((HALF, 768), BF16),
            jax.ShapeDtypeStruct((HALF, 2304), BF16),
        ),
        in_specs=[
            pl.BlockSpec((TILE, 768), lambda i: (i, 0)),
            pl.BlockSpec(marks.shape, lambda i: (0, 0)),
            pl.BlockSpec(table.shape, lambda i: (0, 0)),
            pl.BlockSpec((768, 2304), lambda i: (0, 0), pipeline_mode=pl.Buffered(1)),
        ],
        out_specs=(
            pl.BlockSpec((TILE, 768), lambda i: (i, 0)),
            pl.BlockSpec((TILE, 2304), lambda i: (i, 0)),
        ),
        cost_estimate=pl.CostEstimate(flops=2 * HALF * 768 * 2304, bytes_accessed=8 << 20, transcendentals=0),
    )(patch, marks, table, w_qkv)


def attend_kernel(q_ref, k_ref, v_ref, kx_ref, vx_ref, qa_ref, ka_ref, kxa_ref, o_ref, lse_ref):
    y = lax.axis_index("tm")
    pair = pl.program_id(0)
    lane = lax.broadcasted_iota(jnp.int32, (1, 128), 1)
    keys = jnp.concatenate([k_ref[...], ka_ref[...]], axis=1)
    far_keys = jnp.concatenate([kx_ref[...], kxa_ref[...]], axis=1)
    near_x = pl.multiple_of(y * TILE, TILE)
    near_keys = jnp.concatenate([kx_ref[pl.ds(near_x, TILE), :], kxa_ref[pl.ds(near_x, TILE), :]], axis=1)
    for far in range(2):
        rows = pl.ds(pl.multiple_of((y if far else 1 - y) * TILE, TILE), TILE)
        q = q_ref[rows, :]
        qa = qa_ref[rows, :]
        kept = None
        marks = jnp.where(pair == 0, 0.0, lse_ref[rows, :])
        for h in range(2):
            mine = (lane // 64) == h
            query = jnp.concatenate([jnp.where(mine, q, 0), qa], axis=1)
            own = dot_t(query, keys)
            cross = dot_t(query, near_keys if far else far_keys)
            peak = jnp.maximum(jnp.max(own, axis=-1, keepdims=True), jnp.max(cross, axis=-1, keepdims=True))
            own = jnp.exp(own - peak)
            cross = jnp.exp(cross - peak)
            total = jnp.sum(own, axis=-1, keepdims=True) + jnp.sum(cross, axis=-1, keepdims=True)
            values = vx_ref[pl.ds(near_x, TILE), :] if far else vx_ref[...]
            out = dot(own.astype(BF16), v_ref[...]) + dot(cross.astype(BF16), values)
            out = out / total
            kept = out if h == 0 else jnp.where(mine, out, kept)
            marks = jnp.where(lane == 2 * pair + h, peak + jnp.log(total), marks)
        o_ref[rows, :] = kept.astype(BF16)
        lse_ref[rows, :] = marks


def attend(qkv, qkv_other, qa, ka, kxa):
    def block(first):
        return pl.BlockSpec((HALF, 128), lambda i: (0, first + i))

    whole = pl.BlockSpec((HALF, 128), lambda i: (0, 0))
    return pl.pallas_call(
        attend_kernel,
        grid=(6,),
        out_shape=(jax.ShapeDtypeStruct((HALF, 768), BF16), jax.ShapeDtypeStruct((HALF, 128), F32)),
        in_specs=[block(0), block(6), block(12), block(6), block(12), whole, whole, whole],
        out_specs=(pl.BlockSpec((HALF, 128), lambda i: (0, i)), whole),
        cost_estimate=pl.CostEstimate(
            flops=4 * 12 * HALF * 1024 * 64, bytes_accessed=8 << 20, transcendentals=12 * HALF * 1024
        ),
    )(qkv, qkv, qkv, qkv_other, qkv_other, qa, ka, kxa)


ERFC_P = 0.3275911
ERFC_C = (
    0.1851102167482524,
    0.17993860771517878,
    0.21041948320823337,
    0.011498087426314028,
    0.47813345988158296,
    -0.4317659362057169,
    0.5111742647535956,
    -0.14450823957827402,
)


def gelu_and_slope(u):
    t = 1.0 / (1.0 + (ERFC_P * math.sqrt(0.5)) * jnp.abs(u))
    bell = jnp.exp(-0.5 * (u * u))
    series = ERFC_C[7]
    for c in ERFC_C[6::-1]:
        series = series * t + c
    tail = (0.5 * t) * series * bell
    phi = jnp.where(u < 0, tail, 1.0 - tail)
    return u * phi, phi + u * (bell * (1.0 / math.sqrt(2.0 * math.pi)))


FF_TILE = 384


def middle_kernel(
    p_ref, marks_ref, table_ref, a_ref, wo_ref, cot_ref, wu_ref, wd_ref, ub_ref, mid_ref, h2_ref, act_ref, gu_ref, ubs_ref
):
    y = lax.axis_index("tm")

    @pl.when(pl.program_id(0) == 0)
    def _():
        for tile in range(HALF // TILE):
            rows = slice(tile * TILE, tile * TILE + TILE)
            unused, inputs = masked_inputs(
                p_ref[rows, :], y * HALF + tile * TILE, marks_ref[...], table_ref[R_EMBED : R_EMBED + 1, :]
            )
            mid = inputs + dot(a_ref[rows, :], wo_ref[...]) + table_ref[R_OB : R_OB + 1, :]
            normed, unused = standard(mid)
            mid_ref[rows, :] = mid
            h2_ref[rows, :] = (normed * table_ref[R_G2 : R_G2 + 1, :] + table_ref[R_B2 : R_B2 + 1, :]).astype(BF16)

    sums = jnp.zeros((1, FF_TILE), F32)
    for tile in range(HALF // TILE):
        rows = slice(tile * TILE, tile * TILE + TILE)
        upper = dot(h2_ref[rows, :], wu_ref[...]) + ub_ref[...]
        value, slope = gelu_and_slope(upper)
        act_ref[rows, :] = value.astype(BF16)
        grad = dot_t(cot_ref[rows, :], wd_ref[...])
        low = (grad * slope).astype(BF16)
        gu_ref[rows, :] = low
        sums = sums + jnp.sum(low.astype(F32), axis=0, keepdims=True)
    ubs_ref[...] = sums


def middle_part(patch, marks, table, attended, w_out, cot, w_up, w_down, up_bias):
    def full(shape):
        return pl.BlockSpec(shape, lambda i: (0, 0))

    return pl.pallas_call(
        middle_kernel,
        grid=(3072 // FF_TILE,),
        out_shape=(
            jax.ShapeDtypeStruct((HALF, 768), F32),
            jax.ShapeDtypeStruct((HALF, 768), BF16),
            jax.ShapeDtypeStruct((HALF, 3072), BF16),
            jax.ShapeDtypeStruct((HALF, 3072), BF16),
            jax.ShapeDtypeStruct((1, 3072), F32),
        ),
        in_specs=[
            full((HALF, 768)),
            full(marks.shape),
            full(table.shape),
            full((HALF, 768)),
            full((768, 768)),
            full((HALF, 768)),
            pl.BlockSpec((768, FF_TILE), lambda i: (0, i)),
            pl.BlockSpec((FF_TILE, 768), lambda i: (i, 0)),
            pl.BlockSpec((1, FF_TILE), lambda i: (0, i)),
        ],
        out_specs=(
            full((HALF, 768)),
            full((HALF, 768)),
            pl.BlockSpec((HALF, FF_TILE), lambda i: (0, i)),
            pl.BlockSpec((HALF, FF_TILE), lambda i: (0, i)),
            pl.BlockSpec((1, FF_TILE), lambda i: (0, i)),
        ),
        cost_estimate=pl.CostEstimate(
            flops=2 * HALF * 768 * (768 + 6144), bytes_accessed=24 << 20, transcendentals=HALF * 3072
        ),
    )(patch, marks, table, attended, w_out, cot, w_up, w_down, up_bias)


CHUNKS = 24
T_OWN = 6
T_LAST = 24
T_VEC = 28


def halves_kernel(
    act_h, cot_h, gu_h, mid_h, h2_h, wo_h, qkv_h, qkvx_h, att_h, h1_h, patch_h, wq_h, wu_h, wd_h,
    qa_ref, ka_ref, qxa_ref, kxa_ref, lse_ref, lsex_ref, table_ref, marks_ref, ub_ref,
    parts_h, out_h, gp_h, vec_out,
    act, cot, gu, mid, h2, wo, qkv, qkvx, att, h1, patch, wq, wu, wd,
    acc, gb, do, dox, dqkv, dq, dk, dv, drow, dxrow,
    g, r1, r2, r3, r4, r5, done, v0, v1, v2,
    insem, wusem, wdsem, ssem, rsem, vs, vr, xs, xr, outsem, lastsem,
):
    core, x, y, peers = places()
    pair, yp, xp, zp1, zp2 = peers
    lane = lax.broadcasted_iota(jnp.int32, (1, 128), 1)
    inputs = (
        (act_h, act), (cot_h, cot), (gu_h, gu), (mid_h, mid), (h2_h, h2), (wo_h, wo),
        (qkv_h, qkv), (att_h, att), (qkvx_h, qkvx), (h1_h, h1), (patch_h, patch), (wq_h, wq),
    )
    ACT, COT, GU, MID, H2, WO, QKV, ATT, QKVX, H1, PATCH, WQ = range(12)

    def load(i):
        return pltpu.make_async_copy(inputs[i][0], inputs[i][1], insem.at[i])

    def up_tile(k):
        cols = pl.ds(pl.multiple_of(k * 512, 512), 512)
        return pltpu.make_async_copy(wu_h.at[:, cols], wu.at[k % 2], wusem.at[k % 2])

    def down_tile(k):
        rows = pl.ds(pl.multiple_of(k * 512, 512), 512)
        return pltpu.make_async_copy(wd_h.at[rows, :], wd.at[k % 2], wdsem.at[k % 2])

    for i in (ACT, COT, GU):
        load(i).start()
    up_tile(0).start()
    up_tile(1).start()
    for i in (MID, H2, WO, QKV, ATT, QKVX, H1, PATCH, WQ):
        load(i).start()
    down_tile(0).start()
    down_tile(1).start()
    greet(peers)

    def remote(src, dst, send, recv, dev):
        return pltpu.make_async_remote_copy(
            src_ref=src, dst_ref=dst, send_sem=send, recv_sem=recv, device_id=dev, device_id_type=MESH
        )

    def copy(s, c):
        src, dst, dev = (
            lambda: (g.at[c % 4, 1 - core], r1.at[c], pair),
            lambda: (r1.at[c, 1 - y], r2.at[c], yp),
            lambda: (r2.at[c, 1 - x], r3.at[c], xp),
            lambda: (r3.at[c], r4.at[c], zp1),
            lambda: (r4.at[c], r5.at[c], zp2),
            lambda: (done.at[c, core, x], done.at[c, core, x], xp),
            lambda: (done.at[c, core], done.at[c, core], pair),
        )[s]()
        return remote(src, dst, ssem.at[s, c], rsem.at[s, c], dev)

    def part_out(c):
        return pltpu.make_async_copy(done.at[c], parts_h.at[c], outsem.at[c])

    def stage(s, c):
        if s > 0:
            copy(s - 1, c).wait_recv()
        if s == 1:
            r1[c] = r1[c] + g[c % 4, core]
        elif s == 2:
            r2[c] = r2[c] + r1[c, y]
        elif s == 3:
            r3[c] = r3[c] + r2[c, x]
        elif s == 4:
            r4[c] = r4[c] + r3[c]
        elif s == 5:
            done[c, core, x] = r5[c] + r4[c]
        elif s == 7:
            copy(5, c).wait_send()
            copy(6, c).wait_send()
            part_out(c).start()
        if s < 7:
            copy(s, c).start()

    def vec_copy(s):
        src, dst, dev = (
            lambda: (v0, v1, pair),
            lambda: (v1.at[1 - y], v2.at[0], yp),
            lambda: (v2.at[0], v2.at[1], xp),
            lambda: (v2.at[1], v2.at[2], zp1),
            lambda: (v2.at[2], v2.at[3], zp2),
        )[s]()
        return remote(src, dst, vs.at[s], vr.at[s], dev)

    def vec_stage(s):
        if s > 0:
            vec_copy(s - 1).wait_recv()
        if s == 1:
            v1[...] = v1[...] + v0[...]
        elif s == 2:
            v2[0] = v2[0] + v1[y]
        elif s == 5:
            vec_out[...] = v2[3] + v2[2]
        elif s > 2:
            v2[s - 2] = v2[s - 2] + v2[s - 3]
        if s < 5:
            vec_copy(s).start()

    def far_copy(i):
        src, dst = ((do, dox), (drow, dxrow))[i]
        return remote(src, dst, xs.at[i], xr.at[i], yp)

    def row(r):
        return table_ref[r : r + 1, :]

    def add_vec(r, value):
        for half in range(2):
            v0[half, r : r + 1, :] = v0[half, r : r + 1, :] + value[:, half * 384 : half * 384 + 384]

    def emit(left, right, c):
        number = right.shape[1] // 384
        for i in range(number):

            @pl.when(c + i >= 4)
            def _():
                copy(0, c + i - 4).wait_send()

        for half in range(2):
            block = t_dot(left(half), right).astype(BF16)
            for i in range(number):
                for other in range(4):
                    rows = slice(other * SUB, other * SUB + SUB)
                    g[(c + i) % 4, other // 2, half, other % 2] = block[rows, i * 384 : i * 384 + 384]

    def lanes(start, size=128):
        return pl.ds(pl.multiple_of(start, 128), size)

    def grad_hidden(k):
        up_tile(k).wait()
        for tile in range(2):
            rows = slice(tile * 256, tile * 256 + 256)
            acc[rows, :] = acc[rows, :] + dot_t(gu[rows, lanes(k * 512, 512)], wu[k % 2])

        @pl.when(k + 2 < 6)
        def _():
            up_tile(k + 2).start()

    def second_norm():
        def tile(i, carry):
            rows = pl.ds(pl.multiple_of(i * 128, 128), 128)
            normed, inverse = standard(mid[rows, :])
            grad = acc[rows, :]
            cotangent = cot[rows, :].astype(F32)
            add_vec(6, jnp.sum(grad * normed, axis=0, keepdims=True))
            add_vec(7, jnp.sum(grad, axis=0, keepdims=True))
            add_vec(8, jnp.sum(cotangent, axis=0, keepdims=True))
            total = cotangent + norm_back(grad, normed, inverse, row(R_G2))
            acc[rows, :] = total
            low = total.astype(BF16)
            gb[rows, :] = low
            add_vec(5, jnp.sum(low.astype(F32), axis=0, keepdims=True))
            return carry

        lax.fori_loop(0, 4, tile, 0)

    def grad_attended():
        for tile in range(2):
            rows = slice(tile * 256, tile * 256 + 256)
            do[rows, :] = dot_t(gb[rows, :], wo[...]).astype(BF16)
        for tile in range(4):
            rows = slice(tile * 128, tile * 128 + 128)
            columns = jnp.zeros((128, 128), F32)
            for p in range(6):
                cols = slice(p * 128, p * 128 + 128)
                product = do[rows, cols].astype(F32) * att[rows, cols].astype(F32)
                for h in range(2):
                    total = jnp.sum(jnp.where((lane // 64) == h, product, 0.0), axis=1, keepdims=True)
                    columns = jnp.where(lane == 2 * p + h, total, columns)
            drow[:, rows] = columns.T[:16, :]
        far_copy(0).start()
        far_copy(1).start()

    def piece(keys, key_mask, values, query, query_mask, grad, lse, delta):
        scores = dot_t(jnp.concatenate([keys, key_mask], axis=1), jnp.concatenate([query, query_mask], axis=1))
        probs = jnp.exp(scores - lse)
        grad_scores = probs * (dot_t(values, grad) - delta)
        return probs.astype(BF16), grad_scores.astype(BF16)

    def own_pair(p):
        slot = p % 3

        def head(h, carry):
            mine = (lane // 64) == h
            stat = pl.ds(2 * p + h, 1)
            query = jnp.where(mine, qkv[:, lanes(p * 128)], 0)
            grad = jnp.where(mine, do[:, lanes(p * 128)], 0)
            for tile in range(2):
                rows = slice(tile * 256, tile * 256 + 256)
                keys = qkv[rows, lanes(768 + p * 128)]
                probs, scores = piece(
                    keys, ka_ref[rows, :], qkv[rows, lanes(1536 + p * 128)], query, qa_ref[...], grad,
                    lse_ref[stat, :], drow[stat, :],
                )
                new = dot(scores, query)
                dk[slot, rows, :] = jnp.where(h == 0, new, dk[slot, rows, :] + new)
                new = dot(probs, grad)
                dv[slot, rows, :] = jnp.where(h == 0, new, dv[slot, rows, :] + new)
                new = t_dot(scores, jnp.where(mine, keys, 0))
                dq[slot] = jnp.where((h == 0) & (tile == 0), new, dq[slot] + new)
            return carry

        lax.fori_loop(0, 2, head, 0)

    def far_pair(p):
        slot = p % 3
        near, far = pl.multiple_of((1 - y) * 256, 256), pl.multiple_of(y * 256, 256)

        def head(h, carry):
            mine = (lane // 64) == h
            stat = pl.ds(2 * p + h, 1)
            for first, start, size in ((far, 0, 512), (near, near, 256)):
                rows, others = pl.ds(first, 256), pl.ds(start, size)
                query = jnp.where(mine, qkv[others, lanes(p * 128)], 0)
                grad = jnp.where(mine, do[others, lanes(p * 128)], 0)
                keys = qkvx[rows, lanes(768 + p * 128)]
                probs, scores = piece(
                    keys, kxa_ref[rows, :], qkvx[rows, lanes(1536 + p * 128)], query, qa_ref[others, :], grad,
                    lse_ref[stat, others], drow[stat, others],
                )
                dq[slot, others, :] = dq[slot, others, :] + t_dot(scores, jnp.where(mine, keys, 0))
            for first, start, size in ((near, 0, 512), (far, far, 256)):
                rows, others = pl.ds(first, 256), pl.ds(start, size)
                query = jnp.where(mine, qkvx[others, lanes(p * 128)], 0)
                grad = jnp.where(mine, dox[others, lanes(p * 128)], 0)
                probs, scores = piece(
                    qkv[rows, lanes(768 + p * 128)], ka_ref[rows, :], qkv[rows, lanes(1536 + p * 128)],
                    query, qxa_ref[others, :], grad, lsex_ref[stat, others], dxrow[stat, others],
                )
                dk[slot, rows, :] = dk[slot, rows, :] + dot(scores, query)
                dv[slot, rows, :] = dv[slot, rows, :] + dot(probs, grad)
            return carry

        lax.fori_loop(0, 2, head, 0)
        dqkv[:, lanes(p * 128)] = (dq[slot].astype(BF16).astype(F32) * QUERY_SCALE).astype(BF16)
        dqkv[:, lanes(768 + p * 128)] = dk[slot].astype(BF16)
        dqkv[:, lanes(1536 + p * 128)] = dv[slot].astype(BF16)

    def output_tile(k):
        down_tile(k).wait()
        for tile in range(2):
            rows = slice(tile * 256, tile * 256 + 256)
            mid[rows, :] = mid[rows, :] + dot(act[rows, lanes(k * 512, 512)], wd[k % 2])

        @pl.when(k + 2 < 6)
        def _():
            down_tile(k + 2).start()

    def store_output():
        for tile in range(4):
            rows = slice(tile * 128, tile * 128 + 128)
            gb[rows, :] = (mid[rows, :] + row(R_DB)).astype(BF16)
        pltpu.make_async_copy(gb, out_h, lastsem.at[0]).start()

    def grad_first(part):
        for tile in range(2):
            rows = slice(tile * 256, tile * 256 + 256)
            new = dot_t(dqkv[rows, lanes(part * 768, 768)], wq[:, lanes(part * 768, 768)])
            mid[rows, :] = jnp.where(part == 0, new, mid[rows, :] + new)

    def first_norm():
        def tile(i, carry):
            rows = pl.ds(pl.multiple_of(i * 128, 128), 128)
            flagged, values = masked_inputs(patch[rows, :], y * HALF + i * 128, marks_ref[...], row(R_EMBED))
            normed, inverse = standard(values)
            grad = mid[rows, :]
            add_vec(1, jnp.sum(grad * normed, axis=0, keepdims=True))
            add_vec(2, jnp.sum(grad, axis=0, keepdims=True))
            total = acc[rows, :] + norm_back(grad, normed, inverse, row(R_G1))
            add_vec(0, jnp.sum(jnp.where(flagged, total, 0.0), axis=0, keepdims=True))
            att[rows, :] = jnp.where(flagged, 0.0, total).astype(BF16)
            add_vec(3, jnp.sum(dqkv[rows, :768].astype(F32), axis=0, keepdims=True))
            add_vec(4, jnp.sum(dqkv[rows, 1536:].astype(F32), axis=0, keepdims=True))
            return carry

        lax.fori_loop(0, 4, tile, 0)
        pltpu.make_async_copy(att, gp_h, lastsem.at[1]).start()

    acc[...] = jnp.zeros_like(acc)
    v0[...] = jnp.zeros_like(v0)
    for half in range(2):
        for i in range(4):
            start = half * 1536 + i * 384
            v0[half, 9 + i : 10 + i, :] = ub_ref[:, start : start + 384]
    load(ACT).wait()
    load(COT).wait()

    def step(t, carry):
        even = t % 2 == 0

        @pl.when((t < 8) & even)
        def _():
            start = t * 192
            emit(lambda half: act[:, lanes(half * 1536 + start, 384)], cot[...], t)

        @pl.when((t >= 8) & (t < 16) & even)
        def _():
            emit(lambda half: h2[:, half * 384 : half * 384 + 384], gu[:, lanes((t - 8) * 384, 768)], t)

        @pl.when(t == 16)
        def _():
            emit(lambda half: att[:, half * 384 : half * 384 + 384], gb[...], t)

        @pl.when((t >= 18) & (t < 24))
        def _():
            p = t - 18
            right = jnp.concatenate([dqkv[:, lanes(part * 768 + p * 128)] for part in range(3)], axis=1)
            emit(lambda half: h1[:, half * 384 : half * 384 + 384], right, t)

        for s in range(2):
            c = t - LAGS[s]

            @pl.when((c >= 0) & (c < CHUNKS))
            def _():
                stage(s, c)

        @pl.when(t == 0)
        def _():
            load(GU).wait()

        @pl.when(t < 3)
        def _():
            grad_hidden(2 * t)
            grad_hidden(2 * t + 1)

        @pl.when(t == 3)
        def _():
            load(MID).wait()
            second_norm()

        @pl.when(t == 4)
        def _():
            for i in (WO, ATT):
                load(i).wait()
            grad_attended()

        u = t - T_OWN

        @pl.when(u == 0)
        def _():
            for i in (H2, QKV, QKVX, H1, PATCH, WQ):
                load(i).wait()

        @pl.when((u >= 0) & ((u <= 2) | ((u <= 8) & (u % 2 == 0))))
        def _():
            own_pair(jnp.where(u <= 2, u, (u + 2) // 2))

        @pl.when(u == 3)
        def _():
            far_copy(0).wait_recv()
            far_copy(1).wait_recv()

        @pl.when((u >= 3) & (u <= 11) & ((u >= 10) | (u % 2 == 1)))
        def _():
            far_pair(jnp.where(u <= 9, (u - 3) // 2, u - 6))

        @pl.when((t >= 18) & (t < 24))
        def _():
            output_tile(t - 18)

        @pl.when(t == 23)
        def _():
            store_output()

        @pl.when((t >= T_LAST) & (t < T_LAST + 3))
        def _():
            grad_first(t - T_LAST)

        @pl.when(t == T_LAST + 3)
        def _():
            first_norm()

        for s in range(2, 8):
            c = t - LAGS[s]

            @pl.when((c >= 0) & (c < CHUNKS))
            def _():
                stage(s, c)

        for s in range(6):

            @pl.when(t == T_VEC + s)
            def _():
                vec_stage(s)

        return carry

    lax.fori_loop(0, T_VEC + 6, step, 0)

    def drain(c, carry):
        for s in range(1, 5):
            copy(s, c).wait_send()
        part_out(c).wait()
        return carry

    lax.fori_loop(0, CHUNKS, drain, 0)
    for c in range(CHUNKS - 4, CHUNKS):
        copy(0, c).wait_send()
    for s in range(5):
        vec_copy(s).wait_send()
    for i in range(2):
        far_copy(i).wait_send()
    pltpu.make_async_copy(gb, out_h, lastsem.at[0]).wait()
    pltpu.make_async_copy(att, gp_h, lastsem.at[1]).wait()


def backward(big, weights, small):
    hbm = pl.BlockSpec(memory_space=pl.ANY)
    near = pl.BlockSpec(memory_space=pltpu.VMEM)

    def low(*shape):
        return pltpu.VMEM(shape, BF16)

    def full(*shape):
        return pltpu.VMEM(shape, F32)

    dma = pltpu.SemaphoreType.DMA
    held = [pltpu.VMEM(a.shape, a.dtype) for a in big]
    return pl.pallas_call(
        halves_kernel,
        out_shape=(
            jax.ShapeDtypeStruct((CHUNKS, 2, 2, SUB, COLS), BF16),
            jax.ShapeDtypeStruct((HALF, 768), BF16),
            jax.ShapeDtypeStruct((HALF, 768), BF16),
            jax.ShapeDtypeStruct((16, COLS), F32),
        ),
        in_specs=[hbm] * (len(big) + 2) + [near] * len(small),
        out_specs=(hbm, hbm, hbm, near),
        scratch_shapes=held
        + [
            low(2, 768, 512),
            low(2, 512, 768),
            full(HALF, 768),
            low(HALF, 768),
            low(HALF, 768),
            low(HALF, 768),
            low(HALF, 2304),
            full(3, HALF, 128),
            full(3, HALF, 128),
            full(3, HALF, 128),
            full(16, HALF),
            full(16, HALF),
            low(4, 2, 2, 2, SUB, COLS),
            low(CHUNKS, 2, 2, SUB, COLS),
            low(CHUNKS, 2, SUB, COLS),
            low(CHUNKS, SUB, COLS),
            low(CHUNKS, SUB, COLS),
            low(CHUNKS, SUB, COLS),
            low(CHUNKS, 2, 2, SUB, COLS),
            full(2, 16, COLS),
            full(2, 16, COLS),
            full(4, 16, COLS),
            dma((12,)),
            dma((2,)),
            dma((2,)),
            dma((7, CHUNKS)),
            dma((7, CHUNKS)),
            dma((5,)),
            dma((5,)),
            dma((2,)),
            dma((2,)),
            dma((CHUNKS,)),
            dma((2,)),
        ],
        compiler_params=pltpu.CompilerParams(
            collective_id=0, has_side_effects=True, vmem_limit_bytes=67043328
        ),
    )(*big, *weights, *small)


def widen_kernel(pair_ref, qkv_ref, down_ref, up_ref, out_ref, proj_ref):
    i = pl.program_id(0)
    for first, last, ref in ((0, 4, down_ref), (4, 8, up_ref), (8, 9, out_ref)):

        @pl.when((i >= first) & (i < last))
        def _():
            for c in range(2):
                ref[:, c * 384 : c * 384 + 384] = pair_ref[c].astype(F32)

    @pl.when(i >= 9)
    def _():
        for p in range(6):
            proj_ref[:, p * 128 : p * 128 + 128] = qkv_ref[p].astype(F32)


def widen(parts):
    parts = parts.reshape(CHUNKS, 384, COLS)
    return pl.pallas_call(
        widen_kernel,
        grid=(12,),
        out_shape=(
            jax.ShapeDtypeStruct((1536, 768), F32),
            jax.ShapeDtypeStruct((384, 3072), F32),
            jax.ShapeDtypeStruct((384, 768), F32),
            jax.ShapeDtypeStruct((384, 2304), F32),
        ),
        in_specs=[
            pl.BlockSpec((2, 384, COLS), lambda i: (jnp.minimum(i, 8), 0, 0)),
            pl.BlockSpec((6, 384, 128), lambda i: (3, 0, jnp.maximum(i - 9, 0))),
        ],
        out_specs=(
            pl.BlockSpec((384, 768), lambda i: (jnp.minimum(i, 3), 0)),
            pl.BlockSpec((384, 768), lambda i: (0, jnp.clip(i - 4, 0, 3))),
            pl.BlockSpec((384, 768), lambda i: (0, 0)),
            pl.BlockSpec((384, 768), lambda i: (0, jnp.maximum(i - 9, 0))),
        ),
    )(parts, parts)


def block_shards(
    patches,
    segment_ids,
    mask_positions,
    mask_embed,
    norm1_gain,
    norm1_bias,
    w_qkv,
    query_bias,
    value_bias,
    w_out,
    out_bias,
    norm2_gain,
    norm2_bias,
    w_up,
    up_bias,
    w_down,
    down_bias,
    cotangent,
):
    swap = [(0, 1), (1, 0)]
    width = 768
    patch = patches[0]
    cot = cotangent[0]
    patch_x = lax.ppermute(patch, "tm", swap)
    ids = segment_ids[0]
    ids_x = lax.ppermute(ids, "tm", swap)
    table = jnp.concatenate(
        [
            jnp.stack(
                [
                    mask_embed,
                    norm1_gain,
                    norm1_bias,
                    query_bias,
                    value_bias,
                    out_bias,
                    norm2_gain,
                    norm2_bias,
                    down_bias,
                ]
            ),
            up_bias.reshape(4, 768),
            jnp.zeros((3, 768), BF16),
        ]
    ).astype(F32)
    lane = jnp.arange(128)[None, :]
    qa = jnp.where(ids[:, None] == lane, 1.0, 0.0).astype(BF16)
    ka = jnp.where((lane >= 6) | (ids[:, None] == lane), 0.0, neg_large).astype(BF16)
    qxa = jnp.where(ids_x[:, None] == lane, 1.0, 0.0).astype(BF16)
    kxa = jnp.where((lane >= 6) | (ids_x[:, None] == lane), 0.0, neg_large).astype(BF16)
    hidden1, qkv = front(False, patch, mask_positions, table, w_qkv)
    unused, qkv_x = front(True, patch_x, mask_positions, table, w_qkv)
    attended, lse = attend(qkv, qkv_x, qa, ka, kxa)
    lse_rows = lse[:, :16].T
    lse_rows_x = lax.ppermute(lse_rows, "tm", swap)
    middle, hidden2, activated, grad_upper, up_sums = middle_part(
        patch, mask_positions, table, attended, w_out, cot, w_up, w_down, up_bias.astype(F32)[None]
    )
    parts, output, grad_patches, v = backward(
        (activated, cot, grad_upper, middle, hidden2, w_out, qkv, qkv_x, attended, hidden1, patch, w_qkv),
        (w_up, w_down),
        (qa, ka, qxa, kxa, lse_rows, lse_rows_x, table, mask_positions, up_sums),
    )
    grad_down, grad_up, grad_out, grad_qkv = widen(parts)
    return (
        output[None],
        grad_patches[None],
        v[0],
        v[1],
        v[2],
        grad_qkv,
        v[3],
        v[4],
        grad_out,
        v[5],
        v[6],
        v[7],
        grad_up,
        v[9:13].reshape(-1),
        grad_down,
        v[8],
    )


def shards(
    patches,
    segment_ids,
    mask_positions,
    mask_embed,
    norm1_gain,
    norm1_bias,
    w_qkv,
    query_bias,
    value_bias,
    w_out,
    out_bias,
    norm2_gain,
    norm2_bias,
    w_up,
    up_bias,
    w_down,
    down_bias,
    cotangent,
):
    rows_n, time_n, width = patches.shape
    query_scale = 1.0 / math.sqrt(HEAD)
    gain_one = norm1_gain.astype(jnp.float32)
    gain_two = norm2_gain.astype(jnp.float32)
    offset = lax.axis_index("tm") * time_n
    places = offset + lax.broadcasted_iota(jnp.int32, (rows_n, time_n, 1), 1)
    masked = jnp.any(places == mask_positions[:, None, :], axis=-1)[..., None]
    inputs = jnp.where(
        masked, mask_embed.astype(jnp.float32)[None, None, :], patches.astype(jnp.float32)
    )
    normed1, inverse1 = normalize(inputs)
    hidden1 = (normed1 * gain_one + norm1_bias.astype(jnp.float32)).astype(jnp.bfloat16)
    project = jnp.einsum("rtd,de->rte", hidden1, w_qkv, preferred_element_type=jnp.float32)
    queries = ((project[..., :width] + query_bias.astype(jnp.float32)) * query_scale).astype(
        jnp.bfloat16
    )
    keys_own = project[..., width : 2 * width].astype(jnp.bfloat16)
    values_own = (project[..., 2 * width :] + value_bias.astype(jnp.float32)).astype(jnp.bfloat16)
    keys_all, values_all, segments_all = (
        lax.all_gather(keys_own, "tm", axis=1, tiled=True),
        lax.all_gather(values_own, "tm", axis=1, tiled=True),
        lax.all_gather(segment_ids, "tm", axis=1, tiled=True),
    )
    same = segment_ids[:, :, None] == segments_all[:, None, :]
    query_heads = split_heads(queries)
    head_outputs, log_totals = attend_forward(
        query_heads, split_heads(keys_all), split_heads(values_all), same
    )
    attended = join_heads(head_outputs).astype(jnp.bfloat16)
    middle = (
        inputs
        + jnp.einsum("rtd,de->rte", attended, w_out, preferred_element_type=jnp.float32)
        + out_bias.astype(jnp.float32)
    )
    normed2, inverse2 = normalize(middle)
    hidden2 = (normed2 * gain_two + norm2_bias.astype(jnp.float32)).astype(jnp.bfloat16)
    upper = jnp.einsum(
        "rtd,df->rtf", hidden2, w_up, preferred_element_type=jnp.float32
    ) + up_bias.astype(jnp.float32)
    activated = jax.nn.gelu(upper, approximate=False).astype(jnp.bfloat16)
    result = (
        middle
        + jnp.einsum("rtf,fd->rtd", activated, w_down, preferred_element_type=jnp.float32)
        + down_bias.astype(jnp.float32)
    )
    output = result.astype(jnp.bfloat16)
    grad_result = cotangent.astype(jnp.float32)
    grad_w_down = jnp.einsum(
        "rtf,rtd->fd", activated, cotangent, preferred_element_type=jnp.float32
    )
    grad_down_bias = total_rows(grad_result)
    grad_activated = jnp.einsum(
        "rtd,fd->rtf", cotangent, w_down, preferred_element_type=jnp.float32
    )
    unused, gelu_pull = jax.vjp(partial(jax.nn.gelu, approximate=False), upper)
    grad_upper = gelu_pull(grad_activated)[0].astype(jnp.bfloat16)
    grad_w_up = jnp.einsum("rtd,rtf->df", hidden2, grad_upper, preferred_element_type=jnp.float32)
    grad_up_bias = total_rows(grad_upper)
    grad_hidden2 = jnp.einsum("rtf,df->rtd", grad_upper, w_up, preferred_element_type=jnp.float32)
    grad_gain_two = total_rows(grad_hidden2 * normed2)
    grad_bias_two = total_rows(grad_hidden2)
    grad_middle = grad_result + norm_back(grad_hidden2, normed2, inverse2, gain_two)
    mlp_vectors = jnp.stack([grad_gain_two, grad_bias_two, grad_down_bias], axis=1)
    grad_branch = grad_middle.astype(jnp.bfloat16)
    grad_w_out = jnp.einsum(
        "rtd,rte->de", attended, grad_branch, preferred_element_type=jnp.float32
    )
    grad_out_bias = total_rows(grad_branch)
    grad_attended = jnp.einsum(
        "rte,de->rtd", grad_branch, w_out, preferred_element_type=jnp.float32
    ).astype(jnp.bfloat16)
    keys_back, values_back, segments_back = (
        lax.all_gather(keys_own, "tm", axis=1, tiled=True),
        lax.all_gather(values_own, "tm", axis=1, tiled=True),
        lax.all_gather(segment_ids, "tm", axis=1, tiled=True),
    )
    same_back = segment_ids[:, :, None] == segments_back[:, None, :]
    grad_query_h, grad_keys_h, grad_values_h = attend_backward(
        query_heads,
        split_heads(keys_back),
        split_heads(values_back),
        split_heads(grad_attended),
        log_totals,
        same_back,
    )
    grad_keys, grad_values = (
        lax.psum_scatter(
            join_heads(grad_keys_h).astype(jnp.bfloat16), "tm", scatter_dimension=1, tiled=True
        ).astype(jnp.float32),
        lax.psum_scatter(
            join_heads(grad_values_h).astype(jnp.bfloat16), "tm", scatter_dimension=1, tiled=True
        ).astype(jnp.float32),
    )
    grad_queries = join_heads(grad_query_h).astype(jnp.bfloat16)
    grad_project = jnp.concatenate(
        [
            (grad_queries.astype(jnp.float32) * query_scale).astype(jnp.bfloat16),
            grad_keys.astype(jnp.bfloat16),
            grad_values.astype(jnp.bfloat16),
        ],
        axis=-1,
    )
    grad_w_qkv = jnp.einsum(
        "rtd,rte->de", hidden1, grad_project, preferred_element_type=jnp.float32
    )
    grad_query_bias = total_rows(grad_project[..., :width])
    grad_value_bias = total_rows(grad_project[..., 2 * width :])
    grad_hidden1 = jnp.einsum(
        "rte,de->rtd", grad_project, w_qkv, preferred_element_type=jnp.float32
    )
    grad_gain_one = total_rows(grad_hidden1 * normed1)
    grad_bias_one = total_rows(grad_hidden1)
    grad_inputs = grad_middle + norm_back(grad_hidden1, normed1, inverse1, gain_one)
    grad_mask = total_rows(jnp.where(masked, grad_inputs, 0.0))
    grad_patches = jnp.where(masked, 0.0, grad_inputs).astype(jnp.bfloat16)
    attn_vectors = jnp.stack(
        [grad_mask, grad_gain_one, grad_bias_one, grad_query_bias, grad_value_bias, grad_out_bias],
        axis=1,
    )
    every_part = (
        lax.psum_scatter(
            grad_w_qkv.astype(jnp.bfloat16), "tm", scatter_dimension=0, tiled=True
        ).astype(jnp.float32),
        lax.psum_scatter(
            grad_w_out.astype(jnp.bfloat16), "tm", scatter_dimension=0, tiled=True
        ).astype(jnp.float32),
        lax.psum_scatter(
            attn_vectors.astype(jnp.bfloat16), "tm", scatter_dimension=0, tiled=True
        ).astype(jnp.float32),
        lax.psum_scatter(
            grad_w_up.astype(jnp.bfloat16), "tm", scatter_dimension=0, tiled=True
        ).astype(jnp.float32),
        lax.psum_scatter(
            grad_w_down.astype(jnp.bfloat16), "tm", scatter_dimension=0, tiled=True
        ).astype(jnp.float32),
        lax.psum_scatter(
            mlp_vectors.astype(jnp.bfloat16), "tm", scatter_dimension=0, tiled=True
        ).astype(jnp.float32),
        lax.psum_scatter(
            grad_up_bias.astype(jnp.bfloat16), "tm", scatter_dimension=0, tiled=True
        ).astype(jnp.float32),
    )
    every_part = (
        lax.psum(every_part[0].astype(jnp.bfloat16), "rows").astype(jnp.float32),
        lax.psum(every_part[1].astype(jnp.bfloat16), "rows").astype(jnp.float32),
        lax.psum(every_part[2].astype(jnp.bfloat16), "rows").astype(jnp.float32),
        lax.psum(every_part[3].astype(jnp.bfloat16), "rows").astype(jnp.float32),
        lax.psum(every_part[4].astype(jnp.bfloat16), "rows").astype(jnp.float32),
        lax.psum(every_part[5].astype(jnp.bfloat16), "rows").astype(jnp.float32),
        lax.psum(every_part[6].astype(jnp.bfloat16), "rows").astype(jnp.float32),
    )
    summed_qkv, summed_out, summed_attn, summed_up, summed_down, summed_mlp, summed_up_bias = (
        every_part
    )
    return (
        output,
        grad_patches,
        summed_attn[:, 0],
        summed_attn[:, 1],
        summed_attn[:, 2],
        summed_qkv,
        summed_attn[:, 3],
        summed_attn[:, 4],
        summed_out,
        summed_attn[:, 5],
        summed_mlp[:, 0],
        summed_mlp[:, 1],
        summed_up,
        summed_up_bias,
        summed_down,
        summed_mlp[:, 2],
    )


def solution(mesh):
    placed = (
        P("rows", "tm", None),
        P("rows", "tm"),
        P("rows", None),
        P(),
        P(),
        P(),
        P(),
        P(),
        P(),
        P(),
        P(),
        P(),
        P(),
        P(),
        P(),
        P(),
        P(),
        P("rows", "tm", None),
    )
    return jax.shard_map(
        block_shards if dict(mesh.shape) == {"rows": 16, "tm": 2} else shards,
        mesh=mesh,
        in_specs=placed,
        out_specs=(
            P("rows", "tm", None),
            P("rows", "tm", None),
            P("tm"),
            P("tm"),
            P("tm"),
            P("tm", None),
            P("tm"),
            P("tm"),
            P("tm", None),
            P("tm"),
            P("tm"),
            P("tm"),
            P("tm", None),
            P("tm"),
            P("tm", None),
            P("tm"),
        ),
        check_vma=False,
    )
```

```python
from functools import partial
import math

import jax
import jax.numpy as jnp
from jax import lax
from jax.experimental import pallas as pl
from jax.experimental.pallas import tpu as pltpu
from jax.sharding import PartitionSpec as P

HEADS = 12
HEAD = 64


norm_eps = 1e-06
neg_large = -1e30


def normalize(values):
    center = values - jnp.mean(values, axis=-1, keepdims=True)
    scale_inv = lax.rsqrt(jnp.mean(center * center, axis=-1, keepdims=True) + norm_eps)
    return (center * scale_inv, scale_inv)


def norm_back(grad_out, normed, scale_inv, norm_gain):
    grad_normed = grad_out * norm_gain
    mean_one = jnp.mean(grad_normed, axis=-1, keepdims=True)
    mean_two = jnp.mean(grad_normed * normed, axis=-1, keepdims=True)
    return scale_inv * (grad_normed - mean_one - normed * mean_two)


def split_heads(tensor):
    rows_n, length, width = tensor.shape
    return tensor.reshape(rows_n, length, HEADS, width // HEADS).transpose(2, 0, 1, 3)


def join_heads(tensor):
    heads_n, rows_n, length, size = tensor.shape
    return tensor.transpose(1, 2, 0, 3).reshape(rows_n, length, heads_n * size)


def head_scores(query, keys_h, same):
    scores = jnp.einsum("rqd,rkd->rqk", query, keys_h, preferred_element_type=jnp.float32)
    return jnp.where(same, scores, neg_large)


def attend_forward(query_heads, key_heads, value_heads, same):

    def one_head(operands):
        query, keys_h, values_h = operands
        scores = head_scores(query, keys_h, same)
        peak = jnp.max(scores, axis=-1, keepdims=True)
        total = jnp.sum(jnp.exp(scores - peak), axis=-1, keepdims=True)
        log_total = peak + jnp.log(total)
        weights = jnp.exp(scores - log_total).astype(jnp.bfloat16)
        result = jnp.einsum("rqk,rkd->rqd", weights, values_h, preferred_element_type=jnp.float32)
        return (result, log_total[..., 0])

    return lax.map(one_head, (query_heads, key_heads, value_heads))


def attend_backward(query_heads, key_heads, value_heads, grad_heads, log_totals, same):

    def one_head(operands):
        query, keys_h, values_h, grad_out, log_total = operands
        scores = head_scores(query, keys_h, same)
        probs_full = jnp.exp(scores - log_total[..., None])
        probs_low = probs_full.astype(jnp.bfloat16)
        grad_values = jnp.einsum(
            "rqk,rqd->rkd", probs_low, grad_out, preferred_element_type=jnp.float32
        )
        grad_probs = jnp.einsum(
            "rqd,rkd->rqk", grad_out, values_h, preferred_element_type=jnp.float32
        )
        delta = jnp.sum(grad_probs * probs_full, axis=-1, keepdims=True)
        grad_scores = (probs_full * (grad_probs - delta)).astype(jnp.bfloat16)
        grad_query = jnp.einsum(
            "rqk,rkd->rqd", grad_scores, keys_h, preferred_element_type=jnp.float32
        )
        grad_keys = jnp.einsum(
            "rqk,rqd->rkd", grad_scores, query, preferred_element_type=jnp.float32
        )
        return (grad_query, grad_keys, grad_values)

    return lax.map(one_head, (query_heads, key_heads, value_heads, grad_heads, log_totals))


MESH = pl.DeviceIdType.MESH
SUB = 96
COLS = 384
LAGS = (0, 1, 5, 6, 7, 9, 11, 12)


def places():
    row = lax.axis_index("rows")
    y = lax.axis_index("tm")
    core = row % 2
    x = (row // 2) % 2
    z_low = (row // 4) % 2
    z_high = row // 8
    peers = (
        (row + 1 - 2 * core, y),
        (row, 1 - y),
        (row + 2 - 4 * x, y),
        (row + 4 - 8 * z_low, y),
        (row + 8 - 16 * z_high, y),
    )
    return core, x, y, peers


def greet(peers):
    barrier = pltpu.get_barrier_semaphore()
    for peer in peers:
        pl.semaphore_signal(barrier, inc=1, device_id=peer, device_id_type=MESH)
    pl.semaphore_wait(barrier, len(peers))


def total_rows(tensor):
    return jnp.sum(tensor.astype(jnp.float32), axis=(0, 1))


VMEM = pltpu.VMEM
F32 = jnp.float32
BF16 = jnp.bfloat16
HALF = 512
TILE = 256
R_EMBED, R_G1, R_B1, R_QB, R_VB, R_OB, R_G2, R_B2, R_DB, R_UB = 0, 1, 2, 3, 4, 5, 6, 7, 8, 9
QUERY_SCALE = 1.0 / math.sqrt(HEAD)


def dot(a, b):
    return lax.dot_general(a, b, (((1,), (0,)), ((), ())), preferred_element_type=F32)


def dot_t(a, b):
    return lax.dot_general(a, b, (((1,), (1,)), ((), ())), preferred_element_type=F32)


def t_dot(a, b):
    return lax.dot_general(a, b, (((0,), (0,)), ((), ())), preferred_element_type=F32)


def table_kernel(*refs):
    table_ref = refs[-1]
    table_ref[...] = jnp.zeros_like(table_ref)
    for i, ref in enumerate(refs[:-1]):
        table_ref[i : i + 1, :] = ref[...].astype(F32).reshape(1, 768)


def tabulate(smalls):
    near = pl.BlockSpec(memory_space=pltpu.VMEM)
    return pl.pallas_call(
        table_kernel,
        out_shape=jax.ShapeDtypeStruct((16, 768), F32),
        in_specs=[near] * len(smalls),
        out_specs=near,
    )(*smalls)


def standard(values):
    center = values - jnp.mean(values, axis=-1, keepdims=True)
    scale_inv = lax.rsqrt(jnp.mean(center * center, axis=-1, keepdims=True) + norm_eps)
    return center * scale_inv, scale_inv


def masked_inputs(patch, first, marks, embed):
    at = first + lax.broadcasted_iota(jnp.int32, (patch.shape[0], 1), 0)
    flagged = jnp.max(jnp.where(at == marks, 1.0, 0.0), axis=-1, keepdims=True) > 0.5
    return flagged, jnp.where(flagged, embed, patch.astype(F32))


def project_tile(patch, first, marks_ref, table_ref, w_ref, qkv_ref):
    unused, inputs = masked_inputs(patch, first, marks_ref[...], table_ref[R_EMBED : R_EMBED + 1, :])
    normed, unused = standard(inputs)
    hidden = (normed * table_ref[R_G1 : R_G1 + 1, :] + table_ref[R_B1 : R_B1 + 1, :]).astype(BF16)
    for part in range(6):
        cols = slice(part * 384, part * 384 + 384)
        project = dot(hidden, w_ref[:, cols])
        bias = slice((part % 2) * 384, (part % 2) * 384 + 384)
        if part < 2:
            project = (project + table_ref[R_QB : R_QB + 1, bias]) * QUERY_SCALE
        elif part >= 4:
            project = project + table_ref[R_VB : R_VB + 1, bias]
        qkv_ref[:, cols] = project.astype(BF16)
    return hidden


def own_kernel(p_ref, marks_ref, table_ref, w_ref, qkv_ref, h1_ref):
    first = lax.axis_index("tm") * HALF + pl.program_id(0) * TILE
    h1_ref[...] = project_tile(p_ref[...], first, marks_ref, table_ref, w_ref, qkv_ref)


def other_kernel(near, p_ref, marks_ref, table_ref, w_ref, qkv_ref):
    y = lax.axis_index("tm")
    first = (1 - y) * HALF + (y if near else 1 - y) * TILE
    project_tile(p_ref[...], first, marks_ref, table_ref, w_ref, qkv_ref)


def front(kernel, patch, marks, table, w_qkv):
    own = patch.shape[0] == HALF
    length = HALF if own else TILE
    widths = (2304, 768) if own else (2304,)
    return pl.pallas_call(
        kernel,
        grid=(length // TILE,),
        out_shape=tuple(jax.ShapeDtypeStruct((length, n), BF16) for n in widths),
        in_specs=[
            pl.BlockSpec((TILE, 768), lambda i: (i, 0)),
            pl.BlockSpec(marks.shape, lambda i: (0, 0)),
            pl.BlockSpec(table.shape, lambda i: (0, 0)),
            pl.BlockSpec((768, 2304), lambda i: (0, 0), pipeline_mode=pl.Buffered(1)),
        ],
        out_specs=tuple(pl.BlockSpec((TILE, n), lambda i: (i, 0)) for n in widths),
        cost_estimate=pl.CostEstimate(flops=2 * length * 768 * 2304, bytes_accessed=8 << 20, transcendentals=0),
    )(patch, marks, table, w_qkv)


def attend_kernel(
    q_ref, k_ref, v_ref, kn_ref, vn_ref, kf_ref, vf_ref, qa_ref, ka_ref, kxa_ref, on_ref, of_ref, ln_ref, lf_ref, marks_ref
):
    y = lax.axis_index("tm")
    pair = pl.program_id(0)
    lane = lax.broadcasted_iota(jnp.int32, (1, 128), 1)

    def rows_of(index):
        return pl.ds(pl.multiple_of(index * TILE, TILE), TILE)

    blocks = [
        (k_ref, ka_ref[...], v_ref),
        (kn_ref, kxa_ref[rows_of(y), :], vn_ref),
        (kf_ref, kxa_ref[rows_of(1 - y), :], vf_ref),
    ]
    all_keys = [jnp.concatenate([k[...], a], axis=1) for k, a, unused in blocks]
    for far, number, o_ref, lse_ref in ((0, 3, on_ref, ln_ref), (1, 2, of_ref, lf_ref)):
        rows = rows_of(y if far else 1 - y)
        q = q_ref[rows, :]
        qa = qa_ref[rows, :]
        kept = None
        marks = jnp.where(pair == 0, 0.0, marks_ref[far])
        for h in range(2):
            mine = (lane // 64) == h
            query = jnp.concatenate([jnp.where(mine, q, 0), qa], axis=1)
            scores = [dot_t(query, key) for key in all_keys[:number]]
            peak = jnp.max(scores[0], axis=-1, keepdims=True)
            for more in scores[1:]:
                peak = jnp.maximum(peak, jnp.max(more, axis=-1, keepdims=True))
            total = 0.0
            out = 0.0
            for score, block in zip(scores, blocks):
                weights = jnp.exp(score - peak)
                total = total + jnp.sum(weights, axis=-1, keepdims=True)
                out = out + dot(weights.astype(BF16), block[2][...])
            out = out / total
            kept = out if h == 0 else jnp.where(mine, out, kept)
            marks = jnp.where(lane == 2 * pair + h, peak + jnp.log(total), marks)
        o_ref[...] = kept.astype(BF16)
        marks_ref[far] = marks

    @pl.when(pair == 5)
    def _():
        ln_ref[...] = marks_ref[0].T[:16, :]
        lf_ref[...] = marks_ref[1].T[:16, :]


def attend(qkv, near, far, qa, ka, kxa):
    def block(first, length):
        return pl.BlockSpec((length, 128), lambda i: (0, first + i))

    whole = pl.BlockSpec((HALF, 128), lambda i: (0, 0))
    stat = pl.BlockSpec((16, TILE), lambda i: (0, 0))
    return pl.pallas_call(
        attend_kernel,
        grid=(6,),
        out_shape=(jax.ShapeDtypeStruct((TILE, 768), BF16),) * 2 + (jax.ShapeDtypeStruct((16, TILE), F32),) * 2,
        in_specs=[block(0, HALF), block(6, HALF), block(12, HALF)]
        + [block(6, TILE), block(12, TILE)] * 2
        + [whole] * 3,
        out_specs=(block(0, TILE), block(0, TILE), stat, stat),
        scratch_shapes=[pltpu.VMEM((2, TILE, 128), F32)],
        cost_estimate=pl.CostEstimate(
            flops=4 * 12 * HALF * 1024 * 64, bytes_accessed=8 << 20, transcendentals=12 * HALF * 1024
        ),
    )(qkv, qkv, qkv, near, near, far, far, qa, ka, kxa)


ERFC_P = 0.3275911
ERFC_C = (
    0.1851102167482524,
    0.17993860771517878,
    0.21041948320823337,
    0.011498087426314028,
    0.47813345988158296,
    -0.4317659362057169,
    0.5111742647535956,
    -0.14450823957827402,
)


def gelu_and_slope(u):
    t = 1.0 / (1.0 + (ERFC_P * math.sqrt(0.5)) * jnp.abs(u))
    bell = jnp.exp(-0.5 * (u * u))
    series = ERFC_C[7]
    for c in ERFC_C[6::-1]:
        series = series * t + c
    tail = (0.5 * t) * series * bell
    phi = jnp.where(u < 0, tail, 1.0 - tail)
    return u * phi, phi + u * (bell * (1.0 / math.sqrt(2.0 * math.pi)))


CHUNKS = 24
SLOTS = 5
FF_TILE = 384
T_FORWARD = (0, 0, 1, 2, 3, 4, 5, 6)
EMIT_DOWN, EMIT_UP, EMIT_OUT, EMIT_QKV = (0, 2, 4, 6), (8, 10, 12, 14), (16,), (18, 19, 20, 21, 22, 23)
T_SECOND, T_ATTENDED = (7,), (8,)
T_SEND = (8, 9, 9, 10, 11, 11, 12, 13, 13, 14, 15, 15)
T_OWN = (8, 9, 10, 13, 14, 15)
T_FAR = (12, 13, 14, 16, 17, 18)
T_OUTPUT = (19, 19, 20, 20, 21, 21, 22, 22)
T_GRAD = (24, 24, 25)
T_FIRST = (26,)
T_VEC = 27


def halves_kernel(
    cot_h, wo_h, qkv_h, h1_h, patch_h, wq_h, otn_h, otf_h, atn_h, atf_h, wu_h, wd_h,
    qa_ref, ka_ref, qxa_ref, kxa_ref, lsen_ref, lsef_ref, table_ref, marks_ref, ub_ref,
    parts_h, out_h, gp_h, vec_out,
    cot, wo, qkv, h1, patch, wq, qkvx, att, wu, wd,
    act, gu, mid, h2, acc, gb, do, dox, dqkv, dq, dk, dv, drow, dxrow, lse_ref, lsex_ref,
    g, r1, r2, r3, r4, r5, done, v0, v1, v2,
    insem, wusem, wdsem, ssem, rsem, vs, vr, xs, xr, outsem, lastsem,
):
    core, x, y, peers = places()
    pair, yp, xp, zp1, zp2 = peers
    lane = lax.broadcasted_iota(jnp.int32, (1, 128), 1)
    near_rows = pl.ds(pl.multiple_of((1 - y) * TILE, TILE), TILE)
    far_rows = pl.ds(pl.multiple_of(y * TILE, TILE), TILE)
    inputs = (
        (cot_h, cot), (wo_h, wo), (qkv_h, qkv), (h1_h, h1), (patch_h, patch), (wq_h, wq),
        (otn_h, qkvx.at[far_rows, :]), (otf_h, qkvx.at[near_rows, :]),
        (atn_h, att.at[near_rows, :]), (atf_h, att.at[far_rows, :]),
    )
    COT, WO, QKV, H1, PATCH, WQ, OTN, OTF, ATN, ATF = range(10)

    def lanes(start, size=128):
        return pl.ds(pl.multiple_of(start, 128), size)

    def part_of(n):
        return (n // 2 + 4 * (n % 2)) * (1 - n // 8) + (n - 8) * (n // 8)

    def load(i):
        return pltpu.make_async_copy(inputs[i][0], inputs[i][1], insem.at[i])

    def up_tile(n):
        return pltpu.make_async_copy(wu_h.at[:, lanes(part_of(n) * FF_TILE, FF_TILE)], wu.at[n % 2], wusem.at[n % 2])

    def down_tile(n):
        rows = pl.ds(pl.multiple_of(part_of(n) * FF_TILE, FF_TILE), FF_TILE)
        return pltpu.make_async_copy(wd_h.at[rows, :], wd.at[n % 2], wdsem.at[n % 2])

    for i in (PATCH, WO, ATN, ATF):
        load(i).start()
    for n in range(2):
        up_tile(n).start()
        down_tile(n).start()
    for i in (COT, QKV, OTN, OTF, H1, WQ):
        load(i).start()
    greet(peers)

    def remote(src, dst, send, recv, dev):
        return pltpu.make_async_remote_copy(
            src_ref=src, dst_ref=dst, send_sem=send, recv_sem=recv, device_id=dev, device_id_type=MESH
        )

    def copy(s, c):
        src, dst, dev = (
            lambda: (g.at[c % SLOTS, 1 - core], r1.at[c], pair),
            lambda: (r1.at[c, 1 - y], r2.at[c], yp),
            lambda: (r2.at[c, 1 - x], r3.at[c], xp),
            lambda: (r3.at[c], r4.at[c], zp1),
            lambda: (r4.at[c], r5.at[c], zp2),
            lambda: (done.at[c, core, x], done.at[c, core, x], xp),
            lambda: (done.at[c, core], done.at[c, core], pair),
        )[s]()
        return remote(src, dst, ssem.at[s, c], rsem.at[s, c], dev)

    def part_out(c):
        return pltpu.make_async_copy(done.at[c], parts_h.at[c], outsem.at[c])

    def stage(s, c):
        if s > 0:
            copy(s - 1, c).wait_recv()
        if s == 1:
            r1[c] = r1[c] + g[c % SLOTS, core]
        elif s == 2:
            r2[c] = r2[c] + r1[c, y]
        elif s == 3:
            r3[c] = r3[c] + r2[c, x]
        elif s == 4:
            r4[c] = r4[c] + r3[c]
        elif s == 5:
            done[c, core, x] = r5[c] + r4[c]
        elif s == 7:
            copy(5, c).wait_send()
            copy(6, c).wait_send()
            part_out(c).start()
        if s < 7:
            copy(s, c).start()

    def vec_copy(s):
        src, dst, dev = (
            lambda: (v0, v1, pair),
            lambda: (v1.at[1 - y], v2.at[0], yp),
            lambda: (v2.at[0], v2.at[1], xp),
            lambda: (v2.at[1], v2.at[2], zp1),
            lambda: (v2.at[2], v2.at[3], zp2),
        )[s]()
        return remote(src, dst, vs.at[s], vr.at[s], dev)

    def vec_stage(s):
        if s > 0:
            vec_copy(s - 1).wait_recv()
        if s == 1:
            v1[...] = v1[...] + v0[...]
        elif s == 2:
            v2[0] = v2[0] + v1[y]
        elif s == 5:
            vec_out[...] = v2[3] + v2[2]
        elif s > 2:
            v2[s - 2] = v2[s - 2] + v2[s - 3]
        if s < 5:
            vec_copy(s).start()

    def far_copy(i):
        src, dst = ((lse_ref, lsex_ref), (drow, dxrow))[i]
        return remote(src, dst, xs.at[i], xr.at[i], yp)

    def grad_copy(n):
        rows, cols = pl.ds(pl.multiple_of((n % 2) * TILE, TILE), TILE), lanes((n // 2) * 128)
        return remote(do.at[rows, cols], dox.at[rows, cols], xs.at[2 + n], xr.at[2 + n], yp)

    def row(r):
        return table_ref[r : r + 1, :]

    def add_vec(r, value):
        for half in range(2):
            v0[half, r : r + 1, :] = v0[half, r : r + 1, :] + value[:, half * 384 : half * 384 + 384]

    def emit(left, right, c):
        number = right.shape[1] // 384
        for i in range(number):

            @pl.when(c + i >= SLOTS)
            def _():
                copy(0, c + i - SLOTS).wait_send()

        for half in range(2):
            block = t_dot(left(half), right).astype(BF16)
            for i in range(number):
                for other in range(4):
                    rows = slice(other * SUB, other * SUB + SUB)
                    g[(c + i) % SLOTS, other // 2, half, other % 2] = block[rows, i * 384 : i * 384 + 384]

    def enter():
        for tile in range(HALF // TILE):
            rows = slice(tile * TILE, tile * TILE + TILE)
            unused, values = masked_inputs(patch[rows, :], y * HALF + tile * TILE, marks_ref[...], row(R_EMBED))
            total = values + dot(att[rows, :], wo[...]) + row(R_OB)
            normed, unused = standard(total)
            mid[rows, :] = total
            h2[rows, :] = (normed * row(R_G2) + row(R_B2)).astype(BF16)

    def forward(n):
        k = part_of(n)
        cols = lanes(k * FF_TILE, FF_TILE)
        up_tile(n).wait()
        down_tile(n).wait()
        sums = jnp.zeros((1, FF_TILE), F32)
        for tile in range(HALF // TILE):
            rows = slice(tile * TILE, tile * TILE + TILE)
            value, slope = gelu_and_slope(dot(h2[rows, :], wu[n % 2]) + ub_ref[:, cols])
            act[rows, cols] = value.astype(BF16)
            low = (dot_t(cot[rows, :], wd[n % 2]) * slope).astype(BF16)
            gu[rows, cols] = low
            sums = sums + jnp.sum(low.astype(F32), axis=0, keepdims=True)
            acc[rows, :] = acc[rows, :] + dot_t(low, wu[n % 2])
        v0[k // 4, pl.ds(9 + k % 4, 1), :] = sums
        down_tile(n + 2).start()

        @pl.when(n + 2 < 8)
        def _():
            up_tile(n + 2).start()

    def second_norm():
        def tile(i, carry):
            rows = pl.ds(pl.multiple_of(i * 128, 128), 128)
            normed, inverse = standard(mid[rows, :])
            grad = acc[rows, :]
            cotangent = cot[rows, :].astype(F32)
            add_vec(6, jnp.sum(grad * normed, axis=0, keepdims=True))
            add_vec(7, jnp.sum(grad, axis=0, keepdims=True))
            add_vec(8, jnp.sum(cotangent, axis=0, keepdims=True))
            total = cotangent + norm_back(grad, normed, inverse, row(R_G2))
            acc[rows, :] = total
            low = total.astype(BF16)
            gb[rows, :] = low
            add_vec(5, jnp.sum(low.astype(F32), axis=0, keepdims=True))
            return carry

        lax.fori_loop(0, 4, tile, 0)

    def grad_attended():
        for tile in range(2):
            rows = slice(tile * 256, tile * 256 + 256)
            do[rows, :] = dot_t(gb[rows, :], wo[...]).astype(BF16)
        for tile in range(4):
            rows = slice(tile * 128, tile * 128 + 128)
            columns = jnp.zeros((128, 128), F32)
            for p in range(6):
                cols = slice(p * 128, p * 128 + 128)
                product = do[rows, cols].astype(F32) * att[rows, cols].astype(F32)
                for h in range(2):
                    total = jnp.sum(jnp.where((lane // 64) == h, product, 0.0), axis=1, keepdims=True)
                    columns = jnp.where(lane == 2 * p + h, total, columns)
            drow[:, rows] = columns.T[:16, :]
        far_copy(1).start()

    def piece(keys, key_mask, values, query, query_mask, grad, lse, delta):
        scores = dot_t(jnp.concatenate([keys, key_mask], axis=1), jnp.concatenate([query, query_mask], axis=1))
        probs = jnp.exp(scores - lse)
        grad_scores = probs * (dot_t(values, grad) - delta)
        return probs.astype(BF16), grad_scores.astype(BF16)

    def own_pair(p):
        slot = p % 3

        def head(h, carry):
            mine = (lane // 64) == h
            stat = pl.ds(2 * p + h, 1)
            query = jnp.where(mine, qkv[:, lanes(p * 128)], 0)
            grad = jnp.where(mine, do[:, lanes(p * 128)], 0)
            for tile in range(2):
                rows = slice(tile * 256, tile * 256 + 256)
                keys = qkv[rows, lanes(768 + p * 128)]
                probs, scores = piece(
                    keys, ka_ref[rows, :], qkv[rows, lanes(1536 + p * 128)], query, qa_ref[...], grad,
                    lse_ref[stat, :], drow[stat, :],
                )
                new = dot(scores, query)
                dk[slot, rows, :] = jnp.where(h == 0, new, dk[slot, rows, :] + new)
                new = dot(probs, grad)
                dv[slot, rows, :] = jnp.where(h == 0, new, dv[slot, rows, :] + new)
                new = t_dot(scores, jnp.where(mine, keys, 0))
                dq[slot] = jnp.where((h == 0) & (tile == 0), new, dq[slot] + new)
            return carry

        lax.fori_loop(0, 2, head, 0)

    def far_pair(p):
        slot = p % 3
        grad_copy(2 * p).wait_recv()
        grad_copy(2 * p + 1).wait_recv()
        near, far = pl.multiple_of((1 - y) * 256, 256), pl.multiple_of(y * 256, 256)

        def head(h, carry):
            mine = (lane // 64) == h
            stat = pl.ds(2 * p + h, 1)
            for first, start, size in ((far, 0, 512), (near, near, 256)):
                rows, others = pl.ds(first, 256), pl.ds(start, size)
                query = jnp.where(mine, qkv[others, lanes(p * 128)], 0)
                grad = jnp.where(mine, do[others, lanes(p * 128)], 0)
                keys = qkvx[rows, lanes(768 + p * 128)]
                probs, scores = piece(
                    keys, kxa_ref[rows, :], qkvx[rows, lanes(1536 + p * 128)], query, qa_ref[others, :], grad,
                    lse_ref[stat, others], drow[stat, others],
                )
                dq[slot, others, :] = dq[slot, others, :] + t_dot(scores, jnp.where(mine, keys, 0))
            for first, start, size in ((near, 0, 512), (far, far, 256)):
                rows, others = pl.ds(first, 256), pl.ds(start, size)
                query = jnp.where(mine, qkvx[others, lanes(p * 128)], 0)
                grad = jnp.where(mine, dox[others, lanes(p * 128)], 0)
                probs, scores = piece(
                    qkv[rows, lanes(768 + p * 128)], ka_ref[rows, :], qkv[rows, lanes(1536 + p * 128)],
                    query, qxa_ref[others, :], grad, lsex_ref[stat, others], dxrow[stat, others],
                )
                dk[slot, rows, :] = dk[slot, rows, :] + dot(scores, query)
                dv[slot, rows, :] = dv[slot, rows, :] + dot(probs, grad)
            return carry

        lax.fori_loop(0, 2, head, 0)
        dqkv[:, lanes(p * 128)] = (dq[slot].astype(BF16).astype(F32) * QUERY_SCALE).astype(BF16)
        dqkv[:, lanes(768 + p * 128)] = dk[slot].astype(BF16)
        dqkv[:, lanes(1536 + p * 128)] = dv[slot].astype(BF16)

    def output_tile(i):
        n = i + 8
        down_tile(n).wait()
        for tile in range(2):
            rows = slice(tile * 256, tile * 256 + 256)
            mid[rows, :] = mid[rows, :] + dot(act[rows, lanes(i * FF_TILE, FF_TILE)], wd[n % 2])

        @pl.when(n + 2 < 16)
        def _():
            down_tile(n + 2).start()

    def store_output():
        for tile in range(4):
            rows = slice(tile * 128, tile * 128 + 128)
            gb[rows, :] = (mid[rows, :] + row(R_DB)).astype(BF16)
        pltpu.make_async_copy(gb, out_h, lastsem.at[0]).start()

    def grad_first(part):
        for tile in range(2):
            rows = slice(tile * 256, tile * 256 + 256)
            new = dot_t(dqkv[rows, lanes(part * 768, 768)], wq[:, lanes(part * 768, 768)])
            mid[rows, :] = jnp.where(part == 0, new, mid[rows, :] + new)

    def first_norm():
        def tile(i, carry):
            rows = pl.ds(pl.multiple_of(i * 128, 128), 128)
            flagged, values = masked_inputs(patch[rows, :], y * HALF + i * 128, marks_ref[...], row(R_EMBED))
            normed, inverse = standard(values)
            grad = mid[rows, :]
            add_vec(1, jnp.sum(grad * normed, axis=0, keepdims=True))
            add_vec(2, jnp.sum(grad, axis=0, keepdims=True))
            total = acc[rows, :] + norm_back(grad, normed, inverse, row(R_G1))
            add_vec(0, jnp.sum(jnp.where(flagged, total, 0.0), axis=0, keepdims=True))
            att[rows, :] = jnp.where(flagged, 0.0, total).astype(BF16)
            add_vec(3, jnp.sum(dqkv[rows, :768].astype(F32), axis=0, keepdims=True))
            add_vec(4, jnp.sum(dqkv[rows, 1536:].astype(F32), axis=0, keepdims=True))
            return carry

        lax.fori_loop(0, 4, tile, 0)
        pltpu.make_async_copy(att, gp_h, lastsem.at[1]).start()

    lse_ref[:, near_rows] = lsen_ref[...]
    lse_ref[:, far_rows] = lsef_ref[...]
    far_copy(0).start()
    acc[...] = jnp.zeros_like(acc)
    v0[...] = jnp.zeros_like(v0)
    for i in (PATCH, WO, ATN, ATF):
        load(i).wait()
    enter()
    load(COT).wait()

    def step(t, carry):
        def run(times, body):
            def before(now):
                return sum(jnp.where(now > at, 1, 0) for at in times)

            def one(n, inner):
                body(n)
                return inner

            lax.fori_loop(before(t), before(t + 1), one, 0)

        def need(at, *names):
            @pl.when(t == at)
            def _():
                for i in names:
                    load(i).wait()

        need(2, QKV, OTN, OTF, H1, WQ)
        run(T_FORWARD, forward)
        run(
            EMIT_DOWN,
            lambda n: emit(lambda half: act[:, lanes(half * 1536 + n * 384, 384)], cot[...], 2 * n),
        )
        run(
            EMIT_UP,
            lambda n: emit(lambda half: h2[:, half * 384 : half * 384 + 384], gu[:, lanes(n * 768, 768)], 8 + 2 * n),
        )
        run(EMIT_OUT, lambda n: emit(lambda half: att[:, half * 384 : half * 384 + 384], gb[...], 16))

        def emit_qkv(p):
            right = jnp.concatenate([dqkv[:, lanes(part * 768 + p * 128)] for part in range(3)], axis=1)
            emit(lambda half: h1[:, half * 384 : half * 384 + 384], right, 18 + p)

        run(EMIT_QKV, emit_qkv)
        for s in range(2):
            c = t - LAGS[s]

            @pl.when((c >= 0) & (c < CHUNKS))
            def _():
                stage(s, c)

        run(T_SECOND, lambda n: second_norm())
        run(T_ATTENDED, lambda n: grad_attended())
        run(T_SEND, lambda n: grad_copy(n).start())
        run(T_OWN, own_pair)

        @pl.when(t == T_FAR[0])
        def _():
            far_copy(0).wait_recv()
            far_copy(1).wait_recv()

        run(T_FAR, far_pair)
        run(T_OUTPUT, output_tile)

        @pl.when(t == T_OUTPUT[-1])
        def _():
            store_output()

        run(T_GRAD, grad_first)
        run(T_FIRST, lambda n: first_norm())

        for s in range(2, 8):
            c = t - LAGS[s]

            @pl.when((c >= 0) & (c < CHUNKS))
            def _():
                stage(s, c)

        for s in range(6):

            @pl.when(t == T_VEC + s)
            def _():
                vec_stage(s)

        return carry

    lax.fori_loop(0, max(T_VEC + 6, CHUNKS + LAGS[7]), step, 0)

    def drain(c, carry):
        for s in range(1, 5):
            copy(s, c).wait_send()
        part_out(c).wait()
        return carry

    lax.fori_loop(0, CHUNKS, drain, 0)
    for c in range(CHUNKS - SLOTS, CHUNKS):
        copy(0, c).wait_send()
    for s in range(5):
        vec_copy(s).wait_send()
    for i in range(2):
        far_copy(i).wait_send()

    def drain_grad(n, carry):
        grad_copy(n).wait_send()
        return carry

    lax.fori_loop(0, 12, drain_grad, 0)
    pltpu.make_async_copy(gb, out_h, lastsem.at[0]).wait()
    pltpu.make_async_copy(att, gp_h, lastsem.at[1]).wait()


def backward(big, weights, small):
    hbm = pl.BlockSpec(memory_space=pl.ANY)
    near = pl.BlockSpec(memory_space=pltpu.VMEM)

    def low(*shape):
        return pltpu.VMEM(shape, BF16)

    def full(*shape):
        return pltpu.VMEM(shape, F32)

    dma = pltpu.SemaphoreType.DMA
    held = [pltpu.VMEM(a.shape, a.dtype) for a in big[:6]] + [low(HALF, 2304), low(HALF, 768)]
    return pl.pallas_call(
        halves_kernel,
        out_shape=(
            jax.ShapeDtypeStruct((CHUNKS, 2, 2, SUB, COLS), BF16),
            jax.ShapeDtypeStruct((HALF, 768), BF16),
            jax.ShapeDtypeStruct((HALF, 768), BF16),
            jax.ShapeDtypeStruct((16, COLS), F32),
        ),
        in_specs=[hbm] * (len(big) + 2) + [near] * len(small),
        out_specs=(hbm, hbm, hbm, near),
        scratch_shapes=held
        + [
            low(2, 768, FF_TILE),
            low(2, FF_TILE, 768),
            low(HALF, 3072),
            low(HALF, 3072),
            full(HALF, 768),
            low(HALF, 768),
            full(HALF, 768),
            low(HALF, 768),
            low(HALF, 768),
            low(HALF, 768),
            low(HALF, 2304),
            full(3, HALF, 128),
            full(3, HALF, 128),
            full(3, HALF, 128),
            full(16, HALF),
            full(16, HALF),
            full(16, HALF),
            full(16, HALF),
            low(SLOTS, 2, 2, 2, SUB, COLS),
            low(CHUNKS, 2, 2, SUB, COLS),
            low(CHUNKS, 2, SUB, COLS),
            low(CHUNKS, SUB, COLS),
            low(CHUNKS, SUB, COLS),
            low(CHUNKS, SUB, COLS),
            low(CHUNKS, 2, 2, SUB, COLS),
            full(2, 16, COLS),
            full(2, 16, COLS),
            full(4, 16, COLS),
            dma((10,)),
            dma((2,)),
            dma((2,)),
            dma((7, CHUNKS)),
            dma((7, CHUNKS)),
            dma((5,)),
            dma((5,)),
            dma((14,)),
            dma((14,)),
            dma((CHUNKS,)),
            dma((2,)),
        ],
        compiler_params=pltpu.CompilerParams(
            collective_id=0, has_side_effects=True, vmem_limit_bytes=67043328
        ),
    )(*big, *weights, *small)


def widen_kernel(pair_ref, qkv_ref, down_ref, up_ref, out_ref, proj_ref):
    i = pl.program_id(0)
    for first, last, ref in ((0, 4, down_ref), (4, 8, up_ref), (8, 9, out_ref)):

        @pl.when((i >= first) & (i < last))
        def _():
            for c in range(2):
                ref[:, c * 384 : c * 384 + 384] = pair_ref[c].astype(F32)

    @pl.when(i >= 9)
    def _():
        for p in range(6):
            proj_ref[:, p * 128 : p * 128 + 128] = qkv_ref[p].astype(F32)


def widen(parts):
    parts = parts.reshape(CHUNKS, 384, COLS)
    return pl.pallas_call(
        widen_kernel,
        grid=(12,),
        out_shape=(
            jax.ShapeDtypeStruct((1536, 768), F32),
            jax.ShapeDtypeStruct((384, 3072), F32),
            jax.ShapeDtypeStruct((384, 768), F32),
            jax.ShapeDtypeStruct((384, 2304), F32),
        ),
        in_specs=[
            pl.BlockSpec((2, 384, COLS), lambda i: (jnp.minimum(i, 8), 0, 0)),
            pl.BlockSpec((6, 384, 128), lambda i: (3, 0, jnp.maximum(i - 9, 0))),
        ],
        out_specs=(
            pl.BlockSpec((384, 768), lambda i: (jnp.minimum(i, 3), 0)),
            pl.BlockSpec((384, 768), lambda i: (0, jnp.clip(i - 4, 0, 3))),
            pl.BlockSpec((384, 768), lambda i: (0, 0)),
            pl.BlockSpec((384, 768), lambda i: (0, jnp.maximum(i - 9, 0))),
        ),
    )(parts, parts)


def block_shards(
    patches,
    segment_ids,
    mask_positions,
    mask_embed,
    norm1_gain,
    norm1_bias,
    w_qkv,
    query_bias,
    value_bias,
    w_out,
    out_bias,
    norm2_gain,
    norm2_bias,
    w_up,
    up_bias,
    w_down,
    down_bias,
    cotangent,
):
    swap = [(0, 1), (1, 0)]
    width = 768
    patch = patches[0]
    cot = cotangent[0]
    y = lax.axis_index("tm")
    ids = segment_ids[0]
    ids_row = lax.pad(ids.astype(BF16)[None], jnp.zeros((), BF16), ((0, 15, 0), (0, width - HALF, 0)))
    near = jnp.concatenate([lax.dynamic_slice(patch, ((1 - y) * TILE, 0), (TILE, width)), ids_row])
    near_x = lax.ppermute(near, "tm", swap)
    far_x = lax.ppermute(lax.dynamic_slice(patch, (y * TILE, 0), (TILE, width)), "tm", swap)
    ids_x = near_x[TILE, :HALF].astype(jnp.int32)
    table = tabulate(
        (mask_embed, norm1_gain, norm1_bias, query_bias, value_bias, out_bias, norm2_gain, norm2_bias, down_bias)
    )
    lane = jnp.arange(128)[None, :]
    qa = jnp.where(ids[:, None] == lane, 1.0, 0.0).astype(BF16)
    ka = jnp.where((lane >= 6) | (ids[:, None] == lane), 0.0, neg_large).astype(BF16)
    qxa = jnp.where(ids_x[:, None] == lane, 1.0, 0.0).astype(BF16)
    kxa = jnp.where((lane >= 6) | (ids_x[:, None] == lane), 0.0, neg_large).astype(BF16)
    qkv, hidden1 = front(own_kernel, patch, mask_positions, table, w_qkv)
    (other_near,) = front(partial(other_kernel, True), near_x, mask_positions, table, w_qkv)
    (other_far,) = front(partial(other_kernel, False), far_x, mask_positions, table, w_qkv)
    attended_near, attended_far, lse_near, lse_far = attend(qkv, other_near, other_far, qa, ka, kxa)
    parts, output, grad_patches, v = backward(
        (cot, w_out, qkv, hidden1, patch, w_qkv, other_near, other_far, attended_near, attended_far),
        (w_up, w_down),
        (qa, ka, qxa, kxa, lse_near, lse_far, table, mask_positions, up_bias.astype(F32)[None]),
    )
    grad_down, grad_up, grad_out, grad_qkv = widen(parts)
    return (
        output[None],
        grad_patches[None],
        v[0],
        v[1],
        v[2],
        grad_qkv,
        v[3],
        v[4],
        grad_out,
        v[5],
        v[6],
        v[7],
        grad_up,
        v[9:13].reshape(-1),
        grad_down,
        v[8],
    )


def shards(
    patches,
    segment_ids,
    mask_positions,
    mask_embed,
    norm1_gain,
    norm1_bias,
    w_qkv,
    query_bias,
    value_bias,
    w_out,
    out_bias,
    norm2_gain,
    norm2_bias,
    w_up,
    up_bias,
    w_down,
    down_bias,
    cotangent,
):
    rows_n, time_n, width = patches.shape
    query_scale = 1.0 / math.sqrt(HEAD)
    gain_one = norm1_gain.astype(jnp.float32)
    gain_two = norm2_gain.astype(jnp.float32)
    offset = lax.axis_index("tm") * time_n
    places = offset + lax.broadcasted_iota(jnp.int32, (rows_n, time_n, 1), 1)
    masked = jnp.any(places == mask_positions[:, None, :], axis=-1)[..., None]
    inputs = jnp.where(
        masked, mask_embed.astype(jnp.float32)[None, None, :], patches.astype(jnp.float32)
    )
    normed1, inverse1 = normalize(inputs)
    hidden1 = (normed1 * gain_one + norm1_bias.astype(jnp.float32)).astype(jnp.bfloat16)
    project = jnp.einsum("rtd,de->rte", hidden1, w_qkv, preferred_element_type=jnp.float32)
    queries = ((project[..., :width] + query_bias.astype(jnp.float32)) * query_scale).astype(
        jnp.bfloat16
    )
    keys_own = project[..., width : 2 * width].astype(jnp.bfloat16)
    values_own = (project[..., 2 * width :] + value_bias.astype(jnp.float32)).astype(jnp.bfloat16)
    keys_all, values_all, segments_all = (
        lax.all_gather(keys_own, "tm", axis=1, tiled=True),
        lax.all_gather(values_own, "tm", axis=1, tiled=True),
        lax.all_gather(segment_ids, "tm", axis=1, tiled=True),
    )
    same = segment_ids[:, :, None] == segments_all[:, None, :]
    query_heads = split_heads(queries)
    head_outputs, log_totals = attend_forward(
        query_heads, split_heads(keys_all), split_heads(values_all), same
    )
    attended = join_heads(head_outputs).astype(jnp.bfloat16)
    middle = (
        inputs
        + jnp.einsum("rtd,de->rte", attended, w_out, preferred_element_type=jnp.float32)
        + out_bias.astype(jnp.float32)
    )
    normed2, inverse2 = normalize(middle)
    hidden2 = (normed2 * gain_two + norm2_bias.astype(jnp.float32)).astype(jnp.bfloat16)
    upper = jnp.einsum(
        "rtd,df->rtf", hidden2, w_up, preferred_element_type=jnp.float32
    ) + up_bias.astype(jnp.float32)
    activated = jax.nn.gelu(upper, approximate=False).astype(jnp.bfloat16)
    result = (
        middle
        + jnp.einsum("rtf,fd->rtd", activated, w_down, preferred_element_type=jnp.float32)
        + down_bias.astype(jnp.float32)
    )
    output = result.astype(jnp.bfloat16)
    grad_result = cotangent.astype(jnp.float32)
    grad_w_down = jnp.einsum(
        "rtf,rtd->fd", activated, cotangent, preferred_element_type=jnp.float32
    )
    grad_down_bias = total_rows(grad_result)
    grad_activated = jnp.einsum(
        "rtd,fd->rtf", cotangent, w_down, preferred_element_type=jnp.float32
    )
    unused, gelu_pull = jax.vjp(partial(jax.nn.gelu, approximate=False), upper)
    grad_upper = gelu_pull(grad_activated)[0].astype(jnp.bfloat16)
    grad_w_up = jnp.einsum("rtd,rtf->df", hidden2, grad_upper, preferred_element_type=jnp.float32)
    grad_up_bias = total_rows(grad_upper)
    grad_hidden2 = jnp.einsum("rtf,df->rtd", grad_upper, w_up, preferred_element_type=jnp.float32)
    grad_gain_two = total_rows(grad_hidden2 * normed2)
    grad_bias_two = total_rows(grad_hidden2)
    grad_middle = grad_result + norm_back(grad_hidden2, normed2, inverse2, gain_two)
    mlp_vectors = jnp.stack([grad_gain_two, grad_bias_two, grad_down_bias], axis=1)
    grad_branch = grad_middle.astype(jnp.bfloat16)
    grad_w_out = jnp.einsum(
        "rtd,rte->de", attended, grad_branch, preferred_element_type=jnp.float32
    )
    grad_out_bias = total_rows(grad_branch)
    grad_attended = jnp.einsum(
        "rte,de->rtd", grad_branch, w_out, preferred_element_type=jnp.float32
    ).astype(jnp.bfloat16)
    keys_back, values_back, segments_back = (
        lax.all_gather(keys_own, "tm", axis=1, tiled=True),
        lax.all_gather(values_own, "tm", axis=1, tiled=True),
        lax.all_gather(segment_ids, "tm", axis=1, tiled=True),
    )
    same_back = segment_ids[:, :, None] == segments_back[:, None, :]
    grad_query_h, grad_keys_h, grad_values_h = attend_backward(
        query_heads,
        split_heads(keys_back),
        split_heads(values_back),
        split_heads(grad_attended),
        log_totals,
        same_back,
    )
    grad_keys, grad_values = (
        lax.psum_scatter(
            join_heads(grad_keys_h).astype(jnp.bfloat16), "tm", scatter_dimension=1, tiled=True
        ).astype(jnp.float32),
        lax.psum_scatter(
            join_heads(grad_values_h).astype(jnp.bfloat16), "tm", scatter_dimension=1, tiled=True
        ).astype(jnp.float32),
    )
    grad_queries = join_heads(grad_query_h).astype(jnp.bfloat16)
    grad_project = jnp.concatenate(
        [
            (grad_queries.astype(jnp.float32) * query_scale).astype(jnp.bfloat16),
            grad_keys.astype(jnp.bfloat16),
            grad_values.astype(jnp.bfloat16),
        ],
        axis=-1,
    )
    grad_w_qkv = jnp.einsum(
        "rtd,rte->de", hidden1, grad_project, preferred_element_type=jnp.float32
    )
    grad_query_bias = total_rows(grad_project[..., :width])
    grad_value_bias = total_rows(grad_project[..., 2 * width :])
    grad_hidden1 = jnp.einsum(
        "rte,de->rtd", grad_project, w_qkv, preferred_element_type=jnp.float32
    )
    grad_gain_one = total_rows(grad_hidden1 * normed1)
    grad_bias_one = total_rows(grad_hidden1)
    grad_inputs = grad_middle + norm_back(grad_hidden1, normed1, inverse1, gain_one)
    grad_mask = total_rows(jnp.where(masked, grad_inputs, 0.0))
    grad_patches = jnp.where(masked, 0.0, grad_inputs).astype(jnp.bfloat16)
    attn_vectors = jnp.stack(
        [grad_mask, grad_gain_one, grad_bias_one, grad_query_bias, grad_value_bias, grad_out_bias],
        axis=1,
    )
    every_part = (
        lax.psum_scatter(
            grad_w_qkv.astype(jnp.bfloat16), "tm", scatter_dimension=0, tiled=True
        ).astype(jnp.float32),
        lax.psum_scatter(
            grad_w_out.astype(jnp.bfloat16), "tm", scatter_dimension=0, tiled=True
        ).astype(jnp.float32),
        lax.psum_scatter(
            attn_vectors.astype(jnp.bfloat16), "tm", scatter_dimension=0, tiled=True
        ).astype(jnp.float32),
        lax.psum_scatter(
            grad_w_up.astype(jnp.bfloat16), "tm", scatter_dimension=0, tiled=True
        ).astype(jnp.float32),
        lax.psum_scatter(
            grad_w_down.astype(jnp.bfloat16), "tm", scatter_dimension=0, tiled=True
        ).astype(jnp.float32),
        lax.psum_scatter(
            mlp_vectors.astype(jnp.bfloat16), "tm", scatter_dimension=0, tiled=True
        ).astype(jnp.float32),
        lax.psum_scatter(
            grad_up_bias.astype(jnp.bfloat16), "tm", scatter_dimension=0, tiled=True
        ).astype(jnp.float32),
    )
    every_part = (
        lax.psum(every_part[0].astype(jnp.bfloat16), "rows").astype(jnp.float32),
        lax.psum(every_part[1].astype(jnp.bfloat16), "rows").astype(jnp.float32),
        lax.psum(every_part[2].astype(jnp.bfloat16), "rows").astype(jnp.float32),
        lax.psum(every_part[3].astype(jnp.bfloat16), "rows").astype(jnp.float32),
        lax.psum(every_part[4].astype(jnp.bfloat16), "rows").astype(jnp.float32),
        lax.psum(every_part[5].astype(jnp.bfloat16), "rows").astype(jnp.float32),
        lax.psum(every_part[6].astype(jnp.bfloat16), "rows").astype(jnp.float32),
    )
    summed_qkv, summed_out, summed_attn, summed_up, summed_down, summed_mlp, summed_up_bias = (
        every_part
    )
    return (
        output,
        grad_patches,
        summed_attn[:, 0],
        summed_attn[:, 1],
        summed_attn[:, 2],
        summed_qkv,
        summed_attn[:, 3],
        summed_attn[:, 4],
        summed_out,
        summed_attn[:, 5],
        summed_mlp[:, 0],
        summed_mlp[:, 1],
        summed_up,
        summed_up_bias,
        summed_down,
        summed_mlp[:, 2],
    )


def solution(mesh):
    placed = (
        P("rows", "tm", None),
        P("rows", "tm"),
        P("rows", None),
        P(),
        P(),
        P(),
        P(),
        P(),
        P(),
        P(),
        P(),
        P(),
        P(),
        P(),
        P(),
        P(),
        P(),
        P("rows", "tm", None),
    )
    return jax.shard_map(
        block_shards if dict(mesh.shape) == {"rows": 16, "tm": 2} else shards,
        mesh=mesh,
        in_specs=placed,
        out_specs=(
            P("rows", "tm", None),
            P("rows", "tm", None),
            P("tm"),
            P("tm"),
            P("tm"),
            P("tm", None),
            P("tm"),
            P("tm"),
            P("tm", None),
            P("tm"),
            P("tm"),
            P("tm"),
            P("tm", None),
            P("tm"),
            P("tm", None),
            P("tm"),
        ),
        check_vma=False,
    )
```

```python
from functools import partial
import math

import jax
import jax.numpy as jnp
from jax import lax
from jax.experimental import pallas as pl
from jax.experimental.pallas import tpu as pltpu
from jax.sharding import PartitionSpec as P

HEADS = 12
HEAD = 64


norm_eps = 1e-06
neg_large = -1e30


def normalize(values):
    center = values - jnp.mean(values, axis=-1, keepdims=True)
    scale_inv = lax.rsqrt(jnp.mean(center * center, axis=-1, keepdims=True) + norm_eps)
    return (center * scale_inv, scale_inv)


def norm_back(grad_out, normed, scale_inv, norm_gain):
    grad_normed = grad_out * norm_gain
    mean_one = jnp.mean(grad_normed, axis=-1, keepdims=True)
    mean_two = jnp.mean(grad_normed * normed, axis=-1, keepdims=True)
    return scale_inv * (grad_normed - mean_one - normed * mean_two)


def split_heads(tensor):
    rows_n, length, width = tensor.shape
    return tensor.reshape(rows_n, length, HEADS, width // HEADS).transpose(2, 0, 1, 3)


def join_heads(tensor):
    heads_n, rows_n, length, size = tensor.shape
    return tensor.transpose(1, 2, 0, 3).reshape(rows_n, length, heads_n * size)


def head_scores(query, keys_h, same):
    scores = jnp.einsum("rqd,rkd->rqk", query, keys_h, preferred_element_type=jnp.float32)
    return jnp.where(same, scores, neg_large)


def attend_forward(query_heads, key_heads, value_heads, same):

    def one_head(operands):
        query, keys_h, values_h = operands
        scores = head_scores(query, keys_h, same)
        peak = jnp.max(scores, axis=-1, keepdims=True)
        total = jnp.sum(jnp.exp(scores - peak), axis=-1, keepdims=True)
        log_total = peak + jnp.log(total)
        weights = jnp.exp(scores - log_total).astype(jnp.bfloat16)
        result = jnp.einsum("rqk,rkd->rqd", weights, values_h, preferred_element_type=jnp.float32)
        return (result, log_total[..., 0])

    return lax.map(one_head, (query_heads, key_heads, value_heads))


def attend_backward(query_heads, key_heads, value_heads, grad_heads, log_totals, same):

    def one_head(operands):
        query, keys_h, values_h, grad_out, log_total = operands
        scores = head_scores(query, keys_h, same)
        probs_full = jnp.exp(scores - log_total[..., None])
        probs_low = probs_full.astype(jnp.bfloat16)
        grad_values = jnp.einsum(
            "rqk,rqd->rkd", probs_low, grad_out, preferred_element_type=jnp.float32
        )
        grad_probs = jnp.einsum(
            "rqd,rkd->rqk", grad_out, values_h, preferred_element_type=jnp.float32
        )
        delta = jnp.sum(grad_probs * probs_full, axis=-1, keepdims=True)
        grad_scores = (probs_full * (grad_probs - delta)).astype(jnp.bfloat16)
        grad_query = jnp.einsum(
            "rqk,rkd->rqd", grad_scores, keys_h, preferred_element_type=jnp.float32
        )
        grad_keys = jnp.einsum(
            "rqk,rqd->rkd", grad_scores, query, preferred_element_type=jnp.float32
        )
        return (grad_query, grad_keys, grad_values)

    return lax.map(one_head, (query_heads, key_heads, value_heads, grad_heads, log_totals))


MESH = pl.DeviceIdType.MESH
SUB = 96
COLS = 384
LAGS = (0, 1, 4, 5, 6, 8, 9, 10)


def places():
    row = lax.axis_index("rows")
    y = lax.axis_index("tm")
    core = row % 2
    x = (row // 2) % 2
    z_low = (row // 4) % 2
    z_high = row // 8
    peers = (
        (row + 1 - 2 * core, y),
        (row, 1 - y),
        (row + 2 - 4 * x, y),
        (row + 4 - 8 * z_low, y),
        (row + 8 - 16 * z_high, y),
    )
    return core, x, y, peers


def greet(peers):
    barrier = pltpu.get_barrier_semaphore()
    for peer in peers:
        pl.semaphore_signal(barrier, inc=1, device_id=peer, device_id_type=MESH)
    pl.semaphore_wait(barrier, len(peers))


def total_rows(tensor):
    return jnp.sum(tensor.astype(jnp.float32), axis=(0, 1))


VMEM = pltpu.VMEM
F32 = jnp.float32
BF16 = jnp.bfloat16
HALF = 512
TILE = 256
R_EMBED, R_G1, R_B1, R_QB, R_VB, R_OB, R_G2, R_B2, R_DB, R_UB = 0, 1, 2, 3, 4, 5, 6, 7, 8, 9
QUERY_SCALE = 1.0 / math.sqrt(HEAD)


def dot(a, b):
    return lax.dot_general(a, b, (((1,), (0,)), ((), ())), preferred_element_type=F32)


def dot_t(a, b):
    return lax.dot_general(a, b, (((1,), (1,)), ((), ())), preferred_element_type=F32)


def t_dot(a, b):
    return lax.dot_general(a, b, (((0,), (0,)), ((), ())), preferred_element_type=F32)


def standard(values):
    center = values - jnp.mean(values, axis=-1, keepdims=True)
    scale_inv = lax.rsqrt(jnp.mean(center * center, axis=-1, keepdims=True) + norm_eps)
    return center * scale_inv, scale_inv


def masked_inputs(patch, first, marks, embed):
    at = first + lax.broadcasted_iota(jnp.int32, (patch.shape[0], 1), 0)
    flagged = jnp.max(jnp.where(at == marks, 1.0, 0.0), axis=-1, keepdims=True) > 0.5
    return flagged, jnp.where(flagged, embed, patch.astype(F32))


def project_tile(patch, first, marks_ref, table_ref, w_ref, qkv_ref, rows):
    unused, inputs = masked_inputs(patch, first, marks_ref[...], table_ref[R_EMBED : R_EMBED + 1, :])
    normed, unused = standard(inputs)
    hidden = (normed * table_ref[R_G1 : R_G1 + 1, :] + table_ref[R_B1 : R_B1 + 1, :]).astype(BF16)
    for part in range(6):
        cols = slice(part * 384, part * 384 + 384)
        project = dot(hidden, w_ref[:, cols])
        bias = slice((part % 2) * 384, (part % 2) * 384 + 384)
        if part < 2:
            project = (project + table_ref[R_QB : R_QB + 1, bias]) * QUERY_SCALE
        elif part >= 4:
            project = project + table_ref[R_VB : R_VB + 1, bias]
        qkv_ref[rows, cols] = project.astype(BF16)
    return hidden


def first_kernel(
    patch_h, wq_h, ids_ref, marks_ref, s0, s1, s2, s3, s4, s5, s6, s7, s8,
    qkv_h, h1_h, qkvx_h, att_h, lse_ref, qa_ref, ka_ref, qxa_ref, kxa_ref, table_ref,
    patch, patch_x, ids_x, wq, qkv, qkvx, h1, att, acc, tops, sums, insem, ssem, rsem, outsem,
):
    core, x, y, peers = places()
    partner = peers[1]
    lane = lax.broadcasted_iota(jnp.int32, (1, 128), 1)

    def rows_of(index):
        return pl.ds(pl.multiple_of(index * TILE, TILE), TILE)

    def lanes(start):
        return pl.ds(pl.multiple_of(start, 128), 128)

    near, far = rows_of(1 - y), rows_of(y)
    loads = [pltpu.make_async_copy(a, b, insem.at[i]) for i, (a, b) in enumerate(((patch_h, patch), (wq_h, wq)))]
    for load in loads:
        load.start()
    greet((partner,))
    loads[0].wait()
    sends = [
        pltpu.make_async_remote_copy(
            src_ref=src, dst_ref=dst, send_sem=ssem.at[i], recv_sem=rsem.at[i], device_id=partner, device_id_type=MESH
        )
        for i, (src, dst) in enumerate(
            (
                (ids_ref, ids_x),
                (patch.at[near, :], patch_x.at[near, :]),
                (patch.at[far, :], patch_x.at[far, :]),
            )
        )
    ]
    for send in sends:
        send.start()
    table_ref[...] = jnp.zeros_like(table_ref)
    for i, ref in enumerate((s0, s1, s2, s3, s4, s5, s6, s7, s8)):
        table_ref[i : i + 1, :] = ref[...].astype(F32).reshape(1, 768)

    def masks(ids, one_ref, mask_ref):
        hot = jnp.where(lax.broadcasted_iota(jnp.int32, (128, HALF), 0) == ids, 1.0, 0.0).T
        one_ref[...] = hot.astype(BF16)
        mask_ref[...] = jnp.where((lane >= 6) | (hot > 0.5), 0.0, neg_large).astype(BF16)

    masks(ids_ref[...], qa_ref, ka_ref)
    loads[1].wait()

    def own(i, carry):
        rows = rows_of(i)
        h1[rows, :] = project_tile(patch[rows, :], y * HALF + i * TILE, marks_ref, table_ref, wq, qkv, rows)
        return carry

    lax.fori_loop(0, 2, own, 0)
    stores = [
        pltpu.make_async_copy(a, b, outsem.at[i])
        for i, (a, b) in enumerate(((qkv, qkv_h), (h1, h1_h), (qkvx, qkvx_h), (att, att_h)))
    ]
    stores[0].start()
    stores[1].start()

    def absorb(groups, source, places_of, mask, first):
        def pair(p, carry):
            keys = jnp.concatenate([source[places_of, lanes(768 + p * 128)], mask], axis=1)
            values = source[places_of, lanes(1536 + p * 128)]
            for rows in groups:
                q = qkv[rows, lanes(p * 128)]
                qa = qa_ref[rows, :]
                top, total = tops[rows, :], sums[rows, :]
                if first:
                    top, total = jnp.where(p == 0, 0.0, top), jnp.where(p == 0, 0.0, total)
                else:
                    old = acc[rows, lanes(p * 128)]
                new_top, new_total = top, total
                kept = None
                for h in range(2):
                    mine = (lane // 64) == h
                    here = lane == 2 * p + h
                    scores = dot_t(jnp.concatenate([jnp.where(mine, q, 0), qa], axis=1), keys)
                    peak = jnp.max(scores, axis=-1, keepdims=True)
                    if not first:
                        before = jnp.sum(jnp.where(here, top, 0.0), axis=-1, keepdims=True)
                        peak = jnp.maximum(before, peak)
                        scale = jnp.exp(before - peak)
                    weights = jnp.exp(scores - peak)
                    number = jnp.sum(weights, axis=-1, keepdims=True)
                    out = dot(weights.astype(BF16), values)
                    if not first:
                        number = number + scale * jnp.sum(jnp.where(here, total, 0.0), axis=-1, keepdims=True)
                        out = out + scale * old
                    kept = out if h == 0 else jnp.where(mine, out, kept)
                    new_top = jnp.where(here, peak, new_top)
                    new_total = jnp.where(here, number, new_total)
                acc[rows, lanes(p * 128)] = kept
                tops[rows, :] = new_top
                sums[rows, :] = new_total
            return carry

        lax.fori_loop(0, 6, pair, 0)

    both = (slice(0, TILE), slice(TILE, HALF))
    absorb(both, qkv, slice(None), ka_ref[...], True)
    sends[0].wait_recv()
    masks(ids_x[...], qxa_ref, kxa_ref)
    sends[1].wait_recv()
    project_tile(patch_x[far, :], (1 - y) * HALF + y * TILE, marks_ref, table_ref, wq, qkvx, far)

    absorb(both, qkvx, far, kxa_ref[far, :], False)
    sends[2].wait_recv()
    project_tile(patch_x[near, :], (1 - y) * HALF + (1 - y) * TILE, marks_ref, table_ref, wq, qkvx, near)
    stores[2].start()
    absorb((near,), qkvx, near, kxa_ref[near, :], False)
    total = jnp.where(lane < 12, sums[...], 1.0)
    lse_ref[...] = (tops[...] + jnp.log(total)).T[:16, :]
    for p in range(6):
        for i in range(2):
            rows = slice(i * TILE, i * TILE + TILE)
            low, high = sums[rows, 2 * p : 2 * p + 1], sums[rows, 2 * p + 1 : 2 * p + 2]
            cols = slice(p * 128, p * 128 + 128)
            att[rows, cols] = (acc[rows, cols] / jnp.where(lane < 64, low, high)).astype(BF16)
    stores[3].start()
    for send in sends:
        send.wait_send()
    for store in stores:
        store.wait()


def first_half(patch, w_qkv, ids, marks, smalls):
    hbm = pl.BlockSpec(memory_space=pl.ANY)
    near = pl.BlockSpec(memory_space=pltpu.VMEM)
    dma = pltpu.SemaphoreType.DMA

    def low(*shape):
        return pltpu.VMEM(shape, BF16)

    return pl.pallas_call(
        first_kernel,
        out_shape=tuple(jax.ShapeDtypeStruct((HALF, n), BF16) for n in (2304, 768, 2304, 768))
        + (jax.ShapeDtypeStruct((16, HALF), F32),)
        + (jax.ShapeDtypeStruct((HALF, 128), BF16),) * 4
        + (jax.ShapeDtypeStruct((16, 768), F32),),
        in_specs=[hbm, hbm] + [near] * (2 + len(smalls)),
        out_specs=(hbm,) * 4 + (near,) * 6,
        scratch_shapes=[
            low(HALF, 768),
            low(HALF, 768),
            pltpu.VMEM((1, HALF), jnp.int32),
            low(768, 2304),
            low(HALF, 2304),
            low(HALF, 2304),
            low(HALF, 768),
            low(HALF, 768),
            pltpu.VMEM((HALF, 768), F32),
            pltpu.VMEM((HALF, 128), F32),
            pltpu.VMEM((HALF, 128), F32),
            dma((2,)),
            dma((3,)),
            dma((3,)),
            dma((4,)),
        ],
        compiler_params=pltpu.CompilerParams(collective_id=1, has_side_effects=True, vmem_limit_bytes=67043328),
    )(patch, w_qkv, ids, marks, *smalls)


ERFC_P = 0.3275911
ERFC_C = (
    0.1851102167482524,
    0.17993860771517878,
    0.21041948320823337,
    0.011498087426314028,
    0.47813345988158296,
    -0.4317659362057169,
    0.5111742647535956,
    -0.14450823957827402,
)


def gelu_and_slope(u):
    t = 1.0 / (1.0 + (ERFC_P * math.sqrt(0.5)) * jnp.abs(u))
    bell = jnp.exp(-0.5 * (u * u))
    series = ERFC_C[7]
    for c in ERFC_C[6::-1]:
        series = series * t + c
    tail = (0.5 * t) * series * bell
    phi = jnp.where(u < 0, tail, 1.0 - tail)
    return u * phi, phi + u * (bell * (1.0 / math.sqrt(2.0 * math.pi)))


CHUNKS = 24
SLOTS = 5
FF_TILE = 384
T_FORWARD = (0, 0, 1, 2, 3, 4, 5, 6)
EMIT_DOWN, EMIT_UP, EMIT_OUT, EMIT_QKV = (0, 2, 4, 6), (8, 10, 12, 14), (16,), (18, 19, 20, 21, 22, 23)
T_SECOND, T_ATTENDED = (7,), (8,)
T_SEND = (8, 9, 9, 10, 11, 11, 12, 13, 13, 14, 15, 15)
T_OWN = (8, 9, 10, 13, 14, 15)
T_FAR = (12, 13, 14, 16, 17, 18)
T_OUTPUT = (19, 19, 20, 20, 21, 21, 22, 22)
T_GRAD = (24, 24, 25)
T_FIRST = (26,)
T_VEC = 27


def halves_kernel(
    cot_h, wo_h, qkv_h, h1_h, patch_h, wq_h, qkvx_h, att_h, wu_h, wd_h,
    qa_ref, ka_ref, qxa_ref, kxa_ref, lse_ref, table_ref, marks_ref, ub_ref,
    parts_h, out_h, gp_h, vec_out,
    cot, wo, qkv, h1, patch, wq, qkvx, att, wu, wd,
    act, gu, mid, h2, acc, gb, do, dox, dqkv, dq, dk, dv, drow, dxrow, lsex_ref,
    g, r1, r2, r3, r4, r5, done, v0, v1, v2,
    insem, wusem, wdsem, ssem, rsem, vs, vr, xs, xr, outsem, lastsem,
):
    core, x, y, peers = places()
    pair, yp, xp, zp1, zp2 = peers
    lane = lax.broadcasted_iota(jnp.int32, (1, 128), 1)
    inputs = (
        (cot_h, cot), (wo_h, wo), (qkv_h, qkv), (h1_h, h1), (patch_h, patch), (wq_h, wq),
        (qkvx_h, qkvx), (att_h, att),
    )
    COT, WO, QKV, H1, PATCH, WQ, QKVX, ATT = range(8)

    def lanes(start, size=128):
        return pl.ds(pl.multiple_of(start, 128), size)

    def part_of(n):
        return (n // 2 + 4 * (n % 2)) * (1 - n // 8) + (n - 8) * (n // 8)

    def load(i):
        return pltpu.make_async_copy(inputs[i][0], inputs[i][1], insem.at[i])

    def up_tile(n):
        return pltpu.make_async_copy(wu_h.at[:, lanes(part_of(n) * FF_TILE, FF_TILE)], wu.at[n % 2], wusem.at[n % 2])

    def down_tile(n):
        rows = pl.ds(pl.multiple_of(part_of(n) * FF_TILE, FF_TILE), FF_TILE)
        return pltpu.make_async_copy(wd_h.at[rows, :], wd.at[n % 2], wdsem.at[n % 2])

    for i in (PATCH, WO, ATT):
        load(i).start()
    for n in range(2):
        up_tile(n).start()
        down_tile(n).start()
    for i in (COT, QKV, QKVX, H1, WQ):
        load(i).start()
    greet(peers)

    def remote(src, dst, send, recv, dev):
        return pltpu.make_async_remote_copy(
            src_ref=src, dst_ref=dst, send_sem=send, recv_sem=recv, device_id=dev, device_id_type=MESH
        )

    def copy(s, c):
        src, dst, dev = (
            lambda: (g.at[c % SLOTS, 1 - core], r1.at[c], pair),
            lambda: (r1.at[c, 1 - y], r2.at[c], yp),
            lambda: (r2.at[c, 1 - x], r3.at[c], xp),
            lambda: (r3.at[c], r4.at[c], zp1),
            lambda: (r4.at[c], r5.at[c], zp2),
            lambda: (done.at[c, core, x], done.at[c, core, x], xp),
            lambda: (done.at[c, core], done.at[c, core], pair),
        )[s]()
        return remote(src, dst, ssem.at[s, c], rsem.at[s, c], dev)

    def part_out(c):
        return pltpu.make_async_copy(done.at[c], parts_h.at[c], outsem.at[c])

    def stage(s, c):
        if s > 0:
            copy(s - 1, c).wait_recv()
        if s == 1:
            r1[c] = r1[c] + g[c % SLOTS, core]
        elif s == 2:
            r2[c] = r2[c] + r1[c, y]
        elif s == 3:
            r3[c] = r3[c] + r2[c, x]
        elif s == 4:
            r4[c] = r4[c] + r3[c]
        elif s == 5:
            done[c, core, x] = r5[c] + r4[c]
        elif s == 7:
            copy(5, c).wait_send()
            copy(6, c).wait_send()
            part_out(c).start()
        if s < 7:
            copy(s, c).start()

    def vec_copy(s):
        src, dst, dev = (
            lambda: (v0, v1, pair),
            lambda: (v1.at[1 - y], v2.at[0], yp),
            lambda: (v2.at[0], v2.at[1], xp),
            lambda: (v2.at[1], v2.at[2], zp1),
            lambda: (v2.at[2], v2.at[3], zp2),
        )[s]()
        return remote(src, dst, vs.at[s], vr.at[s], dev)

    def vec_stage(s):
        if s > 0:
            vec_copy(s - 1).wait_recv()
        if s == 1:
            v1[...] = v1[...] + v0[...]
        elif s == 2:
            v2[0] = v2[0] + v1[y]
        elif s == 5:
            vec_out[...] = v2[3] + v2[2]
        elif s > 2:
            v2[s - 2] = v2[s - 2] + v2[s - 3]
        if s < 5:
            vec_copy(s).start()

    def far_copy(i):
        src, dst = ((lse_ref, lsex_ref), (drow, dxrow))[i]
        return remote(src, dst, xs.at[i], xr.at[i], yp)

    def grad_copy(n):
        rows, cols = pl.ds(pl.multiple_of((n % 2) * TILE, TILE), TILE), lanes((n // 2) * 128)
        return remote(do.at[rows, cols], dox.at[rows, cols], xs.at[2 + n], xr.at[2 + n], yp)

    def row(r):
        return table_ref[r : r + 1, :]

    def add_vec(r, value):
        for half in range(2):
            v0[half, r : r + 1, :] = v0[half, r : r + 1, :] + value[:, half * 384 : half * 384 + 384]

    def emit(left, right, c):
        number = right.shape[1] // 384
        for i in range(number):

            @pl.when(c + i >= SLOTS)
            def _():
                copy(0, c + i - SLOTS).wait_send()

        for half in range(2):
            block = t_dot(left(half), right).astype(BF16)
            for i in range(number):
                for other in range(4):
                    rows = slice(other * SUB, other * SUB + SUB)
                    g[(c + i) % SLOTS, other // 2, half, other % 2] = block[rows, i * 384 : i * 384 + 384]

    def enter():
        for tile in range(HALF // TILE):
            rows = slice(tile * TILE, tile * TILE + TILE)
            unused, values = masked_inputs(patch[rows, :], y * HALF + tile * TILE, marks_ref[...], row(R_EMBED))
            total = values + dot(att[rows, :], wo[...]) + row(R_OB)
            normed, unused = standard(total)
            mid[rows, :] = total
            h2[rows, :] = (normed * row(R_G2) + row(R_B2)).astype(BF16)

    def forward(n):
        k = part_of(n)
        cols = lanes(k * FF_TILE, FF_TILE)
        up_tile(n).wait()
        down_tile(n).wait()
        sums = jnp.zeros((1, FF_TILE), F32)
        for tile in range(HALF // TILE):
            rows = slice(tile * TILE, tile * TILE + TILE)
            value, slope = gelu_and_slope(dot(h2[rows, :], wu[n % 2]) + ub_ref[:, cols])
            act[rows, cols] = value.astype(BF16)
            low = (dot_t(cot[rows, :], wd[n % 2]) * slope).astype(BF16)
            gu[rows, cols] = low
            sums = sums + jnp.sum(low.astype(F32), axis=0, keepdims=True)
            acc[rows, :] = acc[rows, :] + dot_t(low, wu[n % 2])
        v0[k // 4, pl.ds(9 + k % 4, 1), :] = sums
        down_tile(n + 2).start()

        @pl.when(n + 2 < 8)
        def _():
            up_tile(n + 2).start()

    def second_norm():
        def tile(i, carry):
            rows = pl.ds(pl.multiple_of(i * 128, 128), 128)
            normed, inverse = standard(mid[rows, :])
            grad = acc[rows, :]
            cotangent = cot[rows, :].astype(F32)
            add_vec(6, jnp.sum(grad * normed, axis=0, keepdims=True))
            add_vec(7, jnp.sum(grad, axis=0, keepdims=True))
            add_vec(8, jnp.sum(cotangent, axis=0, keepdims=True))
            total = cotangent + norm_back(grad, normed, inverse, row(R_G2))
            acc[rows, :] = total
            low = total.astype(BF16)
            gb[rows, :] = low
            add_vec(5, jnp.sum(low.astype(F32), axis=0, keepdims=True))
            return carry

        lax.fori_loop(0, 4, tile, 0)

    def grad_attended():
        for tile in range(2):
            rows = slice(tile * 256, tile * 256 + 256)
            do[rows, :] = dot_t(gb[rows, :], wo[...]).astype(BF16)
        for tile in range(4):
            rows = slice(tile * 128, tile * 128 + 128)
            columns = jnp.zeros((128, 128), F32)
            for p in range(6):
                cols = slice(p * 128, p * 128 + 128)
                product = do[rows, cols].astype(F32) * att[rows, cols].astype(F32)
                for h in range(2):
                    total = jnp.sum(jnp.where((lane // 64) == h, product, 0.0), axis=1, keepdims=True)
                    columns = jnp.where(lane == 2 * p + h, total, columns)
            drow[:, rows] = columns.T[:16, :]
        far_copy(1).start()

    def piece(keys, key_mask, values, query, query_mask, grad, lse, delta):
        scores = dot_t(jnp.concatenate([keys, key_mask], axis=1), jnp.concatenate([query, query_mask], axis=1))
        probs = jnp.exp(scores - lse)
        grad_scores = probs * (dot_t(values, grad) - delta)
        return probs.astype(BF16), grad_scores.astype(BF16)

    def own_pair(p):
        slot = p % 3

        def head(h, carry):
            mine = (lane // 64) == h
            stat = pl.ds(2 * p + h, 1)
            query = jnp.where(mine, qkv[:, lanes(p * 128)], 0)
            grad = jnp.where(mine, do[:, lanes(p * 128)], 0)
            for tile in range(2):
                rows = slice(tile * 256, tile * 256 + 256)
                keys = qkv[rows, lanes(768 + p * 128)]
                probs, scores = piece(
                    keys, ka_ref[rows, :], qkv[rows, lanes(1536 + p * 128)], query, qa_ref[...], grad,
                    lse_ref[stat, :], drow[stat, :],
                )
                new = dot(scores, query)
                dk[slot, rows, :] = jnp.where(h == 0, new, dk[slot, rows, :] + new)
                new = dot(probs, grad)
                dv[slot, rows, :] = jnp.where(h == 0, new, dv[slot, rows, :] + new)
                new = t_dot(scores, jnp.where(mine, keys, 0))
                dq[slot] = jnp.where((h == 0) & (tile == 0), new, dq[slot] + new)
            return carry

        lax.fori_loop(0, 2, head, 0)

    def far_pair(p):
        slot = p % 3
        grad_copy(2 * p).wait_recv()
        grad_copy(2 * p + 1).wait_recv()
        near, far = pl.multiple_of((1 - y) * 256, 256), pl.multiple_of(y * 256, 256)

        def head(h, carry):
            mine = (lane // 64) == h
            stat = pl.ds(2 * p + h, 1)
            for first, start, size in ((far, 0, 512), (near, near, 256)):
                rows, others = pl.ds(first, 256), pl.ds(start, size)
                query = jnp.where(mine, qkv[others, lanes(p * 128)], 0)
                grad = jnp.where(mine, do[others, lanes(p * 128)], 0)
                keys = qkvx[rows, lanes(768 + p * 128)]
                probs, scores = piece(
                    keys, kxa_ref[rows, :], qkvx[rows, lanes(1536 + p * 128)], query, qa_ref[others, :], grad,
                    lse_ref[stat, others], drow[stat, others],
                )
                dq[slot, others, :] = dq[slot, others, :] + t_dot(scores, jnp.where(mine, keys, 0))
            for first, start, size in ((near, 0, 512), (far, far, 256)):
                rows, others = pl.ds(first, 256), pl.ds(start, size)
                query = jnp.where(mine, qkvx[others, lanes(p * 128)], 0)
                grad = jnp.where(mine, dox[others, lanes(p * 128)], 0)
                probs, scores = piece(
                    qkv[rows, lanes(768 + p * 128)], ka_ref[rows, :], qkv[rows, lanes(1536 + p * 128)],
                    query, qxa_ref[others, :], grad, lsex_ref[stat, others], dxrow[stat, others],
                )
                dk[slot, rows, :] = dk[slot, rows, :] + dot(scores, query)
                dv[slot, rows, :] = dv[slot, rows, :] + dot(probs, grad)
            return carry

        lax.fori_loop(0, 2, head, 0)
        dqkv[:, lanes(p * 128)] = (dq[slot].astype(BF16).astype(F32) * QUERY_SCALE).astype(BF16)
        dqkv[:, lanes(768 + p * 128)] = dk[slot].astype(BF16)
        dqkv[:, lanes(1536 + p * 128)] = dv[slot].astype(BF16)

    def output_tile(i):
        n = i + 8
        down_tile(n).wait()
        for tile in range(2):
            rows = slice(tile * 256, tile * 256 + 256)
            mid[rows, :] = mid[rows, :] + dot(act[rows, lanes(i * FF_TILE, FF_TILE)], wd[n % 2])

        @pl.when(n + 2 < 16)
        def _():
            down_tile(n + 2).start()

    def store_output():
        for tile in range(4):
            rows = slice(tile * 128, tile * 128 + 128)
            gb[rows, :] = (mid[rows, :] + row(R_DB)).astype(BF16)
        pltpu.make_async_copy(gb, out_h, lastsem.at[0]).start()

    def grad_first(part):
        for tile in range(2):
            rows = slice(tile * 256, tile * 256 + 256)
            new = dot_t(dqkv[rows, lanes(part * 768, 768)], wq[:, lanes(part * 768, 768)])
            mid[rows, :] = jnp.where(part == 0, new, mid[rows, :] + new)

    def first_norm():
        def tile(i, carry):
            rows = pl.ds(pl.multiple_of(i * 128, 128), 128)
            flagged, values = masked_inputs(patch[rows, :], y * HALF + i * 128, marks_ref[...], row(R_EMBED))
            normed, inverse = standard(values)
            grad = mid[rows, :]
            add_vec(1, jnp.sum(grad * normed, axis=0, keepdims=True))
            add_vec(2, jnp.sum(grad, axis=0, keepdims=True))
            total = acc[rows, :] + norm_back(grad, normed, inverse, row(R_G1))
            add_vec(0, jnp.sum(jnp.where(flagged, total, 0.0), axis=0, keepdims=True))
            att[rows, :] = jnp.where(flagged, 0.0, total).astype(BF16)
            add_vec(3, jnp.sum(dqkv[rows, :768].astype(F32), axis=0, keepdims=True))
            add_vec(4, jnp.sum(dqkv[rows, 1536:].astype(F32), axis=0, keepdims=True))
            return carry

        lax.fori_loop(0, 4, tile, 0)
        pltpu.make_async_copy(att, gp_h, lastsem.at[1]).start()

    far_copy(0).start()
    acc[...] = jnp.zeros_like(acc)
    v0[...] = jnp.zeros_like(v0)
    for i in (PATCH, WO, ATT):
        load(i).wait()
    enter()
    load(COT).wait()

    def step(t, carry):
        def run(times, body):
            def before(now):
                return sum(jnp.where(now > at, 1, 0) for at in times)

            def one(n, inner):
                body(n)
                return inner

            lax.fori_loop(before(t), before(t + 1), one, 0)

        def need(at, *names):
            @pl.when(t == at)
            def _():
                for i in names:
                    load(i).wait()

        need(2, QKV, QKVX, H1, WQ)
        run(T_FORWARD, forward)
        run(
            EMIT_DOWN,
            lambda n: emit(lambda half: act[:, lanes(half * 1536 + n * 384, 384)], cot[...], 2 * n),
        )
        run(
            EMIT_UP,
            lambda n: emit(lambda half: h2[:, half * 384 : half * 384 + 384], gu[:, lanes(n * 768, 768)], 8 + 2 * n),
        )
        run(EMIT_OUT, lambda n: emit(lambda half: att[:, half * 384 : half * 384 + 384], gb[...], 16))

        def emit_qkv(p):
            right = jnp.concatenate([dqkv[:, lanes(part * 768 + p * 128)] for part in range(3)], axis=1)
            emit(lambda half: h1[:, half * 384 : half * 384 + 384], right, 18 + p)

        run(EMIT_QKV, emit_qkv)
        for s in range(2):
            c = t - LAGS[s]

            @pl.when((c >= 0) & (c < CHUNKS))
            def _():
                stage(s, c)

        run(T_SECOND, lambda n: second_norm())
        run(T_ATTENDED, lambda n: grad_attended())
        run(T_SEND, lambda n: grad_copy(n).start())
        run(T_OWN, own_pair)

        @pl.when(t == T_FAR[0])
        def _():
            far_copy(0).wait_recv()
            far_copy(1).wait_recv()

        run(T_FAR, far_pair)
        run(T_OUTPUT, output_tile)

        @pl.when(t == T_OUTPUT[-1])
        def _():
            store_output()

        run(T_GRAD, grad_first)
        run(T_FIRST, lambda n: first_norm())

        for s in range(2, 8):
            c = t - LAGS[s]

            @pl.when((c >= 0) & (c < CHUNKS))
            def _():
                stage(s, c)

        for s in range(6):

            @pl.when(t == T_VEC + s)
            def _():
                vec_stage(s)

        return carry

    lax.fori_loop(0, max(T_VEC + 6, CHUNKS + LAGS[7]), step, 0)

    def drain(c, carry):
        for s in range(1, 5):
            copy(s, c).wait_send()
        part_out(c).wait()
        return carry

    lax.fori_loop(0, CHUNKS, drain, 0)
    for c in range(CHUNKS - SLOTS, CHUNKS):
        copy(0, c).wait_send()
    for s in range(5):
        vec_copy(s).wait_send()
    for i in range(2):
        far_copy(i).wait_send()

    def drain_grad(n, carry):
        grad_copy(n).wait_send()
        return carry

    lax.fori_loop(0, 12, drain_grad, 0)
    pltpu.make_async_copy(gb, out_h, lastsem.at[0]).wait()
    pltpu.make_async_copy(att, gp_h, lastsem.at[1]).wait()


def backward(big, weights, small):
    hbm = pl.BlockSpec(memory_space=pl.ANY)
    near = pl.BlockSpec(memory_space=pltpu.VMEM)

    def low(*shape):
        return pltpu.VMEM(shape, BF16)

    def full(*shape):
        return pltpu.VMEM(shape, F32)

    dma = pltpu.SemaphoreType.DMA
    held = [pltpu.VMEM(a.shape, a.dtype) for a in big]
    return pl.pallas_call(
        halves_kernel,
        out_shape=(
            jax.ShapeDtypeStruct((CHUNKS, 2, 2, SUB, COLS), BF16),
            jax.ShapeDtypeStruct((HALF, 768), BF16),
            jax.ShapeDtypeStruct((HALF, 768), BF16),
            jax.ShapeDtypeStruct((16, COLS), F32),
        ),
        in_specs=[hbm] * (len(big) + 2) + [near] * len(small),
        out_specs=(hbm, hbm, hbm, near),
        scratch_shapes=held
        + [
            low(2, 768, FF_TILE),
            low(2, FF_TILE, 768),
            low(HALF, 3072),
            low(HALF, 3072),
            full(HALF, 768),
            low(HALF, 768),
            full(HALF, 768),
            low(HALF, 768),
            low(HALF, 768),
            low(HALF, 768),
            low(HALF, 2304),
            full(3, HALF, 128),
            full(3, HALF, 128),
            full(3, HALF, 128),
            full(16, HALF),
            full(16, HALF),
            full(16, HALF),
            low(SLOTS, 2, 2, 2, SUB, COLS),
            low(CHUNKS, 2, 2, SUB, COLS),
            low(CHUNKS, 2, SUB, COLS),
            low(CHUNKS, SUB, COLS),
            low(CHUNKS, SUB, COLS),
            low(CHUNKS, SUB, COLS),
            low(CHUNKS, 2, 2, SUB, COLS),
            full(2, 16, COLS),
            full(2, 16, COLS),
            full(4, 16, COLS),
            dma((8,)),
            dma((2,)),
            dma((2,)),
            dma((7, CHUNKS)),
            dma((7, CHUNKS)),
            dma((5,)),
            dma((5,)),
            dma((14,)),
            dma((14,)),
            dma((CHUNKS,)),
            dma((2,)),
        ],
        compiler_params=pltpu.CompilerParams(
            collective_id=0, has_side_effects=True, vmem_limit_bytes=67043328
        ),
    )(*big, *weights, *small)


def widen_kernel(pair_ref, qkv_ref, down_ref, up_ref, out_ref, proj_ref):
    i = pl.program_id(0)
    for first, last, ref in ((0, 4, down_ref), (4, 8, up_ref), (8, 9, out_ref)):

        @pl.when((i >= first) & (i < last))
        def _():
            for c in range(2):
                ref[:, c * 384 : c * 384 + 384] = pair_ref[c].astype(F32)

    @pl.when(i >= 9)
    def _():
        for p in range(6):
            proj_ref[:, p * 128 : p * 128 + 128] = qkv_ref[p].astype(F32)


def widen(parts):
    parts = parts.reshape(CHUNKS, 384, COLS)
    return pl.pallas_call(
        widen_kernel,
        grid=(12,),
        out_shape=(
            jax.ShapeDtypeStruct((1536, 768), F32),
            jax.ShapeDtypeStruct((384, 3072), F32),
            jax.ShapeDtypeStruct((384, 768), F32),
            jax.ShapeDtypeStruct((384, 2304), F32),
        ),
        in_specs=[
            pl.BlockSpec((2, 384, COLS), lambda i: (jnp.minimum(i, 8), 0, 0)),
            pl.BlockSpec((6, 384, 128), lambda i: (3, 0, jnp.maximum(i - 9, 0))),
        ],
        out_specs=(
            pl.BlockSpec((384, 768), lambda i: (jnp.minimum(i, 3), 0)),
            pl.BlockSpec((384, 768), lambda i: (0, jnp.clip(i - 4, 0, 3))),
            pl.BlockSpec((384, 768), lambda i: (0, 0)),
            pl.BlockSpec((384, 768), lambda i: (0, jnp.maximum(i - 9, 0))),
        ),
    )(parts, parts)


def block_shards(
    patches,
    segment_ids,
    mask_positions,
    mask_embed,
    norm1_gain,
    norm1_bias,
    w_qkv,
    query_bias,
    value_bias,
    w_out,
    out_bias,
    norm2_gain,
    norm2_bias,
    w_up,
    up_bias,
    w_down,
    down_bias,
    cotangent,
):
    patch = patches[0]
    cot = cotangent[0]
    qkv, hidden1, qkv_x, attended, lse, qa, ka, qxa, kxa, table = first_half(
        patch,
        w_qkv,
        segment_ids,
        mask_positions,
        (mask_embed, norm1_gain, norm1_bias, query_bias, value_bias, out_bias, norm2_gain, norm2_bias, down_bias),
    )
    parts, output, grad_patches, v = backward(
        (cot, w_out, qkv, hidden1, patch, w_qkv, qkv_x, attended),
        (w_up, w_down),
        (qa, ka, qxa, kxa, lse, table, mask_positions, up_bias.astype(F32)[None]),
    )
    grad_down, grad_up, grad_out, grad_qkv = widen(parts)
    return (
        output[None],
        grad_patches[None],
        v[0],
        v[1],
        v[2],
        grad_qkv,
        v[3],
        v[4],
        grad_out,
        v[5],
        v[6],
        v[7],
        grad_up,
        v[9:13].reshape(-1),
        grad_down,
        v[8],
    )


def shards(
    patches,
    segment_ids,
    mask_positions,
    mask_embed,
    norm1_gain,
    norm1_bias,
    w_qkv,
    query_bias,
    value_bias,
    w_out,
    out_bias,
    norm2_gain,
    norm2_bias,
    w_up,
    up_bias,
    w_down,
    down_bias,
    cotangent,
):
    rows_n, time_n, width = patches.shape
    query_scale = 1.0 / math.sqrt(HEAD)
    gain_one = norm1_gain.astype(jnp.float32)
    gain_two = norm2_gain.astype(jnp.float32)
    offset = lax.axis_index("tm") * time_n
    places = offset + lax.broadcasted_iota(jnp.int32, (rows_n, time_n, 1), 1)
    masked = jnp.any(places == mask_positions[:, None, :], axis=-1)[..., None]
    inputs = jnp.where(
        masked, mask_embed.astype(jnp.float32)[None, None, :], patches.astype(jnp.float32)
    )
    normed1, inverse1 = normalize(inputs)
    hidden1 = (normed1 * gain_one + norm1_bias.astype(jnp.float32)).astype(jnp.bfloat16)
    project = jnp.einsum("rtd,de->rte", hidden1, w_qkv, preferred_element_type=jnp.float32)
    queries = ((project[..., :width] + query_bias.astype(jnp.float32)) * query_scale).astype(
        jnp.bfloat16
    )
    keys_own = project[..., width : 2 * width].astype(jnp.bfloat16)
    values_own = (project[..., 2 * width :] + value_bias.astype(jnp.float32)).astype(jnp.bfloat16)
    keys_all, values_all, segments_all = (
        lax.all_gather(keys_own, "tm", axis=1, tiled=True),
        lax.all_gather(values_own, "tm", axis=1, tiled=True),
        lax.all_gather(segment_ids, "tm", axis=1, tiled=True),
    )
    same = segment_ids[:, :, None] == segments_all[:, None, :]
    query_heads = split_heads(queries)
    head_outputs, log_totals = attend_forward(
        query_heads, split_heads(keys_all), split_heads(values_all), same
    )
    attended = join_heads(head_outputs).astype(jnp.bfloat16)
    middle = (
        inputs
        + jnp.einsum("rtd,de->rte", attended, w_out, preferred_element_type=jnp.float32)
        + out_bias.astype(jnp.float32)
    )
    normed2, inverse2 = normalize(middle)
    hidden2 = (normed2 * gain_two + norm2_bias.astype(jnp.float32)).astype(jnp.bfloat16)
    upper = jnp.einsum(
        "rtd,df->rtf", hidden2, w_up, preferred_element_type=jnp.float32
    ) + up_bias.astype(jnp.float32)
    activated = jax.nn.gelu(upper, approximate=False).astype(jnp.bfloat16)
    result = (
        middle
        + jnp.einsum("rtf,fd->rtd", activated, w_down, preferred_element_type=jnp.float32)
        + down_bias.astype(jnp.float32)
    )
    output = result.astype(jnp.bfloat16)
    grad_result = cotangent.astype(jnp.float32)
    grad_w_down = jnp.einsum(
        "rtf,rtd->fd", activated, cotangent, preferred_element_type=jnp.float32
    )
    grad_down_bias = total_rows(grad_result)
    grad_activated = jnp.einsum(
        "rtd,fd->rtf", cotangent, w_down, preferred_element_type=jnp.float32
    )
    unused, gelu_pull = jax.vjp(partial(jax.nn.gelu, approximate=False), upper)
    grad_upper = gelu_pull(grad_activated)[0].astype(jnp.bfloat16)
    grad_w_up = jnp.einsum("rtd,rtf->df", hidden2, grad_upper, preferred_element_type=jnp.float32)
    grad_up_bias = total_rows(grad_upper)
    grad_hidden2 = jnp.einsum("rtf,df->rtd", grad_upper, w_up, preferred_element_type=jnp.float32)
    grad_gain_two = total_rows(grad_hidden2 * normed2)
    grad_bias_two = total_rows(grad_hidden2)
    grad_middle = grad_result + norm_back(grad_hidden2, normed2, inverse2, gain_two)
    mlp_vectors = jnp.stack([grad_gain_two, grad_bias_two, grad_down_bias], axis=1)
    grad_branch = grad_middle.astype(jnp.bfloat16)
    grad_w_out = jnp.einsum(
        "rtd,rte->de", attended, grad_branch, preferred_element_type=jnp.float32
    )
    grad_out_bias = total_rows(grad_branch)
    grad_attended = jnp.einsum(
        "rte,de->rtd", grad_branch, w_out, preferred_element_type=jnp.float32
    ).astype(jnp.bfloat16)
    keys_back, values_back, segments_back = (
        lax.all_gather(keys_own, "tm", axis=1, tiled=True),
        lax.all_gather(values_own, "tm", axis=1, tiled=True),
        lax.all_gather(segment_ids, "tm", axis=1, tiled=True),
    )
    same_back = segment_ids[:, :, None] == segments_back[:, None, :]
    grad_query_h, grad_keys_h, grad_values_h = attend_backward(
        query_heads,
        split_heads(keys_back),
        split_heads(values_back),
        split_heads(grad_attended),
        log_totals,
        same_back,
    )
    grad_keys, grad_values = (
        lax.psum_scatter(
            join_heads(grad_keys_h).astype(jnp.bfloat16), "tm", scatter_dimension=1, tiled=True
        ).astype(jnp.float32),
        lax.psum_scatter(
            join_heads(grad_values_h).astype(jnp.bfloat16), "tm", scatter_dimension=1, tiled=True
        ).astype(jnp.float32),
    )
    grad_queries = join_heads(grad_query_h).astype(jnp.bfloat16)
    grad_project = jnp.concatenate(
        [
            (grad_queries.astype(jnp.float32) * query_scale).astype(jnp.bfloat16),
            grad_keys.astype(jnp.bfloat16),
            grad_values.astype(jnp.bfloat16),
        ],
        axis=-1,
    )
    grad_w_qkv = jnp.einsum(
        "rtd,rte->de", hidden1, grad_project, preferred_element_type=jnp.float32
    )
    grad_query_bias = total_rows(grad_project[..., :width])
    grad_value_bias = total_rows(grad_project[..., 2 * width :])
    grad_hidden1 = jnp.einsum(
        "rte,de->rtd", grad_project, w_qkv, preferred_element_type=jnp.float32
    )
    grad_gain_one = total_rows(grad_hidden1 * normed1)
    grad_bias_one = total_rows(grad_hidden1)
    grad_inputs = grad_middle + norm_back(grad_hidden1, normed1, inverse1, gain_one)
    grad_mask = total_rows(jnp.where(masked, grad_inputs, 0.0))
    grad_patches = jnp.where(masked, 0.0, grad_inputs).astype(jnp.bfloat16)
    attn_vectors = jnp.stack(
        [grad_mask, grad_gain_one, grad_bias_one, grad_query_bias, grad_value_bias, grad_out_bias],
        axis=1,
    )
    every_part = (
        lax.psum_scatter(
            grad_w_qkv.astype(jnp.bfloat16), "tm", scatter_dimension=0, tiled=True
        ).astype(jnp.float32),
        lax.psum_scatter(
            grad_w_out.astype(jnp.bfloat16), "tm", scatter_dimension=0, tiled=True
        ).astype(jnp.float32),
        lax.psum_scatter(
            attn_vectors.astype(jnp.bfloat16), "tm", scatter_dimension=0, tiled=True
        ).astype(jnp.float32),
        lax.psum_scatter(
            grad_w_up.astype(jnp.bfloat16), "tm", scatter_dimension=0, tiled=True
        ).astype(jnp.float32),
        lax.psum_scatter(
            grad_w_down.astype(jnp.bfloat16), "tm", scatter_dimension=0, tiled=True
        ).astype(jnp.float32),
        lax.psum_scatter(
            mlp_vectors.astype(jnp.bfloat16), "tm", scatter_dimension=0, tiled=True
        ).astype(jnp.float32),
        lax.psum_scatter(
            grad_up_bias.astype(jnp.bfloat16), "tm", scatter_dimension=0, tiled=True
        ).astype(jnp.float32),
    )
    every_part = (
        lax.psum(every_part[0].astype(jnp.bfloat16), "rows").astype(jnp.float32),
        lax.psum(every_part[1].astype(jnp.bfloat16), "rows").astype(jnp.float32),
        lax.psum(every_part[2].astype(jnp.bfloat16), "rows").astype(jnp.float32),
        lax.psum(every_part[3].astype(jnp.bfloat16), "rows").astype(jnp.float32),
        lax.psum(every_part[4].astype(jnp.bfloat16), "rows").astype(jnp.float32),
        lax.psum(every_part[5].astype(jnp.bfloat16), "rows").astype(jnp.float32),
        lax.psum(every_part[6].astype(jnp.bfloat16), "rows").astype(jnp.float32),
    )
    summed_qkv, summed_out, summed_attn, summed_up, summed_down, summed_mlp, summed_up_bias = (
        every_part
    )
    return (
        output,
        grad_patches,
        summed_attn[:, 0],
        summed_attn[:, 1],
        summed_attn[:, 2],
        summed_qkv,
        summed_attn[:, 3],
        summed_attn[:, 4],
        summed_out,
        summed_attn[:, 5],
        summed_mlp[:, 0],
        summed_mlp[:, 1],
        summed_up,
        summed_up_bias,
        summed_down,
        summed_mlp[:, 2],
    )


def solution(mesh):
    placed = (
        P("rows", "tm", None),
        P("rows", "tm"),
        P("rows", None),
        P(),
        P(),
        P(),
        P(),
        P(),
        P(),
        P(),
        P(),
        P(),
        P(),
        P(),
        P(),
        P(),
        P(),
        P("rows", "tm", None),
    )
    return jax.shard_map(
        block_shards if dict(mesh.shape) == {"rows": 16, "tm": 2} else shards,
        mesh=mesh,
        in_specs=placed,
        out_specs=(
            P("rows", "tm", None),
            P("rows", "tm", None),
            P("tm"),
            P("tm"),
            P("tm"),
            P("tm", None),
            P("tm"),
            P("tm"),
            P("tm", None),
            P("tm"),
            P("tm"),
            P("tm"),
            P("tm", None),
            P("tm"),
            P("tm", None),
            P("tm"),
        ),
        check_vma=False,
    )
```

```python
from functools import partial
import math

import jax
import jax.numpy as jnp
from jax import lax
from jax.experimental import pallas as pl
from jax.experimental.pallas import tpu as pltpu
from jax.sharding import PartitionSpec as P

HEADS = 12
HEAD = 64


norm_eps = 1e-06
neg_large = -1e30


def normalize(values):
    center = values - jnp.mean(values, axis=-1, keepdims=True)
    scale_inv = lax.rsqrt(jnp.mean(center * center, axis=-1, keepdims=True) + norm_eps)
    return (center * scale_inv, scale_inv)


def norm_back(grad_out, normed, scale_inv, norm_gain):
    grad_normed = grad_out * norm_gain
    mean_one = jnp.mean(grad_normed, axis=-1, keepdims=True)
    mean_two = jnp.mean(grad_normed * normed, axis=-1, keepdims=True)
    return scale_inv * (grad_normed - mean_one - normed * mean_two)


def split_heads(tensor):
    rows_n, length, width = tensor.shape
    return tensor.reshape(rows_n, length, HEADS, width // HEADS).transpose(2, 0, 1, 3)


def join_heads(tensor):
    heads_n, rows_n, length, size = tensor.shape
    return tensor.transpose(1, 2, 0, 3).reshape(rows_n, length, heads_n * size)


def head_scores(query, keys_h, same):
    scores = jnp.einsum("rqd,rkd->rqk", query, keys_h, preferred_element_type=jnp.float32)
    return jnp.where(same, scores, neg_large)


def attend_forward(query_heads, key_heads, value_heads, same):

    def one_head(operands):
        query, keys_h, values_h = operands
        scores = head_scores(query, keys_h, same)
        peak = jnp.max(scores, axis=-1, keepdims=True)
        total = jnp.sum(jnp.exp(scores - peak), axis=-1, keepdims=True)
        log_total = peak + jnp.log(total)
        weights = jnp.exp(scores - log_total).astype(jnp.bfloat16)
        result = jnp.einsum("rqk,rkd->rqd", weights, values_h, preferred_element_type=jnp.float32)
        return (result, log_total[..., 0])

    return lax.map(one_head, (query_heads, key_heads, value_heads))


def attend_backward(query_heads, key_heads, value_heads, grad_heads, log_totals, same):

    def one_head(operands):
        query, keys_h, values_h, grad_out, log_total = operands
        scores = head_scores(query, keys_h, same)
        probs_full = jnp.exp(scores - log_total[..., None])
        probs_low = probs_full.astype(jnp.bfloat16)
        grad_values = jnp.einsum(
            "rqk,rqd->rkd", probs_low, grad_out, preferred_element_type=jnp.float32
        )
        grad_probs = jnp.einsum(
            "rqd,rkd->rqk", grad_out, values_h, preferred_element_type=jnp.float32
        )
        delta = jnp.sum(grad_probs * probs_full, axis=-1, keepdims=True)
        grad_scores = (probs_full * (grad_probs - delta)).astype(jnp.bfloat16)
        grad_query = jnp.einsum(
            "rqk,rkd->rqd", grad_scores, keys_h, preferred_element_type=jnp.float32
        )
        grad_keys = jnp.einsum(
            "rqk,rqd->rkd", grad_scores, query, preferred_element_type=jnp.float32
        )
        return (grad_query, grad_keys, grad_values)

    return lax.map(one_head, (query_heads, key_heads, value_heads, grad_heads, log_totals))


MESH = pl.DeviceIdType.MESH
SUB = 96
COLS = 384
LAGS = (0, 1, 4, 5, 6, 8, 9, 10)


def places():
    row = lax.axis_index("rows")
    y = lax.axis_index("tm")
    core = row % 2
    x = (row // 2) % 2
    z_low = (row // 4) % 2
    z_high = row // 8
    peers = (
        (row + 1 - 2 * core, y),
        (row, 1 - y),
        (row + 2 - 4 * x, y),
        (row + 4 - 8 * z_low, y),
        (row + 8 - 16 * z_high, y),
    )
    return core, x, y, peers


def greet(peers):
    barrier = pltpu.get_barrier_semaphore()
    for peer in peers:
        pl.semaphore_signal(barrier, inc=1, device_id=peer, device_id_type=MESH)
    pl.semaphore_wait(barrier, len(peers))


def total_rows(tensor):
    return jnp.sum(tensor.astype(jnp.float32), axis=(0, 1))


VMEM = pltpu.VMEM
F32 = jnp.float32
BF16 = jnp.bfloat16
HALF = 512
TILE = 256
R_EMBED, R_G1, R_B1, R_QB, R_VB, R_OB, R_G2, R_B2, R_DB, R_UB = 0, 1, 2, 3, 4, 5, 6, 7, 8, 9
QUERY_SCALE = 1.0 / math.sqrt(HEAD)


def dot(a, b):
    return lax.dot_general(a, b, (((1,), (0,)), ((), ())), preferred_element_type=F32)


def dot_t(a, b):
    return lax.dot_general(a, b, (((1,), (1,)), ((), ())), preferred_element_type=F32)


def t_dot(a, b):
    return lax.dot_general(a, b, (((0,), (0,)), ((), ())), preferred_element_type=F32)


def standard(values):
    center = values - jnp.mean(values, axis=-1, keepdims=True)
    scale_inv = lax.rsqrt(jnp.mean(center * center, axis=-1, keepdims=True) + norm_eps)
    return center * scale_inv, scale_inv


def masked_inputs(patch, first, marks, embed):
    at = first + lax.broadcasted_iota(jnp.int32, (patch.shape[0], 1), 0)
    flagged = jnp.max(jnp.where(at == marks, 1.0, 0.0), axis=-1, keepdims=True) > 0.5
    return flagged, jnp.where(flagged, embed, patch.astype(F32))


def project_tile(patch, first, marks_ref, table_ref, w_ref, qkv_ref, rows):
    unused, inputs = masked_inputs(patch, first, marks_ref[...], table_ref[R_EMBED : R_EMBED + 1, :])
    normed, unused = standard(inputs)
    hidden = (normed * table_ref[R_G1 : R_G1 + 1, :] + table_ref[R_B1 : R_B1 + 1, :]).astype(BF16)
    for part in range(6):
        cols = slice(part * 384, part * 384 + 384)
        project = dot(hidden, w_ref[:, cols])
        bias = slice((part % 2) * 384, (part % 2) * 384 + 384)
        if part < 2:
            project = (project + table_ref[R_QB : R_QB + 1, bias]) * QUERY_SCALE
        elif part >= 4:
            project = project + table_ref[R_VB : R_VB + 1, bias]
        qkv_ref[rows, cols] = project.astype(BF16)
    return hidden


def first_kernel(
    patch_h, wq_h, ids_ref, marks_ref, s0, s1, s2, s3, s4, s5, s6, s7, s8,
    qkv_h, h1_h, qkvx_h, att_h, lse_ref, qa_ref, ka_ref, qxa_ref, kxa_ref, table_ref,
    patch, patch_x, ids_x, wq, qkv, qkvx, h1, att, acc, tops, sums, insem, ssem, rsem, outsem,
):
    core, x, y, peers = places()
    partner = peers[1]
    lane = lax.broadcasted_iota(jnp.int32, (1, 128), 1)

    def rows_of(index):
        return pl.ds(pl.multiple_of(index * TILE, TILE), TILE)

    def lanes(start):
        return pl.ds(pl.multiple_of(start, 128), 128)

    near, far = rows_of(1 - y), rows_of(y)
    loads = [pltpu.make_async_copy(a, b, insem.at[i]) for i, (a, b) in enumerate(((patch_h, patch), (wq_h, wq)))]
    for load in loads:
        load.start()
    greet((partner,))
    loads[0].wait()
    sends = [
        pltpu.make_async_remote_copy(
            src_ref=src, dst_ref=dst, send_sem=ssem.at[i], recv_sem=rsem.at[i], device_id=partner, device_id_type=MESH
        )
        for i, (src, dst) in enumerate(
            (
                (ids_ref, ids_x),
                (patch.at[near, :], patch_x.at[near, :]),
                (patch.at[far, :], patch_x.at[far, :]),
            )
        )
    ]
    for send in sends:
        send.start()
    table_ref[...] = jnp.zeros_like(table_ref)
    for i, ref in enumerate((s0, s1, s2, s3, s4, s5, s6, s7, s8)):
        table_ref[i : i + 1, :] = ref[...].astype(F32).reshape(1, 768)

    def masks(ids, one_ref, mask_ref):
        hot = jnp.where(lax.broadcasted_iota(jnp.int32, (128, HALF), 0) == ids, 1.0, 0.0).T
        one_ref[...] = hot.astype(BF16)
        mask_ref[...] = jnp.where((lane >= 6) | (hot > 0.5), 0.0, neg_large).astype(BF16)

    masks(ids_ref[...], qa_ref, ka_ref)
    loads[1].wait()

    def own(i, carry):
        rows = rows_of(i)
        h1[rows, :] = project_tile(patch[rows, :], y * HALF + i * TILE, marks_ref, table_ref, wq, qkv, rows)
        return carry

    lax.fori_loop(0, 2, own, 0)
    stores = [
        pltpu.make_async_copy(a, b, outsem.at[i])
        for i, (a, b) in enumerate(((qkv, qkv_h), (h1, h1_h), (qkvx, qkvx_h), (att, att_h)))
    ]
    stores[0].start()
    stores[1].start()

    def absorb(groups, source, places_of, mask, first):
        def pair(p, carry):
            keys = jnp.concatenate([source[places_of, lanes(768 + p * 128)], mask], axis=1)
            values = source[places_of, lanes(1536 + p * 128)]
            for rows in groups:
                q = qkv[rows, lanes(p * 128)]
                qa = qa_ref[rows, :]
                top, total = tops[rows, :], sums[rows, :]
                if first:
                    top, total = jnp.where(p == 0, 0.0, top), jnp.where(p == 0, 0.0, total)
                else:
                    old = acc[rows, lanes(p * 128)]
                new_top, new_total = top, total
                kept = None
                for h in range(2):
                    mine = (lane // 64) == h
                    here = lane == 2 * p + h
                    scores = dot_t(jnp.concatenate([jnp.where(mine, q, 0), qa], axis=1), keys)
                    peak = jnp.max(scores, axis=-1, keepdims=True)
                    if not first:
                        before = jnp.sum(jnp.where(here, top, 0.0), axis=-1, keepdims=True)
                        peak = jnp.maximum(before, peak)
                        scale = jnp.exp(before - peak)
                    weights = jnp.exp(scores - peak)
                    number = jnp.sum(weights, axis=-1, keepdims=True)
                    out = dot(weights.astype(BF16), values)
                    if not first:
                        number = number + scale * jnp.sum(jnp.where(here, total, 0.0), axis=-1, keepdims=True)
                        out = out + scale * old
                    kept = out if h == 0 else jnp.where(mine, out, kept)
                    new_top = jnp.where(here, peak, new_top)
                    new_total = jnp.where(here, number, new_total)
                acc[rows, lanes(p * 128)] = kept
                tops[rows, :] = new_top
                sums[rows, :] = new_total
            return carry

        lax.fori_loop(0, 6, pair, 0)

    both = (slice(0, TILE), slice(TILE, HALF))
    absorb(both, qkv, slice(None), ka_ref[...], True)
    sends[0].wait_recv()
    masks(ids_x[...], qxa_ref, kxa_ref)
    sends[1].wait_recv()
    project_tile(patch_x[far, :], (1 - y) * HALF + y * TILE, marks_ref, table_ref, wq, qkvx, far)

    absorb(both, qkvx, far, kxa_ref[far, :], False)
    sends[2].wait_recv()
    project_tile(patch_x[near, :], (1 - y) * HALF + (1 - y) * TILE, marks_ref, table_ref, wq, qkvx, near)
    stores[2].start()
    absorb((near,), qkvx, near, kxa_ref[near, :], False)
    total = jnp.where(lane < 12, sums[...], 1.0)
    lse_ref[...] = (tops[...] + jnp.log(total)).T[:16, :]
    for p in range(6):
        for i in range(2):
            rows = slice(i * TILE, i * TILE + TILE)
            low, high = sums[rows, 2 * p : 2 * p + 1], sums[rows, 2 * p + 1 : 2 * p + 2]
            cols = slice(p * 128, p * 128 + 128)
            att[rows, cols] = (acc[rows, cols] / jnp.where(lane < 64, low, high)).astype(BF16)
    stores[3].start()
    for send in sends:
        send.wait_send()
    for store in stores:
        store.wait()


def first_half(patch, w_qkv, ids, marks, smalls):
    hbm = pl.BlockSpec(memory_space=pl.ANY)
    near = pl.BlockSpec(memory_space=pltpu.VMEM)
    dma = pltpu.SemaphoreType.DMA

    def low(*shape):
        return pltpu.VMEM(shape, BF16)

    return pl.pallas_call(
        first_kernel,
        out_shape=tuple(jax.ShapeDtypeStruct((HALF, n), BF16) for n in (2304, 768, 2304, 768))
        + (jax.ShapeDtypeStruct((16, HALF), F32),)
        + (jax.ShapeDtypeStruct((HALF, 128), BF16),) * 4
        + (jax.ShapeDtypeStruct((16, 768), F32),),
        in_specs=[hbm, hbm] + [near] * (2 + len(smalls)),
        out_specs=(hbm,) * 4 + (near,) * 6,
        scratch_shapes=[
            low(HALF, 768),
            low(HALF, 768),
            pltpu.VMEM((1, HALF), jnp.int32),
            low(768, 2304),
            low(HALF, 2304),
            low(HALF, 2304),
            low(HALF, 768),
            low(HALF, 768),
            pltpu.VMEM((HALF, 768), F32),
            pltpu.VMEM((HALF, 128), F32),
            pltpu.VMEM((HALF, 128), F32),
            dma((2,)),
            dma((3,)),
            dma((3,)),
            dma((4,)),
        ],
        compiler_params=pltpu.CompilerParams(collective_id=1, has_side_effects=True, vmem_limit_bytes=67043328),
    )(patch, w_qkv, ids, marks, *smalls)


ERFC_P = 0.3275911
ERFC_C = (
    0.1851102167482524,
    0.17993860771517878,
    0.21041948320823337,
    0.011498087426314028,
    0.47813345988158296,
    -0.4317659362057169,
    0.5111742647535956,
    -0.14450823957827402,
)


def gelu_and_slope(u):
    t = 1.0 / (1.0 + (ERFC_P * math.sqrt(0.5)) * jnp.abs(u))
    bell = jnp.exp(-0.5 * (u * u))
    series = ERFC_C[7]
    for c in ERFC_C[6::-1]:
        series = series * t + c
    tail = (0.5 * t) * series * bell
    phi = jnp.where(u < 0, tail, 1.0 - tail)
    return u * phi, phi + u * (bell * (1.0 / math.sqrt(2.0 * math.pi)))


CHUNKS = 24
SLOTS = 5
FF_TILE = 384
T_FORWARD = (0, 0, 1, 2, 3, 4, 5, 6)
EMIT_DOWN, EMIT_UP, EMIT_OUT, EMIT_QKV = (0, 2, 4, 6), (8, 10, 12, 14), (16,), (18, 19, 20, 21, 22, 23)
T_SECOND, T_ATTENDED = (7,), (8,)
T_SEND = (8, 9, 9, 10, 11, 11, 12, 13, 13, 14, 15, 15)
T_OWN = (8, 9, 10, 13, 14, 15)
T_FAR = (12, 13, 14, 16, 17, 18)
T_OUTPUT = (19, 19, 20, 20, 21, 21, 22, 22)
T_GRAD = (24, 24, 25)
T_FIRST = (26,)
T_VEC = 27


def halves_kernel(
    cot_h, wo_h, qkv_h, h1_h, patch_h, wq_h, qkvx_h, att_h, wu_h, wd_h,
    qa_ref, ka_ref, qxa_ref, kxa_ref, lse_ref, table_ref, marks_ref, ub_ref,
    parts_h, out_h, gp_h, vec_out,
    cot, wo, qkv, h1, patch, wq, qkvx, att, wu, wd,
    act, gu, mid, h2, acc, gb, do, dox, dqkv, dq, dk, dv, drow, dxrow, lsex_ref, ub,
    g, r1, r2, r3, r4, r5, done, v0, v1, v2,
    insem, wusem, wdsem, ssem, rsem, vs, vr, xs, xr, outsem, lastsem,
):
    core, x, y, peers = places()
    pair, yp, xp, zp1, zp2 = peers
    lane = lax.broadcasted_iota(jnp.int32, (1, 128), 1)
    inputs = (
        (cot_h, cot), (wo_h, wo), (qkv_h, qkv), (h1_h, h1), (patch_h, patch), (wq_h, wq),
        (qkvx_h, qkvx), (att_h, att),
    )
    COT, WO, QKV, H1, PATCH, WQ, QKVX, ATT = range(8)

    def lanes(start, size=128):
        return pl.ds(pl.multiple_of(start, 128), size)

    def part_of(n):
        return (n // 2 + 4 * (n % 2)) * (1 - n // 8) + (n - 8) * (n // 8)

    def load(i):
        return pltpu.make_async_copy(inputs[i][0], inputs[i][1], insem.at[i])

    def up_tile(n):
        return pltpu.make_async_copy(wu_h.at[:, lanes(part_of(n) * FF_TILE, FF_TILE)], wu.at[n % 2], wusem.at[n % 2])

    def down_tile(n):
        rows = pl.ds(pl.multiple_of(part_of(n) * FF_TILE, FF_TILE), FF_TILE)
        return pltpu.make_async_copy(wd_h.at[rows, :], wd.at[n % 2], wdsem.at[n % 2])

    for i in (PATCH, WO, ATT):
        load(i).start()
    for n in range(2):
        up_tile(n).start()
        down_tile(n).start()
    for i in (COT, QKV, QKVX, H1, WQ):
        load(i).start()
    greet(peers)

    def remote(src, dst, send, recv, dev):
        return pltpu.make_async_remote_copy(
            src_ref=src, dst_ref=dst, send_sem=send, recv_sem=recv, device_id=dev, device_id_type=MESH
        )

    def copy(s, c):
        src, dst, dev = (
            lambda: (g.at[c % SLOTS, 1 - core], r1.at[c], pair),
            lambda: (r1.at[c, 1 - y], r2.at[c], yp),
            lambda: (r2.at[c, 1 - x], r3.at[c], xp),
            lambda: (r3.at[c], r4.at[c], zp1),
            lambda: (r4.at[c], r5.at[c], zp2),
            lambda: (done.at[c, core, x], done.at[c, core, x], xp),
            lambda: (done.at[c, core], done.at[c, core], pair),
        )[s]()
        return remote(src, dst, ssem.at[s, c], rsem.at[s, c], dev)

    def part_out(c):
        return pltpu.make_async_copy(done.at[c], parts_h.at[c], outsem.at[c])

    def stage(s, c):
        if s > 0:
            copy(s - 1, c).wait_recv()
        if s == 1:
            r1[c] = r1[c] + g[c % SLOTS, core]
        elif s == 2:
            r2[c] = r2[c] + r1[c, y]
        elif s == 3:
            r3[c] = r3[c] + r2[c, x]
        elif s == 4:
            r4[c] = r4[c] + r3[c]
        elif s == 5:
            done[c, core, x] = r5[c] + r4[c]
        elif s == 7:
            copy(5, c).wait_send()
            copy(6, c).wait_send()
            part_out(c).start()
        if s < 7:
            copy(s, c).start()

    def vec_copy(s):
        src, dst, dev = (
            lambda: (v0, v1, pair),
            lambda: (v1.at[1 - y], v2.at[0], yp),
            lambda: (v2.at[0], v2.at[1], xp),
            lambda: (v2.at[1], v2.at[2], zp1),
            lambda: (v2.at[2], v2.at[3], zp2),
        )[s]()
        return remote(src, dst, vs.at[s], vr.at[s], dev)

    def vec_stage(s):
        if s > 0:
            vec_copy(s - 1).wait_recv()
        if s == 1:
            v1[...] = v1[...] + v0[...]
        elif s == 2:
            v2[0] = v2[0] + v1[y]
        elif s == 5:
            vec_out[...] = v2[3] + v2[2]
        elif s > 2:
            v2[s - 2] = v2[s - 2] + v2[s - 3]
        if s < 5:
            vec_copy(s).start()

    def far_copy(i):
        src, dst = ((lse_ref, lsex_ref), (drow, dxrow))[i]
        return remote(src, dst, xs.at[i], xr.at[i], yp)

    def grad_copy(n):
        rows, cols = pl.ds(pl.multiple_of((n % 2) * TILE, TILE), TILE), lanes((n // 2) * 128)
        return remote(do.at[rows, cols], dox.at[rows, cols], xs.at[2 + n], xr.at[2 + n], yp)

    def row(r):
        return table_ref[r : r + 1, :]

    def add_vec(r, value):
        for half in range(2):
            v0[half, r : r + 1, :] = v0[half, r : r + 1, :] + value[:, half * 384 : half * 384 + 384]

    def emit(left, right, c):
        number = right.shape[1] // 384
        for i in range(number):

            @pl.when(c + i >= SLOTS)
            def _():
                copy(0, c + i - SLOTS).wait_send()

        for half in range(2):
            block = t_dot(left(half), right).astype(BF16)
            for i in range(number):
                for other in range(4):
                    rows = slice(other * SUB, other * SUB + SUB)
                    g[(c + i) % SLOTS, other // 2, half, other % 2] = block[rows, i * 384 : i * 384 + 384]

    def enter():
        for tile in range(HALF // TILE):
            rows = slice(tile * TILE, tile * TILE + TILE)
            unused, values = masked_inputs(patch[rows, :], y * HALF + tile * TILE, marks_ref[...], row(R_EMBED))
            total = values + dot(att[rows, :], wo[...]) + row(R_OB)
            normed, unused = standard(total)
            mid[rows, :] = total
            h2[rows, :] = (normed * row(R_G2) + row(R_B2)).astype(BF16)

    def forward(n):
        k = part_of(n)
        cols = lanes(k * FF_TILE, FF_TILE)
        up_tile(n).wait()
        down_tile(n).wait()
        sums = jnp.zeros((1, FF_TILE), F32)
        for tile in range(HALF // TILE):
            rows = slice(tile * TILE, tile * TILE + TILE)
            value, slope = gelu_and_slope(dot(h2[rows, :], wu[n % 2]) + ub[:, cols])
            act[rows, cols] = value.astype(BF16)
            low = (dot_t(cot[rows, :], wd[n % 2]) * slope).astype(BF16)
            gu[rows, cols] = low
            sums = sums + jnp.sum(low.astype(F32), axis=0, keepdims=True)
            acc[rows, :] = acc[rows, :] + dot_t(low, wu[n % 2])
        v0[k // 4, pl.ds(9 + k % 4, 1), :] = sums
        down_tile(n + 2).start()

        @pl.when(n + 2 < 8)
        def _():
            up_tile(n + 2).start()

    def second_norm():
        def tile(i, carry):
            rows = pl.ds(pl.multiple_of(i * 128, 128), 128)
            normed, inverse = standard(mid[rows, :])
            grad = acc[rows, :]
            cotangent = cot[rows, :].astype(F32)
            add_vec(6, jnp.sum(grad * normed, axis=0, keepdims=True))
            add_vec(7, jnp.sum(grad, axis=0, keepdims=True))
            add_vec(8, jnp.sum(cotangent, axis=0, keepdims=True))
            total = cotangent + norm_back(grad, normed, inverse, row(R_G2))
            acc[rows, :] = total
            low = total.astype(BF16)
            gb[rows, :] = low
            add_vec(5, jnp.sum(low.astype(F32), axis=0, keepdims=True))
            return carry

        lax.fori_loop(0, 4, tile, 0)

    def grad_attended():
        for tile in range(2):
            rows = slice(tile * 256, tile * 256 + 256)
            do[rows, :] = dot_t(gb[rows, :], wo[...]).astype(BF16)
        for tile in range(4):
            rows = slice(tile * 128, tile * 128 + 128)
            columns = jnp.zeros((128, 128), F32)
            for p in range(6):
                cols = slice(p * 128, p * 128 + 128)
                product = do[rows, cols].astype(F32) * att[rows, cols].astype(F32)
                for h in range(2):
                    total = jnp.sum(jnp.where((lane // 64) == h, product, 0.0), axis=1, keepdims=True)
                    columns = jnp.where(lane == 2 * p + h, total, columns)
            drow[:, rows] = columns.T[:16, :]
        far_copy(1).start()

    def piece(keys, key_mask, values, query, query_mask, grad, lse, delta):
        scores = dot_t(jnp.concatenate([keys, key_mask], axis=1), jnp.concatenate([query, query_mask], axis=1))
        probs = jnp.exp(scores - lse)
        grad_scores = probs * (dot_t(values, grad) - delta)
        return probs.astype(BF16), grad_scores.astype(BF16)

    def own_pair(p):
        slot = p % 3

        def head(h, carry):
            mine = (lane // 64) == h
            stat = pl.ds(2 * p + h, 1)
            query = jnp.where(mine, qkv[:, lanes(p * 128)], 0)
            grad = jnp.where(mine, do[:, lanes(p * 128)], 0)
            for tile in range(2):
                rows = slice(tile * 256, tile * 256 + 256)
                keys = qkv[rows, lanes(768 + p * 128)]
                probs, scores = piece(
                    keys, ka_ref[rows, :], qkv[rows, lanes(1536 + p * 128)], query, qa_ref[...], grad,
                    lse_ref[stat, :], drow[stat, :],
                )
                new = dot(scores, query)
                dk[slot, rows, :] = jnp.where(h == 0, new, dk[slot, rows, :] + new)
                new = dot(probs, grad)
                dv[slot, rows, :] = jnp.where(h == 0, new, dv[slot, rows, :] + new)
                new = t_dot(scores, jnp.where(mine, keys, 0))
                dq[slot] = jnp.where((h == 0) & (tile == 0), new, dq[slot] + new)
            return carry

        lax.fori_loop(0, 2, head, 0)

    def far_pair(p):
        slot = p % 3
        grad_copy(2 * p).wait_recv()
        grad_copy(2 * p + 1).wait_recv()
        near, far = pl.multiple_of((1 - y) * 256, 256), pl.multiple_of(y * 256, 256)

        def head(h, carry):
            mine = (lane // 64) == h
            stat = pl.ds(2 * p + h, 1)
            for first, start, size in ((far, 0, 512), (near, near, 256)):
                rows, others = pl.ds(first, 256), pl.ds(start, size)
                query = jnp.where(mine, qkv[others, lanes(p * 128)], 0)
                grad = jnp.where(mine, do[others, lanes(p * 128)], 0)
                keys = qkvx[rows, lanes(768 + p * 128)]
                probs, scores = piece(
                    keys, kxa_ref[rows, :], qkvx[rows, lanes(1536 + p * 128)], query, qa_ref[others, :], grad,
                    lse_ref[stat, others], drow[stat, others],
                )
                dq[slot, others, :] = dq[slot, others, :] + t_dot(scores, jnp.where(mine, keys, 0))
            for first, start, size in ((near, 0, 512), (far, far, 256)):
                rows, others = pl.ds(first, 256), pl.ds(start, size)
                query = jnp.where(mine, qkvx[others, lanes(p * 128)], 0)
                grad = jnp.where(mine, dox[others, lanes(p * 128)], 0)
                probs, scores = piece(
                    qkv[rows, lanes(768 + p * 128)], ka_ref[rows, :], qkv[rows, lanes(1536 + p * 128)],
                    query, qxa_ref[others, :], grad, lsex_ref[stat, others], dxrow[stat, others],
                )
                dk[slot, rows, :] = dk[slot, rows, :] + dot(scores, query)
                dv[slot, rows, :] = dv[slot, rows, :] + dot(probs, grad)
            return carry

        lax.fori_loop(0, 2, head, 0)
        dqkv[:, lanes(p * 128)] = (dq[slot].astype(BF16).astype(F32) * QUERY_SCALE).astype(BF16)
        dqkv[:, lanes(768 + p * 128)] = dk[slot].astype(BF16)
        dqkv[:, lanes(1536 + p * 128)] = dv[slot].astype(BF16)

    def output_tile(i):
        n = i + 8
        down_tile(n).wait()
        for tile in range(2):
            rows = slice(tile * 256, tile * 256 + 256)
            mid[rows, :] = mid[rows, :] + dot(act[rows, lanes(i * FF_TILE, FF_TILE)], wd[n % 2])

        @pl.when(n + 2 < 16)
        def _():
            down_tile(n + 2).start()

    def store_output():
        for tile in range(4):
            rows = slice(tile * 128, tile * 128 + 128)
            gb[rows, :] = (mid[rows, :] + row(R_DB)).astype(BF16)
        pltpu.make_async_copy(gb, out_h, lastsem.at[0]).start()

    def grad_first(part):
        for tile in range(2):
            rows = slice(tile * 256, tile * 256 + 256)
            new = dot_t(dqkv[rows, lanes(part * 768, 768)], wq[:, lanes(part * 768, 768)])
            mid[rows, :] = jnp.where(part == 0, new, mid[rows, :] + new)

    def first_norm():
        def tile(i, carry):
            rows = pl.ds(pl.multiple_of(i * 128, 128), 128)
            flagged, values = masked_inputs(patch[rows, :], y * HALF + i * 128, marks_ref[...], row(R_EMBED))
            normed, inverse = standard(values)
            grad = mid[rows, :]
            add_vec(1, jnp.sum(grad * normed, axis=0, keepdims=True))
            add_vec(2, jnp.sum(grad, axis=0, keepdims=True))
            total = acc[rows, :] + norm_back(grad, normed, inverse, row(R_G1))
            add_vec(0, jnp.sum(jnp.where(flagged, total, 0.0), axis=0, keepdims=True))
            att[rows, :] = jnp.where(flagged, 0.0, total).astype(BF16)
            add_vec(3, jnp.sum(dqkv[rows, :768].astype(F32), axis=0, keepdims=True))
            add_vec(4, jnp.sum(dqkv[rows, 1536:].astype(F32), axis=0, keepdims=True))
            return carry

        lax.fori_loop(0, 4, tile, 0)
        pltpu.make_async_copy(att, gp_h, lastsem.at[1]).start()

    far_copy(0).start()
    ub[...] = ub_ref[...].astype(F32).reshape(1, 3072)
    acc[...] = jnp.zeros_like(acc)
    v0[...] = jnp.zeros_like(v0)
    for i in (PATCH, WO, ATT):
        load(i).wait()
    enter()
    load(COT).wait()

    def step(t, carry):
        def run(times, body):
            def before(now):
                return sum(jnp.where(now > at, 1, 0) for at in times)

            def one(n, inner):
                body(n)
                return inner

            lax.fori_loop(before(t), before(t + 1), one, 0)

        def need(at, *names):
            @pl.when(t == at)
            def _():
                for i in names:
                    load(i).wait()

        for s in range(2, 8):
            c = t - LAGS[s]

            @pl.when((c >= 0) & (c < CHUNKS))
            def _():
                stage(s, c)

        need(2, QKV, QKVX, H1, WQ)
        run(T_FORWARD, forward)
        run(
            EMIT_DOWN,
            lambda n: emit(lambda half: act[:, lanes(half * 1536 + n * 384, 384)], cot[...], 2 * n),
        )
        run(
            EMIT_UP,
            lambda n: emit(lambda half: h2[:, half * 384 : half * 384 + 384], gu[:, lanes(n * 768, 768)], 8 + 2 * n),
        )
        run(EMIT_OUT, lambda n: emit(lambda half: att[:, half * 384 : half * 384 + 384], gb[...], 16))

        def emit_qkv(p):
            right = jnp.concatenate([dqkv[:, lanes(part * 768 + p * 128)] for part in range(3)], axis=1)
            emit(lambda half: h1[:, half * 384 : half * 384 + 384], right, 18 + p)

        run(EMIT_QKV, emit_qkv)
        @pl.when(t < CHUNKS)
        def _():
            stage(0, t)

        @pl.when((t >= LAGS[1]) & (t < CHUNKS + LAGS[1]))
        def _():
            stage(1, t - LAGS[1])


        run(T_SECOND, lambda n: second_norm())
        run(T_ATTENDED, lambda n: grad_attended())
        run(T_SEND, lambda n: grad_copy(n).start())
        run(T_OWN, own_pair)

        @pl.when(t == T_FAR[0])
        def _():
            far_copy(0).wait_recv()
            far_copy(1).wait_recv()

        run(T_FAR, far_pair)
        run(T_OUTPUT, output_tile)

        @pl.when(t == T_OUTPUT[-1])
        def _():
            store_output()

        run(T_GRAD, grad_first)
        run(T_FIRST, lambda n: first_norm())

        for s in range(6):

            @pl.when(t == T_VEC + s)
            def _():
                vec_stage(s)

        return carry

    lax.fori_loop(0, max(T_VEC + 6, CHUNKS + LAGS[7]), step, 0)

    def drain(c, carry):
        for s in range(1, 5):
            copy(s, c).wait_send()
        part_out(c).wait()
        return carry

    lax.fori_loop(0, CHUNKS, drain, 0)
    for c in range(CHUNKS - SLOTS, CHUNKS):
        copy(0, c).wait_send()
    for s in range(5):
        vec_copy(s).wait_send()
    for i in range(2):
        far_copy(i).wait_send()

    def drain_grad(n, carry):
        grad_copy(n).wait_send()
        return carry

    lax.fori_loop(0, 12, drain_grad, 0)
    pltpu.make_async_copy(gb, out_h, lastsem.at[0]).wait()
    pltpu.make_async_copy(att, gp_h, lastsem.at[1]).wait()


def backward(big, weights, small):
    hbm = pl.BlockSpec(memory_space=pl.ANY)
    near = pl.BlockSpec(memory_space=pltpu.VMEM)

    def low(*shape):
        return pltpu.VMEM(shape, BF16)

    def full(*shape):
        return pltpu.VMEM(shape, F32)

    dma = pltpu.SemaphoreType.DMA
    held = [pltpu.VMEM(a.shape, a.dtype) for a in big]
    return pl.pallas_call(
        halves_kernel,
        out_shape=(
            jax.ShapeDtypeStruct((CHUNKS, 2, 2, SUB, COLS), BF16),
            jax.ShapeDtypeStruct((HALF, 768), BF16),
            jax.ShapeDtypeStruct((HALF, 768), BF16),
            jax.ShapeDtypeStruct((16, COLS), F32),
        ),
        in_specs=[hbm] * (len(big) + 2) + [near] * len(small),
        out_specs=(hbm, hbm, hbm, near),
        scratch_shapes=held
        + [
            low(2, 768, FF_TILE),
            low(2, FF_TILE, 768),
            low(HALF, 3072),
            low(HALF, 3072),
            full(HALF, 768),
            low(HALF, 768),
            full(HALF, 768),
            low(HALF, 768),
            low(HALF, 768),
            low(HALF, 768),
            low(HALF, 2304),
            full(3, HALF, 128),
            full(3, HALF, 128),
            full(3, HALF, 128),
            full(16, HALF),
            full(16, HALF),
            full(16, HALF),
            full(1, 3072),
            low(SLOTS, 2, 2, 2, SUB, COLS),
            low(CHUNKS, 2, 2, SUB, COLS),
            low(CHUNKS, 2, SUB, COLS),
            low(CHUNKS, SUB, COLS),
            low(CHUNKS, SUB, COLS),
            low(CHUNKS, SUB, COLS),
            low(CHUNKS, 2, 2, SUB, COLS),
            full(2, 16, COLS),
            full(2, 16, COLS),
            full(4, 16, COLS),
            dma((8,)),
            dma((2,)),
            dma((2,)),
            dma((7, CHUNKS)),
            dma((7, CHUNKS)),
            dma((5,)),
            dma((5,)),
            dma((14,)),
            dma((14,)),
            dma((CHUNKS,)),
            dma((2,)),
        ],
        compiler_params=pltpu.CompilerParams(
            collective_id=0, has_side_effects=True, vmem_limit_bytes=67043328
        ),
    )(*big, *weights, *small)


def widen_kernel(four_ref, qkv_ref, down_ref, up_ref, out_ref, proj_ref):
    i = pl.program_id(0)

    @pl.when(i < 2)
    def _():
        for c in range(4):
            rows = slice(c // 2 * 384, c // 2 * 384 + 384)
            down_ref[rows, c % 2 * 384 : c % 2 * 384 + 384] = four_ref[c].astype(F32)

    for first, last, ref in ((2, 4, up_ref), (4, 5, out_ref)):

        @pl.when((i >= first) & (i < last))
        def _():
            for c in range(ref.shape[1] // 384):
                ref[:, c * 384 : c * 384 + 384] = four_ref[c].astype(F32)

    @pl.when(i >= 5)
    def _():
        for p in range(6):
            proj_ref[:, p * 128 : p * 128 + 128] = qkv_ref[p].astype(F32)


def widen(parts):
    parts = parts.reshape(CHUNKS, 384, COLS)
    return pl.pallas_call(
        widen_kernel,
        grid=(8,),
        out_shape=(
            jax.ShapeDtypeStruct((1536, 768), F32),
            jax.ShapeDtypeStruct((384, 3072), F32),
            jax.ShapeDtypeStruct((384, 768), F32),
            jax.ShapeDtypeStruct((384, 2304), F32),
        ),
        in_specs=[
            pl.BlockSpec((4, 384, COLS), lambda i: (jnp.minimum(i, 4), 0, 0)),
            pl.BlockSpec((6, 384, 128), lambda i: (3, 0, jnp.maximum(i - 5, 0))),
        ],
        out_specs=(
            pl.BlockSpec((768, 768), lambda i: (jnp.minimum(i, 1), 0)),
            pl.BlockSpec((384, 1536), lambda i: (0, jnp.clip(i - 2, 0, 1))),
            pl.BlockSpec((384, 768), lambda i: (0, 0)),
            pl.BlockSpec((384, 768), lambda i: (0, jnp.maximum(i - 5, 0))),
        ),
    )(parts, parts)


def block_shards(
    patches,
    segment_ids,
    mask_positions,
    mask_embed,
    norm1_gain,
    norm1_bias,
    w_qkv,
    query_bias,
    value_bias,
    w_out,
    out_bias,
    norm2_gain,
    norm2_bias,
    w_up,
    up_bias,
    w_down,
    down_bias,
    cotangent,
):
    patch = patches[0]
    cot = cotangent[0]
    qkv, hidden1, qkv_x, attended, lse, qa, ka, qxa, kxa, table = first_half(
        patch,
        w_qkv,
        segment_ids,
        mask_positions,
        (mask_embed, norm1_gain, norm1_bias, query_bias, value_bias, out_bias, norm2_gain, norm2_bias, down_bias),
    )
    parts, output, grad_patches, v = backward(
        (cot, w_out, qkv, hidden1, patch, w_qkv, qkv_x, attended),
        (w_up, w_down),
        (qa, ka, qxa, kxa, lse, table, mask_positions, up_bias),
    )
    grad_down, grad_up, grad_out, grad_qkv = widen(parts)
    return (
        output[None],
        grad_patches[None],
        v[0],
        v[1],
        v[2],
        grad_qkv,
        v[3],
        v[4],
        grad_out,
        v[5],
        v[6],
        v[7],
        grad_up,
        v[9:13].reshape(-1),
        grad_down,
        v[8],
    )


def shards(
    patches,
    segment_ids,
    mask_positions,
    mask_embed,
    norm1_gain,
    norm1_bias,
    w_qkv,
    query_bias,
    value_bias,
    w_out,
    out_bias,
    norm2_gain,
    norm2_bias,
    w_up,
    up_bias,
    w_down,
    down_bias,
    cotangent,
):
    rows_n, time_n, width = patches.shape
    query_scale = 1.0 / math.sqrt(HEAD)
    gain_one = norm1_gain.astype(jnp.float32)
    gain_two = norm2_gain.astype(jnp.float32)
    offset = lax.axis_index("tm") * time_n
    places = offset + lax.broadcasted_iota(jnp.int32, (rows_n, time_n, 1), 1)
    masked = jnp.any(places == mask_positions[:, None, :], axis=-1)[..., None]
    inputs = jnp.where(
        masked, mask_embed.astype(jnp.float32)[None, None, :], patches.astype(jnp.float32)
    )
    normed1, inverse1 = normalize(inputs)
    hidden1 = (normed1 * gain_one + norm1_bias.astype(jnp.float32)).astype(jnp.bfloat16)
    project = jnp.einsum("rtd,de->rte", hidden1, w_qkv, preferred_element_type=jnp.float32)
    queries = ((project[..., :width] + query_bias.astype(jnp.float32)) * query_scale).astype(
        jnp.bfloat16
    )
    keys_own = project[..., width : 2 * width].astype(jnp.bfloat16)
    values_own = (project[..., 2 * width :] + value_bias.astype(jnp.float32)).astype(jnp.bfloat16)
    keys_all, values_all, segments_all = (
        lax.all_gather(keys_own, "tm", axis=1, tiled=True),
        lax.all_gather(values_own, "tm", axis=1, tiled=True),
        lax.all_gather(segment_ids, "tm", axis=1, tiled=True),
    )
    same = segment_ids[:, :, None] == segments_all[:, None, :]
    query_heads = split_heads(queries)
    head_outputs, log_totals = attend_forward(
        query_heads, split_heads(keys_all), split_heads(values_all), same
    )
    attended = join_heads(head_outputs).astype(jnp.bfloat16)
    middle = (
        inputs
        + jnp.einsum("rtd,de->rte", attended, w_out, preferred_element_type=jnp.float32)
        + out_bias.astype(jnp.float32)
    )
    normed2, inverse2 = normalize(middle)
    hidden2 = (normed2 * gain_two + norm2_bias.astype(jnp.float32)).astype(jnp.bfloat16)
    upper = jnp.einsum(
        "rtd,df->rtf", hidden2, w_up, preferred_element_type=jnp.float32
    ) + up_bias.astype(jnp.float32)
    activated = jax.nn.gelu(upper, approximate=False).astype(jnp.bfloat16)
    result = (
        middle
        + jnp.einsum("rtf,fd->rtd", activated, w_down, preferred_element_type=jnp.float32)
        + down_bias.astype(jnp.float32)
    )
    output = result.astype(jnp.bfloat16)
    grad_result = cotangent.astype(jnp.float32)
    grad_w_down = jnp.einsum(
        "rtf,rtd->fd", activated, cotangent, preferred_element_type=jnp.float32
    )
    grad_down_bias = total_rows(grad_result)
    grad_activated = jnp.einsum(
        "rtd,fd->rtf", cotangent, w_down, preferred_element_type=jnp.float32
    )
    unused, gelu_pull = jax.vjp(partial(jax.nn.gelu, approximate=False), upper)
    grad_upper = gelu_pull(grad_activated)[0].astype(jnp.bfloat16)
    grad_w_up = jnp.einsum("rtd,rtf->df", hidden2, grad_upper, preferred_element_type=jnp.float32)
    grad_up_bias = total_rows(grad_upper)
    grad_hidden2 = jnp.einsum("rtf,df->rtd", grad_upper, w_up, preferred_element_type=jnp.float32)
    grad_gain_two = total_rows(grad_hidden2 * normed2)
    grad_bias_two = total_rows(grad_hidden2)
    grad_middle = grad_result + norm_back(grad_hidden2, normed2, inverse2, gain_two)
    mlp_vectors = jnp.stack([grad_gain_two, grad_bias_two, grad_down_bias], axis=1)
    grad_branch = grad_middle.astype(jnp.bfloat16)
    grad_w_out = jnp.einsum(
        "rtd,rte->de", attended, grad_branch, preferred_element_type=jnp.float32
    )
    grad_out_bias = total_rows(grad_branch)
    grad_attended = jnp.einsum(
        "rte,de->rtd", grad_branch, w_out, preferred_element_type=jnp.float32
    ).astype(jnp.bfloat16)
    keys_back, values_back, segments_back = (
        lax.all_gather(keys_own, "tm", axis=1, tiled=True),
        lax.all_gather(values_own, "tm", axis=1, tiled=True),
        lax.all_gather(segment_ids, "tm", axis=1, tiled=True),
    )
    same_back = segment_ids[:, :, None] == segments_back[:, None, :]
    grad_query_h, grad_keys_h, grad_values_h = attend_backward(
        query_heads,
        split_heads(keys_back),
        split_heads(values_back),
        split_heads(grad_attended),
        log_totals,
        same_back,
    )
    grad_keys, grad_values = (
        lax.psum_scatter(
            join_heads(grad_keys_h).astype(jnp.bfloat16), "tm", scatter_dimension=1, tiled=True
        ).astype(jnp.float32),
        lax.psum_scatter(
            join_heads(grad_values_h).astype(jnp.bfloat16), "tm", scatter_dimension=1, tiled=True
        ).astype(jnp.float32),
    )
    grad_queries = join_heads(grad_query_h).astype(jnp.bfloat16)
    grad_project = jnp.concatenate(
        [
            (grad_queries.astype(jnp.float32) * query_scale).astype(jnp.bfloat16),
            grad_keys.astype(jnp.bfloat16),
            grad_values.astype(jnp.bfloat16),
        ],
        axis=-1,
    )
    grad_w_qkv = jnp.einsum(
        "rtd,rte->de", hidden1, grad_project, preferred_element_type=jnp.float32
    )
    grad_query_bias = total_rows(grad_project[..., :width])
    grad_value_bias = total_rows(grad_project[..., 2 * width :])
    grad_hidden1 = jnp.einsum(
        "rte,de->rtd", grad_project, w_qkv, preferred_element_type=jnp.float32
    )
    grad_gain_one = total_rows(grad_hidden1 * normed1)
    grad_bias_one = total_rows(grad_hidden1)
    grad_inputs = grad_middle + norm_back(grad_hidden1, normed1, inverse1, gain_one)
    grad_mask = total_rows(jnp.where(masked, grad_inputs, 0.0))
    grad_patches = jnp.where(masked, 0.0, grad_inputs).astype(jnp.bfloat16)
    attn_vectors = jnp.stack(
        [grad_mask, grad_gain_one, grad_bias_one, grad_query_bias, grad_value_bias, grad_out_bias],
        axis=1,
    )
    every_part = (
        lax.psum_scatter(
            grad_w_qkv.astype(jnp.bfloat16), "tm", scatter_dimension=0, tiled=True
        ).astype(jnp.float32),
        lax.psum_scatter(
            grad_w_out.astype(jnp.bfloat16), "tm", scatter_dimension=0, tiled=True
        ).astype(jnp.float32),
        lax.psum_scatter(
            attn_vectors.astype(jnp.bfloat16), "tm", scatter_dimension=0, tiled=True
        ).astype(jnp.float32),
        lax.psum_scatter(
            grad_w_up.astype(jnp.bfloat16), "tm", scatter_dimension=0, tiled=True
        ).astype(jnp.float32),
        lax.psum_scatter(
            grad_w_down.astype(jnp.bfloat16), "tm", scatter_dimension=0, tiled=True
        ).astype(jnp.float32),
        lax.psum_scatter(
            mlp_vectors.astype(jnp.bfloat16), "tm", scatter_dimension=0, tiled=True
        ).astype(jnp.float32),
        lax.psum_scatter(
            grad_up_bias.astype(jnp.bfloat16), "tm", scatter_dimension=0, tiled=True
        ).astype(jnp.float32),
    )
    every_part = (
        lax.psum(every_part[0].astype(jnp.bfloat16), "rows").astype(jnp.float32),
        lax.psum(every_part[1].astype(jnp.bfloat16), "rows").astype(jnp.float32),
        lax.psum(every_part[2].astype(jnp.bfloat16), "rows").astype(jnp.float32),
        lax.psum(every_part[3].astype(jnp.bfloat16), "rows").astype(jnp.float32),
        lax.psum(every_part[4].astype(jnp.bfloat16), "rows").astype(jnp.float32),
        lax.psum(every_part[5].astype(jnp.bfloat16), "rows").astype(jnp.float32),
        lax.psum(every_part[6].astype(jnp.bfloat16), "rows").astype(jnp.float32),
    )
    summed_qkv, summed_out, summed_attn, summed_up, summed_down, summed_mlp, summed_up_bias = (
        every_part
    )
    return (
        output,
        grad_patches,
        summed_attn[:, 0],
        summed_attn[:, 1],
        summed_attn[:, 2],
        summed_qkv,
        summed_attn[:, 3],
        summed_attn[:, 4],
        summed_out,
        summed_attn[:, 5],
        summed_mlp[:, 0],
        summed_mlp[:, 1],
        summed_up,
        summed_up_bias,
        summed_down,
        summed_mlp[:, 2],
    )


def solution(mesh):
    placed = (
        P("rows", "tm", None),
        P("rows", "tm"),
        P("rows", None),
        P(),
        P(),
        P(),
        P(),
        P(),
        P(),
        P(),
        P(),
        P(),
        P(),
        P(),
        P(),
        P(),
        P(),
        P("rows", "tm", None),
    )
    return jax.shard_map(
        block_shards if dict(mesh.shape) == {"rows": 16, "tm": 2} else shards,
        mesh=mesh,
        in_specs=placed,
        out_specs=(
            P("rows", "tm", None),
            P("rows", "tm", None),
            P("tm"),
            P("tm"),
            P("tm"),
            P("tm", None),
            P("tm"),
            P("tm"),
            P("tm", None),
            P("tm"),
            P("tm"),
            P("tm"),
            P("tm", None),
            P("tm"),
            P("tm", None),
            P("tm"),
        ),
        check_vma=False,
    )
```

```python
from functools import partial
import math

import jax
import jax.numpy as jnp
from jax import lax
from jax.experimental import pallas as pl
from jax.experimental.pallas import tpu as pltpu
from jax.sharding import PartitionSpec as P

HEADS = 12
HEAD = 64


norm_eps = 1e-06
neg_large = -1e30


def normalize(values):
    center = values - jnp.mean(values, axis=-1, keepdims=True)
    scale_inv = lax.rsqrt(jnp.mean(center * center, axis=-1, keepdims=True) + norm_eps)
    return (center * scale_inv, scale_inv)


def norm_back(grad_out, normed, scale_inv, norm_gain):
    grad_normed = grad_out * norm_gain
    mean_one = jnp.mean(grad_normed, axis=-1, keepdims=True)
    mean_two = jnp.mean(grad_normed * normed, axis=-1, keepdims=True)
    return scale_inv * (grad_normed - mean_one - normed * mean_two)


def split_heads(tensor):
    rows_n, length, width = tensor.shape
    return tensor.reshape(rows_n, length, HEADS, width // HEADS).transpose(2, 0, 1, 3)


def join_heads(tensor):
    heads_n, rows_n, length, size = tensor.shape
    return tensor.transpose(1, 2, 0, 3).reshape(rows_n, length, heads_n * size)


def head_scores(query, keys_h, same):
    scores = jnp.einsum("rqd,rkd->rqk", query, keys_h, preferred_element_type=jnp.float32)
    return jnp.where(same, scores, neg_large)


def attend_forward(query_heads, key_heads, value_heads, same):

    def one_head(operands):
        query, keys_h, values_h = operands
        scores = head_scores(query, keys_h, same)
        peak = jnp.max(scores, axis=-1, keepdims=True)
        total = jnp.sum(jnp.exp(scores - peak), axis=-1, keepdims=True)
        log_total = peak + jnp.log(total)
        weights = jnp.exp(scores - log_total).astype(jnp.bfloat16)
        result = jnp.einsum("rqk,rkd->rqd", weights, values_h, preferred_element_type=jnp.float32)
        return (result, log_total[..., 0])

    return lax.map(one_head, (query_heads, key_heads, value_heads))


def attend_backward(query_heads, key_heads, value_heads, grad_heads, log_totals, same):

    def one_head(operands):
        query, keys_h, values_h, grad_out, log_total = operands
        scores = head_scores(query, keys_h, same)
        probs_full = jnp.exp(scores - log_total[..., None])
        probs_low = probs_full.astype(jnp.bfloat16)
        grad_values = jnp.einsum(
            "rqk,rqd->rkd", probs_low, grad_out, preferred_element_type=jnp.float32
        )
        grad_probs = jnp.einsum(
            "rqd,rkd->rqk", grad_out, values_h, preferred_element_type=jnp.float32
        )
        delta = jnp.sum(grad_probs * probs_full, axis=-1, keepdims=True)
        grad_scores = (probs_full * (grad_probs - delta)).astype(jnp.bfloat16)
        grad_query = jnp.einsum(
            "rqk,rkd->rqd", grad_scores, keys_h, preferred_element_type=jnp.float32
        )
        grad_keys = jnp.einsum(
            "rqk,rqd->rkd", grad_scores, query, preferred_element_type=jnp.float32
        )
        return (grad_query, grad_keys, grad_values)

    return lax.map(one_head, (query_heads, key_heads, value_heads, grad_heads, log_totals))


MESH = pl.DeviceIdType.MESH
SUB = 96
COLS = 384
LAGS = (0, 1, 4, 5, 6, 8, 9, 10)


def places():
    row = lax.axis_index("rows")
    y = lax.axis_index("tm")
    core = row % 2
    x = (row // 2) % 2
    z_low = (row // 4) % 2
    z_high = row // 8
    peers = (
        (row + 1 - 2 * core, y),
        (row, 1 - y),
        (row + 2 - 4 * x, y),
        (row + 4 - 8 * z_low, y),
        (row + 8 - 16 * z_high, y),
    )
    return core, x, y, peers


def greet(peers):
    barrier = pltpu.get_barrier_semaphore()
    for peer in peers:
        pl.semaphore_signal(barrier, inc=1, device_id=peer, device_id_type=MESH)
    pl.semaphore_wait(barrier, len(peers))


def total_rows(tensor):
    return jnp.sum(tensor.astype(jnp.float32), axis=(0, 1))


VMEM = pltpu.VMEM
F32 = jnp.float32
BF16 = jnp.bfloat16
HALF = 512
TILE = 256
R_EMBED, R_G1, R_B1, R_QB, R_VB, R_OB, R_G2, R_B2, R_DB, R_UB = 0, 1, 2, 3, 4, 5, 6, 7, 8, 9
QUERY_SCALE = 1.0 / math.sqrt(HEAD)


def dot(a, b):
    return lax.dot_general(a, b, (((1,), (0,)), ((), ())), preferred_element_type=F32)


def dot_t(a, b):
    return lax.dot_general(a, b, (((1,), (1,)), ((), ())), preferred_element_type=F32)


def t_dot(a, b):
    return lax.dot_general(a, b, (((0,), (0,)), ((), ())), preferred_element_type=F32)


def standard(values):
    center = values - jnp.mean(values, axis=-1, keepdims=True)
    scale_inv = lax.rsqrt(jnp.mean(center * center, axis=-1, keepdims=True) + norm_eps)
    return center * scale_inv, scale_inv


def masked_inputs(patch, first, marks, embed):
    at = first + lax.broadcasted_iota(jnp.int32, (patch.shape[0], 1), 0)
    flagged = jnp.max(jnp.where(at == marks, 1.0, 0.0), axis=-1, keepdims=True) > 0.5
    return flagged, jnp.where(flagged, embed, patch.astype(F32))


def project_tile(patch, first, marks_ref, table_ref, w_ref, qkv_ref, rows):
    unused, inputs = masked_inputs(patch, first, marks_ref[...], table_ref[R_EMBED : R_EMBED + 1, :])
    normed, unused = standard(inputs)
    hidden = (normed * table_ref[R_G1 : R_G1 + 1, :] + table_ref[R_B1 : R_B1 + 1, :]).astype(BF16)
    for part in range(6):
        cols = slice(part * 384, part * 384 + 384)
        project = dot(hidden, w_ref[:, cols])
        bias = slice((part % 2) * 384, (part % 2) * 384 + 384)
        if part < 2:
            project = (project + table_ref[R_QB : R_QB + 1, bias]) * QUERY_SCALE
        elif part >= 4:
            project = project + table_ref[R_VB : R_VB + 1, bias]
        qkv_ref[rows, cols] = project.astype(BF16)
    return hidden


def first_kernel(
    patch_h, wq_h, ids_ref, marks_ref, s0, s1, s2, s3, s4, s5, s6, s7, s8,
    qkv_h, h1_h, qkvx_h, att_h, lse_ref, qa_ref, ka_ref, qxa_ref, kxa_ref, table_ref,
    patch, patch_x, ids_x, wq, qkv, qkvx, h1, att, acc, tops, sums, insem, ssem, rsem, outsem,
):
    core, x, y, peers = places()
    partner = peers[1]
    lane = lax.broadcasted_iota(jnp.int32, (1, 128), 1)

    def rows_of(index):
        return pl.ds(pl.multiple_of(index * TILE, TILE), TILE)

    def lanes(start):
        return pl.ds(pl.multiple_of(start, 128), 128)

    near, far = rows_of(1 - y), rows_of(y)
    loads = [pltpu.make_async_copy(a, b, insem.at[i]) for i, (a, b) in enumerate(((patch_h, patch), (wq_h, wq)))]
    for load in loads:
        load.start()
    greet((partner,))
    loads[0].wait()
    sends = [
        pltpu.make_async_remote_copy(
            src_ref=src, dst_ref=dst, send_sem=ssem.at[i], recv_sem=rsem.at[i], device_id=partner, device_id_type=MESH
        )
        for i, (src, dst) in enumerate(
            (
                (ids_ref, ids_x),
                (patch.at[near, :], patch_x.at[near, :]),
                (patch.at[far, :], patch_x.at[far, :]),
            )
        )
    ]
    for send in sends:
        send.start()
    table_ref[...] = jnp.zeros_like(table_ref)
    for i, ref in enumerate((s0, s1, s2, s3, s4, s5, s6, s7, s8)):
        table_ref[i : i + 1, :] = ref[...].astype(F32).reshape(1, 768)

    def masks(ids, one_ref, mask_ref):
        hot = jnp.where(lax.broadcasted_iota(jnp.int32, (128, HALF), 0) == ids, 1.0, 0.0).T
        one_ref[...] = hot.astype(BF16)
        mask_ref[...] = jnp.where((lane >= 6) | (hot > 0.5), 0.0, neg_large).astype(BF16)

    masks(ids_ref[...], qa_ref, ka_ref)
    loads[1].wait()

    def own(i, carry):
        rows = rows_of(i)
        h1[rows, :] = project_tile(patch[rows, :], y * HALF + i * TILE, marks_ref, table_ref, wq, qkv, rows)
        return carry

    lax.fori_loop(0, 2, own, 0)
    stores = [
        pltpu.make_async_copy(a, b, outsem.at[i])
        for i, (a, b) in enumerate(((qkv, qkv_h), (h1, h1_h), (qkvx, qkvx_h), (att, att_h)))
    ]
    stores[0].start()
    stores[1].start()

    def absorb(groups, source, places_of, mask, first):
        def pair(p, carry):
            keys = jnp.concatenate([source[places_of, lanes(768 + p * 128)], mask], axis=1)
            values = source[places_of, lanes(1536 + p * 128)]
            for rows in groups:
                q = qkv[rows, lanes(p * 128)]
                qa = qa_ref[rows, :]
                top, total = tops[rows, :], sums[rows, :]
                if first:
                    top, total = jnp.where(p == 0, 0.0, top), jnp.where(p == 0, 0.0, total)
                else:
                    old = acc[rows, lanes(p * 128)]
                new_top, new_total = top, total
                kept = None
                for h in range(2):
                    mine = (lane // 64) == h
                    here = lane == 2 * p + h
                    scores = dot_t(jnp.concatenate([jnp.where(mine, q, 0), qa], axis=1), keys)
                    peak = jnp.max(scores, axis=-1, keepdims=True)
                    if not first:
                        before = jnp.sum(jnp.where(here, top, 0.0), axis=-1, keepdims=True)
                        peak = jnp.maximum(before, peak)
                        scale = jnp.exp(before - peak)
                    weights = jnp.exp(scores - peak)
                    number = jnp.sum(weights, axis=-1, keepdims=True)
                    out = dot(weights.astype(BF16), values)
                    if not first:
                        number = number + scale * jnp.sum(jnp.where(here, total, 0.0), axis=-1, keepdims=True)
                        out = out + scale * old
                    kept = out if h == 0 else jnp.where(mine, out, kept)
                    new_top = jnp.where(here, peak, new_top)
                    new_total = jnp.where(here, number, new_total)
                acc[rows, lanes(p * 128)] = kept
                tops[rows, :] = new_top
                sums[rows, :] = new_total
            return carry

        lax.fori_loop(0, 6, pair, 0)

    both = (slice(0, TILE), slice(TILE, HALF))
    absorb(both, qkv, slice(None), ka_ref[...], True)
    sends[0].wait_recv()
    masks(ids_x[...], qxa_ref, kxa_ref)
    sends[1].wait_recv()
    project_tile(patch_x[far, :], (1 - y) * HALF + y * TILE, marks_ref, table_ref, wq, qkvx, far)

    absorb(both, qkvx, far, kxa_ref[far, :], False)
    sends[2].wait_recv()
    project_tile(patch_x[near, :], (1 - y) * HALF + (1 - y) * TILE, marks_ref, table_ref, wq, qkvx, near)
    stores[2].start()
    absorb((near,), qkvx, near, kxa_ref[near, :], False)
    total = jnp.where(lane < 12, sums[...], 1.0)
    lse_ref[...] = (tops[...] + jnp.log(total)).T[:16, :]
    for p in range(6):
        for i in range(2):
            rows = slice(i * TILE, i * TILE + TILE)
            low, high = sums[rows, 2 * p : 2 * p + 1], sums[rows, 2 * p + 1 : 2 * p + 2]
            cols = slice(p * 128, p * 128 + 128)
            att[rows, cols] = (acc[rows, cols] / jnp.where(lane < 64, low, high)).astype(BF16)
    stores[3].start()
    for send in sends:
        send.wait_send()
    for store in stores:
        store.wait()


def first_half(patch, w_qkv, ids, marks, smalls):
    hbm = pl.BlockSpec(memory_space=pl.ANY)
    near = pl.BlockSpec(memory_space=pltpu.VMEM)
    dma = pltpu.SemaphoreType.DMA

    def low(*shape):
        return pltpu.VMEM(shape, BF16)

    return pl.pallas_call(
        first_kernel,
        out_shape=tuple(jax.ShapeDtypeStruct((HALF, n), BF16) for n in (2304, 768, 2304, 768))
        + (jax.ShapeDtypeStruct((16, HALF), F32),)
        + (jax.ShapeDtypeStruct((HALF, 128), BF16),) * 4
        + (jax.ShapeDtypeStruct((16, 768), F32),),
        in_specs=[hbm, hbm] + [near] * (2 + len(smalls)),
        out_specs=(hbm,) * 4 + (near,) * 6,
        scratch_shapes=[
            low(HALF, 768),
            low(HALF, 768),
            pltpu.VMEM((1, HALF), jnp.int32),
            low(768, 2304),
            low(HALF, 2304),
            low(HALF, 2304),
            low(HALF, 768),
            low(HALF, 768),
            pltpu.VMEM((HALF, 768), F32),
            pltpu.VMEM((HALF, 128), F32),
            pltpu.VMEM((HALF, 128), F32),
            dma((2,)),
            dma((3,)),
            dma((3,)),
            dma((4,)),
        ],
        compiler_params=pltpu.CompilerParams(collective_id=1, has_side_effects=True, vmem_limit_bytes=67043328),
    )(patch, w_qkv, ids, marks, *smalls)


ERFC_P = 0.3275911
ERFC_C = (
    0.1851102167482524,
    0.17993860771517878,
    0.21041948320823337,
    0.011498087426314028,
    0.47813345988158296,
    -0.4317659362057169,
    0.5111742647535956,
    -0.14450823957827402,
)


def gelu_and_slope(u):
    t = 1.0 / (1.0 + (ERFC_P * math.sqrt(0.5)) * jnp.abs(u))
    bell = jnp.exp(-0.5 * (u * u))
    series = ERFC_C[7]
    for c in ERFC_C[6::-1]:
        series = series * t + c
    tail = (0.5 * t) * series * bell
    phi = jnp.where(u < 0, tail, 1.0 - tail)
    return u * phi, phi + u * (bell * (1.0 / math.sqrt(2.0 * math.pi)))


CHUNKS = 24
SLOTS = 5
FF_TILE = 384
T_FORWARD = (0, 0, 1, 2, 3, 4, 5, 6)
EMIT_DOWN, EMIT_UP, EMIT_OUT, EMIT_QKV = (0, 2, 4, 6), (8, 10, 12, 14), (16,), (18, 19, 20, 21, 22, 23)
T_SECOND, T_ATTENDED = (7,), (8,)
T_SEND = (8, 9, 10, 11, 12, 13, 14, 15, 16, 17, 18, 19)
T_OWN = (8, 9, 10, 12, 14, 16)
T_FAR = (11, 13, 15, 17, 19, 21)
T_OUTPUT = (19, 19, 20, 20, 21, 21, 22, 22)
T_GRAD = (24, 24, 25)
T_FIRST = (26,)
T_VEC = 27


def halves_kernel(
    cot_h, wo_h, qkv_h, h1_h, patch_h, wq_h, qkvx_h, att_h, wu_h, wd_h,
    qa_ref, ka_ref, qxa_ref, kxa_ref, lse_ref, table_ref, marks_ref, ub_ref,
    parts_h, out_h, gp_h, vec_out,
    cot, wo, qkv, h1, patch, wq, qkvx, att, wu, wd,
    act, gu, mid, h2, acc, gb, do, dox, dqkv, dq, dk, dv, drow, dxrow, lsex_ref, ub,
    g, r1, r2, r3, r4, r5, done, v0, v1, v2,
    insem, wusem, wdsem, ssem, rsem, vs, vr, xs, xr, outsem, lastsem,
):
    core, x, y, peers = places()
    pair, yp, xp, zp1, zp2 = peers
    lane = lax.broadcasted_iota(jnp.int32, (1, 128), 1)
    inputs = (
        (cot_h, cot), (wo_h, wo), (qkv_h, qkv), (h1_h, h1), (patch_h, patch), (wq_h, wq),
        (qkvx_h, qkvx), (att_h, att),
    )
    COT, WO, QKV, H1, PATCH, WQ, QKVX, ATT = range(8)

    def lanes(start, size=128):
        return pl.ds(pl.multiple_of(start, 128), size)

    def part_of(n):
        return (n // 2 + 4 * (n % 2)) * (1 - n // 8) + (n - 8) * (n // 8)

    def load(i):
        return pltpu.make_async_copy(inputs[i][0], inputs[i][1], insem.at[i])

    def up_tile(n):
        return pltpu.make_async_copy(wu_h.at[:, lanes(part_of(n) * FF_TILE, FF_TILE)], wu.at[n % 2], wusem.at[n % 2])

    def down_tile(n):
        rows = pl.ds(pl.multiple_of(part_of(n) * FF_TILE, FF_TILE), FF_TILE)
        return pltpu.make_async_copy(wd_h.at[rows, :], wd.at[n % 2], wdsem.at[n % 2])

    for i in (PATCH, WO, ATT):
        load(i).start()
    for n in range(2):
        up_tile(n).start()
        down_tile(n).start()
    for i in (COT, QKV, QKVX, H1, WQ):
        load(i).start()
    greet(peers)

    def remote(src, dst, send, recv, dev):
        return pltpu.make_async_remote_copy(
            src_ref=src, dst_ref=dst, send_sem=send, recv_sem=recv, device_id=dev, device_id_type=MESH
        )

    def copy(s, c):
        src, dst, dev = (
            lambda: (g.at[c % SLOTS, 1 - core], r1.at[c], pair),
            lambda: (r1.at[c, 1 - y], r2.at[c], yp),
            lambda: (r2.at[c, 1 - x], r3.at[c], xp),
            lambda: (r3.at[c], r4.at[c], zp1),
            lambda: (r4.at[c], r5.at[c], zp2),
            lambda: (done.at[c, core, x], done.at[c, core, x], xp),
            lambda: (done.at[c, core], done.at[c, core], pair),
        )[s]()
        return remote(src, dst, ssem.at[s, c], rsem.at[s, c], dev)

    def part_out(c):
        return pltpu.make_async_copy(done.at[c], parts_h.at[c], outsem.at[c])

    def stage(s, c):
        if s > 0:
            copy(s - 1, c).wait_recv()
        if s == 1:
            r1[c] = r1[c] + g[c % SLOTS, core]
        elif s == 2:
            r2[c] = r2[c] + r1[c, y]
        elif s == 3:
            r3[c] = r3[c] + r2[c, x]
        elif s == 4:
            r4[c] = r4[c] + r3[c]
        elif s == 5:
            done[c, core, x] = r5[c] + r4[c]
        elif s == 7:
            copy(5, c).wait_send()
            copy(6, c).wait_send()
            part_out(c).start()
        if s < 7:
            copy(s, c).start()

    def vec_copy(s):
        src, dst, dev = (
            lambda: (v0, v1, pair),
            lambda: (v1.at[1 - y], v2.at[0], yp),
            lambda: (v2.at[0], v2.at[1], xp),
            lambda: (v2.at[1], v2.at[2], zp1),
            lambda: (v2.at[2], v2.at[3], zp2),
        )[s]()
        return remote(src, dst, vs.at[s], vr.at[s], dev)

    def vec_stage(s):
        if s > 0:
            vec_copy(s - 1).wait_recv()
        if s == 1:
            v1[...] = v1[...] + v0[...]
        elif s == 2:
            v2[0] = v2[0] + v1[y]
        elif s == 5:
            vec_out[...] = v2[3] + v2[2]
        elif s > 2:
            v2[s - 2] = v2[s - 2] + v2[s - 3]
        if s < 5:
            vec_copy(s).start()

    def far_copy(i):
        src, dst = ((lse_ref, lsex_ref), (drow, dxrow))[i]
        return remote(src, dst, xs.at[i], xr.at[i], yp)

    def grad_copy(n):
        rows, cols = pl.ds(pl.multiple_of((n % 2) * TILE, TILE), TILE), lanes((n // 2) * 128)
        return remote(do.at[rows, cols], dox.at[rows, cols], xs.at[2 + n], xr.at[2 + n], yp)

    def row(r):
        return table_ref[r : r + 1, :]

    def add_vec(r, value):
        for half in range(2):
            v0[half, r : r + 1, :] = v0[half, r : r + 1, :] + value[:, half * 384 : half * 384 + 384]

    def emit(left, right, c):
        number = right.shape[1] // 384
        for i in range(number):

            @pl.when(c + i >= SLOTS)
            def _():
                copy(0, c + i - SLOTS).wait_send()

        for half in range(2):
            block = t_dot(left(half), right).astype(BF16)
            for i in range(number):
                for other in range(4):
                    rows = slice(other * SUB, other * SUB + SUB)
                    g[(c + i) % SLOTS, other // 2, half, other % 2] = block[rows, i * 384 : i * 384 + 384]

    def enter():
        for tile in range(HALF // TILE):
            rows = slice(tile * TILE, tile * TILE + TILE)
            unused, values = masked_inputs(patch[rows, :], y * HALF + tile * TILE, marks_ref[...], row(R_EMBED))
            total = values + dot(att[rows, :], wo[...]) + row(R_OB)
            normed, unused = standard(total)
            mid[rows, :] = total
            h2[rows, :] = (normed * row(R_G2) + row(R_B2)).astype(BF16)

    def forward(n):
        k = part_of(n)
        cols = lanes(k * FF_TILE, FF_TILE)
        up_tile(n).wait()
        down_tile(n).wait()
        sums = jnp.zeros((1, FF_TILE), F32)
        for tile in range(HALF // TILE):
            rows = slice(tile * TILE, tile * TILE + TILE)
            value, slope = gelu_and_slope(dot(h2[rows, :], wu[n % 2]) + ub[:, cols])
            act[rows, cols] = value.astype(BF16)
            low = (dot_t(cot[rows, :], wd[n % 2]) * slope).astype(BF16)
            gu[rows, cols] = low
            sums = sums + jnp.sum(low.astype(F32), axis=0, keepdims=True)
            acc[rows, :] = acc[rows, :] + dot_t(low, wu[n % 2])
        v0[k // 4, pl.ds(9 + k % 4, 1), :] = sums
        down_tile(n + 2).start()

        @pl.when(n + 2 < 8)
        def _():
            up_tile(n + 2).start()

    def second_norm():
        def tile(i, carry):
            rows = pl.ds(pl.multiple_of(i * 128, 128), 128)
            normed, inverse = standard(mid[rows, :])
            grad = acc[rows, :]
            cotangent = cot[rows, :].astype(F32)
            add_vec(6, jnp.sum(grad * normed, axis=0, keepdims=True))
            add_vec(7, jnp.sum(grad, axis=0, keepdims=True))
            add_vec(8, jnp.sum(cotangent, axis=0, keepdims=True))
            total = cotangent + norm_back(grad, normed, inverse, row(R_G2))
            acc[rows, :] = total
            low = total.astype(BF16)
            gb[rows, :] = low
            add_vec(5, jnp.sum(low.astype(F32), axis=0, keepdims=True))
            return carry

        lax.fori_loop(0, 4, tile, 0)

    def grad_attended():
        for tile in range(2):
            rows = slice(tile * 256, tile * 256 + 256)
            do[rows, :] = dot_t(gb[rows, :], wo[...]).astype(BF16)
        for tile in range(4):
            rows = slice(tile * 128, tile * 128 + 128)
            columns = jnp.zeros((128, 128), F32)
            for p in range(6):
                cols = slice(p * 128, p * 128 + 128)
                product = do[rows, cols].astype(F32) * att[rows, cols].astype(F32)
                for h in range(2):
                    total = jnp.sum(jnp.where((lane // 64) == h, product, 0.0), axis=1, keepdims=True)
                    columns = jnp.where(lane == 2 * p + h, total, columns)
            drow[:, rows] = columns.T[:16, :]
        far_copy(1).start()

    def piece(keys, key_mask, values, query, query_mask, grad, lse, delta):
        scores = dot_t(jnp.concatenate([keys, key_mask], axis=1), jnp.concatenate([query, query_mask], axis=1))
        probs = jnp.exp(scores - lse)
        grad_scores = probs * (dot_t(values, grad) - delta)
        return probs.astype(BF16), grad_scores.astype(BF16)

    def own_pair(p):
        slot = p % 3

        def head(h, carry):
            mine = (lane // 64) == h
            stat = pl.ds(2 * p + h, 1)
            query = jnp.where(mine, qkv[:, lanes(p * 128)], 0)
            grad = jnp.where(mine, do[:, lanes(p * 128)], 0)
            for tile in range(2):
                rows = slice(tile * 256, tile * 256 + 256)
                keys = qkv[rows, lanes(768 + p * 128)]
                probs, scores = piece(
                    keys, ka_ref[rows, :], qkv[rows, lanes(1536 + p * 128)], query, qa_ref[...], grad,
                    lse_ref[stat, :], drow[stat, :],
                )
                new = dot(scores, query)
                dk[slot, rows, :] = jnp.where(h == 0, new, dk[slot, rows, :] + new)
                new = dot(probs, grad)
                dv[slot, rows, :] = jnp.where(h == 0, new, dv[slot, rows, :] + new)
                new = t_dot(scores, jnp.where(mine, keys, 0))
                dq[slot] = jnp.where((h == 0) & (tile == 0), new, dq[slot] + new)
            return carry

        lax.fori_loop(0, 2, head, 0)

    def far_pair(p):
        slot = p % 3
        grad_copy(2 * p).wait_recv()
        grad_copy(2 * p + 1).wait_recv()
        near, far = pl.multiple_of((1 - y) * 256, 256), pl.multiple_of(y * 256, 256)

        def head(h, carry):
            mine = (lane // 64) == h
            stat = pl.ds(2 * p + h, 1)
            for first, start, size in ((far, 0, 512), (near, near, 256)):
                rows, others = pl.ds(first, 256), pl.ds(start, size)
                query = jnp.where(mine, qkv[others, lanes(p * 128)], 0)
                grad = jnp.where(mine, do[others, lanes(p * 128)], 0)
                keys = qkvx[rows, lanes(768 + p * 128)]
                probs, scores = piece(
                    keys, kxa_ref[rows, :], qkvx[rows, lanes(1536 + p * 128)], query, qa_ref[others, :], grad,
                    lse_ref[stat, others], drow[stat, others],
                )
                dq[slot, others, :] = dq[slot, others, :] + t_dot(scores, jnp.where(mine, keys, 0))
            for first, start, size in ((near, 0, 512), (far, far, 256)):
                rows, others = pl.ds(first, 256), pl.ds(start, size)
                query = jnp.where(mine, qkvx[others, lanes(p * 128)], 0)
                grad = jnp.where(mine, dox[others, lanes(p * 128)], 0)
                probs, scores = piece(
                    qkv[rows, lanes(768 + p * 128)], ka_ref[rows, :], qkv[rows, lanes(1536 + p * 128)],
                    query, qxa_ref[others, :], grad, lsex_ref[stat, others], dxrow[stat, others],
                )
                dk[slot, rows, :] = dk[slot, rows, :] + dot(scores, query)
                dv[slot, rows, :] = dv[slot, rows, :] + dot(probs, grad)
            return carry

        lax.fori_loop(0, 2, head, 0)
        dqkv[:, lanes(p * 128)] = (dq[slot].astype(BF16).astype(F32) * QUERY_SCALE).astype(BF16)
        dqkv[:, lanes(768 + p * 128)] = dk[slot].astype(BF16)
        dqkv[:, lanes(1536 + p * 128)] = dv[slot].astype(BF16)

    def output_tile(i):
        n = i + 8
        down_tile(n).wait()
        for tile in range(2):
            rows = slice(tile * 256, tile * 256 + 256)
            mid[rows, :] = mid[rows, :] + dot(act[rows, lanes(i * FF_TILE, FF_TILE)], wd[n % 2])

        @pl.when(n + 2 < 16)
        def _():
            down_tile(n + 2).start()

    def store_output():
        for tile in range(4):
            rows = slice(tile * 128, tile * 128 + 128)
            gb[rows, :] = (mid[rows, :] + row(R_DB)).astype(BF16)
        pltpu.make_async_copy(gb, out_h, lastsem.at[0]).start()

    def grad_first(part):
        for tile in range(2):
            rows = slice(tile * 256, tile * 256 + 256)
            new = dot_t(dqkv[rows, lanes(part * 768, 768)], wq[:, lanes(part * 768, 768)])
            mid[rows, :] = jnp.where(part == 0, new, mid[rows, :] + new)

    def first_norm():
        def tile(i, carry):
            rows = pl.ds(pl.multiple_of(i * 128, 128), 128)
            flagged, values = masked_inputs(patch[rows, :], y * HALF + i * 128, marks_ref[...], row(R_EMBED))
            normed, inverse = standard(values)
            grad = mid[rows, :]
            add_vec(1, jnp.sum(grad * normed, axis=0, keepdims=True))
            add_vec(2, jnp.sum(grad, axis=0, keepdims=True))
            total = acc[rows, :] + norm_back(grad, normed, inverse, row(R_G1))
            add_vec(0, jnp.sum(jnp.where(flagged, total, 0.0), axis=0, keepdims=True))
            att[rows, :] = jnp.where(flagged, 0.0, total).astype(BF16)
            add_vec(3, jnp.sum(dqkv[rows, :768].astype(F32), axis=0, keepdims=True))
            add_vec(4, jnp.sum(dqkv[rows, 1536:].astype(F32), axis=0, keepdims=True))
            return carry

        lax.fori_loop(0, 4, tile, 0)
        pltpu.make_async_copy(att, gp_h, lastsem.at[1]).start()

    far_copy(0).start()
    ub[...] = ub_ref[...].astype(F32).reshape(1, 3072)
    acc[...] = jnp.zeros_like(acc)
    v0[...] = jnp.zeros_like(v0)
    for i in (PATCH, WO, ATT):
        load(i).wait()
    enter()
    load(COT).wait()

    def step(t, carry):
        def run(times, body):
            def before(now):
                return sum(jnp.where(now > at, 1, 0) for at in times)

            def one(n, inner):
                body(n)
                return inner

            lax.fori_loop(before(t), before(t + 1), one, 0)

        def need(at, *names):
            @pl.when(t == at)
            def _():
                for i in names:
                    load(i).wait()

        for s in range(2, 8):
            c = t - LAGS[s]

            @pl.when((c >= 0) & (c < CHUNKS))
            def _():
                stage(s, c)

        need(2, QKV, QKVX, H1, WQ)
        run(T_FORWARD, forward)
        run(
            EMIT_DOWN,
            lambda n: emit(lambda half: act[:, lanes(half * 1536 + n * 384, 384)], cot[...], 2 * n),
        )
        run(
            EMIT_UP,
            lambda n: emit(lambda half: h2[:, half * 384 : half * 384 + 384], gu[:, lanes(n * 768, 768)], 8 + 2 * n),
        )
        run(EMIT_OUT, lambda n: emit(lambda half: att[:, half * 384 : half * 384 + 384], gb[...], 16))

        def emit_qkv(p):
            right = jnp.concatenate([dqkv[:, lanes(part * 768 + p * 128)] for part in range(3)], axis=1)
            emit(lambda half: h1[:, half * 384 : half * 384 + 384], right, 18 + p)

        run(EMIT_QKV, emit_qkv)
        @pl.when(t < CHUNKS)
        def _():
            stage(0, t)

        @pl.when((t >= LAGS[1]) & (t < CHUNKS + LAGS[1]))
        def _():
            stage(1, t - LAGS[1])


        run(T_SECOND, lambda n: second_norm())
        run(T_ATTENDED, lambda n: grad_attended())
        run(T_SEND, lambda n: grad_copy(n).start())
        run(T_OWN, own_pair)

        @pl.when(t == T_FAR[0])
        def _():
            far_copy(0).wait_recv()
            far_copy(1).wait_recv()

        run(T_FAR, far_pair)
        run(T_OUTPUT, output_tile)

        @pl.when(t == T_OUTPUT[-1])
        def _():
            store_output()

        run(T_GRAD, grad_first)
        run(T_FIRST, lambda n: first_norm())

        for s in range(6):

            @pl.when(t == T_VEC + s)
            def _():
                vec_stage(s)

        return carry

    lax.fori_loop(0, max(T_VEC + 6, CHUNKS + LAGS[7]), step, 0)

    def drain(c, carry):
        for s in range(1, 5):
            copy(s, c).wait_send()
        part_out(c).wait()
        return carry

    lax.fori_loop(0, CHUNKS, drain, 0)
    for c in range(CHUNKS - SLOTS, CHUNKS):
        copy(0, c).wait_send()
    for s in range(5):
        vec_copy(s).wait_send()
    for i in range(2):
        far_copy(i).wait_send()

    def drain_grad(n, carry):
        grad_copy(n).wait_send()
        return carry

    lax.fori_loop(0, 12, drain_grad, 0)
    pltpu.make_async_copy(gb, out_h, lastsem.at[0]).wait()
    pltpu.make_async_copy(att, gp_h, lastsem.at[1]).wait()


def backward(big, weights, small):
    hbm = pl.BlockSpec(memory_space=pl.ANY)
    near = pl.BlockSpec(memory_space=pltpu.VMEM)

    def low(*shape):
        return pltpu.VMEM(shape, BF16)

    def full(*shape):
        return pltpu.VMEM(shape, F32)

    dma = pltpu.SemaphoreType.DMA
    held = [pltpu.VMEM(a.shape, a.dtype) for a in big]
    return pl.pallas_call(
        halves_kernel,
        out_shape=(
            jax.ShapeDtypeStruct((CHUNKS, 2, 2, SUB, COLS), BF16),
            jax.ShapeDtypeStruct((HALF, 768), BF16),
            jax.ShapeDtypeStruct((HALF, 768), BF16),
            jax.ShapeDtypeStruct((16, COLS), F32),
        ),
        in_specs=[hbm] * (len(big) + 2) + [near] * len(small),
        out_specs=(hbm, hbm, hbm, near),
        scratch_shapes=held
        + [
            low(2, 768, FF_TILE),
            low(2, FF_TILE, 768),
            low(HALF, 3072),
            low(HALF, 3072),
            full(HALF, 768),
            low(HALF, 768),
            full(HALF, 768),
            low(HALF, 768),
            low(HALF, 768),
            low(HALF, 768),
            low(HALF, 2304),
            full(3, HALF, 128),
            full(3, HALF, 128),
            full(3, HALF, 128),
            full(16, HALF),
            full(16, HALF),
            full(16, HALF),
            full(1, 3072),
            low(SLOTS, 2, 2, 2, SUB, COLS),
            low(CHUNKS, 2, 2, SUB, COLS),
            low(CHUNKS, 2, SUB, COLS),
            low(CHUNKS, SUB, COLS),
            low(CHUNKS, SUB, COLS),
            low(CHUNKS, SUB, COLS),
            low(CHUNKS, 2, 2, SUB, COLS),
            full(2, 16, COLS),
            full(2, 16, COLS),
            full(4, 16, COLS),
            dma((8,)),
            dma((2,)),
            dma((2,)),
            dma((7, CHUNKS)),
            dma((7, CHUNKS)),
            dma((5,)),
            dma((5,)),
            dma((14,)),
            dma((14,)),
            dma((CHUNKS,)),
            dma((2,)),
        ],
        compiler_params=pltpu.CompilerParams(
            collective_id=0, has_side_effects=True, vmem_limit_bytes=67043328
        ),
    )(*big, *weights, *small)


def widen_kernel(four_ref, qkv_ref, down_ref, up_ref, out_ref, proj_ref):
    i = pl.program_id(0)

    @pl.when(i < 2)
    def _():
        for c in range(4):
            rows = slice(c // 2 * 384, c // 2 * 384 + 384)
            down_ref[rows, c % 2 * 384 : c % 2 * 384 + 384] = four_ref[c].astype(F32)

    for first, last, ref in ((2, 4, up_ref), (4, 5, out_ref)):

        @pl.when((i >= first) & (i < last))
        def _():
            for c in range(ref.shape[1] // 384):
                ref[:, c * 384 : c * 384 + 384] = four_ref[c].astype(F32)

    @pl.when(i >= 5)
    def _():
        for p in range(6):
            proj_ref[:, p * 128 : p * 128 + 128] = qkv_ref[p].astype(F32)


def widen(parts):
    parts = parts.reshape(CHUNKS, 384, COLS)
    return pl.pallas_call(
        widen_kernel,
        grid=(8,),
        out_shape=(
            jax.ShapeDtypeStruct((1536, 768), F32),
            jax.ShapeDtypeStruct((384, 3072), F32),
            jax.ShapeDtypeStruct((384, 768), F32),
            jax.ShapeDtypeStruct((384, 2304), F32),
        ),
        in_specs=[
            pl.BlockSpec((4, 384, COLS), lambda i: (jnp.minimum(i, 4), 0, 0)),
            pl.BlockSpec((6, 384, 128), lambda i: (3, 0, jnp.maximum(i - 5, 0))),
        ],
        out_specs=(
            pl.BlockSpec((768, 768), lambda i: (jnp.minimum(i, 1), 0)),
            pl.BlockSpec((384, 1536), lambda i: (0, jnp.clip(i - 2, 0, 1))),
            pl.BlockSpec((384, 768), lambda i: (0, 0)),
            pl.BlockSpec((384, 768), lambda i: (0, jnp.maximum(i - 5, 0))),
        ),
    )(parts, parts)


def block_shards(
    patches,
    segment_ids,
    mask_positions,
    mask_embed,
    norm1_gain,
    norm1_bias,
    w_qkv,
    query_bias,
    value_bias,
    w_out,
    out_bias,
    norm2_gain,
    norm2_bias,
    w_up,
    up_bias,
    w_down,
    down_bias,
    cotangent,
):
    patch = patches[0]
    cot = cotangent[0]
    qkv, hidden1, qkv_x, attended, lse, qa, ka, qxa, kxa, table = first_half(
        patch,
        w_qkv,
        segment_ids,
        mask_positions,
        (mask_embed, norm1_gain, norm1_bias, query_bias, value_bias, out_bias, norm2_gain, norm2_bias, down_bias),
    )
    parts, output, grad_patches, v = backward(
        (cot, w_out, qkv, hidden1, patch, w_qkv, qkv_x, attended),
        (w_up, w_down),
        (qa, ka, qxa, kxa, lse, table, mask_positions, up_bias),
    )
    grad_down, grad_up, grad_out, grad_qkv = widen(parts)
    return (
        output[None],
        grad_patches[None],
        v[0],
        v[1],
        v[2],
        grad_qkv,
        v[3],
        v[4],
        grad_out,
        v[5],
        v[6],
        v[7],
        grad_up,
        v[9:13].reshape(-1),
        grad_down,
        v[8],
    )


def shards(
    patches,
    segment_ids,
    mask_positions,
    mask_embed,
    norm1_gain,
    norm1_bias,
    w_qkv,
    query_bias,
    value_bias,
    w_out,
    out_bias,
    norm2_gain,
    norm2_bias,
    w_up,
    up_bias,
    w_down,
    down_bias,
    cotangent,
):
    rows_n, time_n, width = patches.shape
    query_scale = 1.0 / math.sqrt(HEAD)
    gain_one = norm1_gain.astype(jnp.float32)
    gain_two = norm2_gain.astype(jnp.float32)
    offset = lax.axis_index("tm") * time_n
    places = offset + lax.broadcasted_iota(jnp.int32, (rows_n, time_n, 1), 1)
    masked = jnp.any(places == mask_positions[:, None, :], axis=-1)[..., None]
    inputs = jnp.where(
        masked, mask_embed.astype(jnp.float32)[None, None, :], patches.astype(jnp.float32)
    )
    normed1, inverse1 = normalize(inputs)
    hidden1 = (normed1 * gain_one + norm1_bias.astype(jnp.float32)).astype(jnp.bfloat16)
    project = jnp.einsum("rtd,de->rte", hidden1, w_qkv, preferred_element_type=jnp.float32)
    queries = ((project[..., :width] + query_bias.astype(jnp.float32)) * query_scale).astype(
        jnp.bfloat16
    )
    keys_own = project[..., width : 2 * width].astype(jnp.bfloat16)
    values_own = (project[..., 2 * width :] + value_bias.astype(jnp.float32)).astype(jnp.bfloat16)
    keys_all, values_all, segments_all = (
        lax.all_gather(keys_own, "tm", axis=1, tiled=True),
        lax.all_gather(values_own, "tm", axis=1, tiled=True),
        lax.all_gather(segment_ids, "tm", axis=1, tiled=True),
    )
    same = segment_ids[:, :, None] == segments_all[:, None, :]
    query_heads = split_heads(queries)
    head_outputs, log_totals = attend_forward(
        query_heads, split_heads(keys_all), split_heads(values_all), same
    )
    attended = join_heads(head_outputs).astype(jnp.bfloat16)
    middle = (
        inputs
        + jnp.einsum("rtd,de->rte", attended, w_out, preferred_element_type=jnp.float32)
        + out_bias.astype(jnp.float32)
    )
    normed2, inverse2 = normalize(middle)
    hidden2 = (normed2 * gain_two + norm2_bias.astype(jnp.float32)).astype(jnp.bfloat16)
    upper = jnp.einsum(
        "rtd,df->rtf", hidden2, w_up, preferred_element_type=jnp.float32
    ) + up_bias.astype(jnp.float32)
    activated = jax.nn.gelu(upper, approximate=False).astype(jnp.bfloat16)
    result = (
        middle
        + jnp.einsum("rtf,fd->rtd", activated, w_down, preferred_element_type=jnp.float32)
        + down_bias.astype(jnp.float32)
    )
    output = result.astype(jnp.bfloat16)
    grad_result = cotangent.astype(jnp.float32)
    grad_w_down = jnp.einsum(
        "rtf,rtd->fd", activated, cotangent, preferred_element_type=jnp.float32
    )
    grad_down_bias = total_rows(grad_result)
    grad_activated = jnp.einsum(
        "rtd,fd->rtf", cotangent, w_down, preferred_element_type=jnp.float32
    )
    unused, gelu_pull = jax.vjp(partial(jax.nn.gelu, approximate=False), upper)
    grad_upper = gelu_pull(grad_activated)[0].astype(jnp.bfloat16)
    grad_w_up = jnp.einsum("rtd,rtf->df", hidden2, grad_upper, preferred_element_type=jnp.float32)
    grad_up_bias = total_rows(grad_upper)
    grad_hidden2 = jnp.einsum("rtf,df->rtd", grad_upper, w_up, preferred_element_type=jnp.float32)
    grad_gain_two = total_rows(grad_hidden2 * normed2)
    grad_bias_two = total_rows(grad_hidden2)
    grad_middle = grad_result + norm_back(grad_hidden2, normed2, inverse2, gain_two)
    mlp_vectors = jnp.stack([grad_gain_two, grad_bias_two, grad_down_bias], axis=1)
    grad_branch = grad_middle.astype(jnp.bfloat16)
    grad_w_out = jnp.einsum(
        "rtd,rte->de", attended, grad_branch, preferred_element_type=jnp.float32
    )
    grad_out_bias = total_rows(grad_branch)
    grad_attended = jnp.einsum(
        "rte,de->rtd", grad_branch, w_out, preferred_element_type=jnp.float32
    ).astype(jnp.bfloat16)
    keys_back, values_back, segments_back = (
        lax.all_gather(keys_own, "tm", axis=1, tiled=True),
        lax.all_gather(values_own, "tm", axis=1, tiled=True),
        lax.all_gather(segment_ids, "tm", axis=1, tiled=True),
    )
    same_back = segment_ids[:, :, None] == segments_back[:, None, :]
    grad_query_h, grad_keys_h, grad_values_h = attend_backward(
        query_heads,
        split_heads(keys_back),
        split_heads(values_back),
        split_heads(grad_attended),
        log_totals,
        same_back,
    )
    grad_keys, grad_values = (
        lax.psum_scatter(
            join_heads(grad_keys_h).astype(jnp.bfloat16), "tm", scatter_dimension=1, tiled=True
        ).astype(jnp.float32),
        lax.psum_scatter(
            join_heads(grad_values_h).astype(jnp.bfloat16), "tm", scatter_dimension=1, tiled=True
        ).astype(jnp.float32),
    )
    grad_queries = join_heads(grad_query_h).astype(jnp.bfloat16)
    grad_project = jnp.concatenate(
        [
            (grad_queries.astype(jnp.float32) * query_scale).astype(jnp.bfloat16),
            grad_keys.astype(jnp.bfloat16),
            grad_values.astype(jnp.bfloat16),
        ],
        axis=-1,
    )
    grad_w_qkv = jnp.einsum(
        "rtd,rte->de", hidden1, grad_project, preferred_element_type=jnp.float32
    )
    grad_query_bias = total_rows(grad_project[..., :width])
    grad_value_bias = total_rows(grad_project[..., 2 * width :])
    grad_hidden1 = jnp.einsum(
        "rte,de->rtd", grad_project, w_qkv, preferred_element_type=jnp.float32
    )
    grad_gain_one = total_rows(grad_hidden1 * normed1)
    grad_bias_one = total_rows(grad_hidden1)
    grad_inputs = grad_middle + norm_back(grad_hidden1, normed1, inverse1, gain_one)
    grad_mask = total_rows(jnp.where(masked, grad_inputs, 0.0))
    grad_patches = jnp.where(masked, 0.0, grad_inputs).astype(jnp.bfloat16)
    attn_vectors = jnp.stack(
        [grad_mask, grad_gain_one, grad_bias_one, grad_query_bias, grad_value_bias, grad_out_bias],
        axis=1,
    )
    every_part = (
        lax.psum_scatter(
            grad_w_qkv.astype(jnp.bfloat16), "tm", scatter_dimension=0, tiled=True
        ).astype(jnp.float32),
        lax.psum_scatter(
            grad_w_out.astype(jnp.bfloat16), "tm", scatter_dimension=0, tiled=True
        ).astype(jnp.float32),
        lax.psum_scatter(
            attn_vectors.astype(jnp.bfloat16), "tm", scatter_dimension=0, tiled=True
        ).astype(jnp.float32),
        lax.psum_scatter(
            grad_w_up.astype(jnp.bfloat16), "tm", scatter_dimension=0, tiled=True
        ).astype(jnp.float32),
        lax.psum_scatter(
            grad_w_down.astype(jnp.bfloat16), "tm", scatter_dimension=0, tiled=True
        ).astype(jnp.float32),
        lax.psum_scatter(
            mlp_vectors.astype(jnp.bfloat16), "tm", scatter_dimension=0, tiled=True
        ).astype(jnp.float32),
        lax.psum_scatter(
            grad_up_bias.astype(jnp.bfloat16), "tm", scatter_dimension=0, tiled=True
        ).astype(jnp.float32),
    )
    every_part = (
        lax.psum(every_part[0].astype(jnp.bfloat16), "rows").astype(jnp.float32),
        lax.psum(every_part[1].astype(jnp.bfloat16), "rows").astype(jnp.float32),
        lax.psum(every_part[2].astype(jnp.bfloat16), "rows").astype(jnp.float32),
        lax.psum(every_part[3].astype(jnp.bfloat16), "rows").astype(jnp.float32),
        lax.psum(every_part[4].astype(jnp.bfloat16), "rows").astype(jnp.float32),
        lax.psum(every_part[5].astype(jnp.bfloat16), "rows").astype(jnp.float32),
        lax.psum(every_part[6].astype(jnp.bfloat16), "rows").astype(jnp.float32),
    )
    summed_qkv, summed_out, summed_attn, summed_up, summed_down, summed_mlp, summed_up_bias = (
        every_part
    )
    return (
        output,
        grad_patches,
        summed_attn[:, 0],
        summed_attn[:, 1],
        summed_attn[:, 2],
        summed_qkv,
        summed_attn[:, 3],
        summed_attn[:, 4],
        summed_out,
        summed_attn[:, 5],
        summed_mlp[:, 0],
        summed_mlp[:, 1],
        summed_up,
        summed_up_bias,
        summed_down,
        summed_mlp[:, 2],
    )


def solution(mesh):
    placed = (
        P("rows", "tm", None),
        P("rows", "tm"),
        P("rows", None),
        P(),
        P(),
        P(),
        P(),
        P(),
        P(),
        P(),
        P(),
        P(),
        P(),
        P(),
        P(),
        P(),
        P(),
        P("rows", "tm", None),
    )
    return jax.shard_map(
        block_shards if dict(mesh.shape) == {"rows": 16, "tm": 2} else shards,
        mesh=mesh,
        in_specs=placed,
        out_specs=(
            P("rows", "tm", None),
            P("rows", "tm", None),
            P("tm"),
            P("tm"),
            P("tm"),
            P("tm", None),
            P("tm"),
            P("tm"),
            P("tm", None),
            P("tm"),
            P("tm"),
            P("tm"),
            P("tm", None),
            P("tm"),
            P("tm", None),
            P("tm"),
        ),
        check_vma=False,
    )
```
